32 devices in a mesh: dp: 8 (over y, x, core), seq: 4 (over z).
Axes of the slice: x: 2, y: 2, z: 4, core: 2. Of those that a mesh axis runs over, the one named last changes fastest.
Arguments:
- text_in: bfloat16 [16, 256, 768], P('dp', 'seq'), may hold values from -6 to 6
- image_in: bfloat16 [16, 160, 1024], P('dp', 'seq'), may hold values from -6 to 6
- text_seg: int32 [16, 256], P('dp'), may hold values from 0 to 4, as said below
- image_seg: int32 [16, 160], P('dp'), may hold values from 0 to 4, as said below
- text_co_in: bfloat16 [768, 3072], replicated, may hold values from -0.21875 to 0.21875
- image_co_in: bfloat16 [1024, 3072], replicated, may hold values from -0.1875 to 0.1875
- text_co_out: bfloat16 [1024, 768], replicated, may hold values from -1 to 1
- image_co_out: bfloat16 [1024, 1024], replicated, may hold values from -1 to 1
- text_up: bfloat16 [768, 3072], replicated, may hold values from -0.21875 to 0.21875
- text_down: bfloat16 [3072, 768], replicated, may hold values from -0.15625 to 0.15625
- image_up: bfloat16 [1024, 1024], replicated, may hold values from -0.1875 to 0.1875
- image_down: bfloat16 [1024, 1024], replicated, may hold values from -0.25 to 0.25
- text_qkv: bfloat16 [768, 2304], replicated, may hold values from -0.21875 to 0.21875
- text_proj: bfloat16 [768, 768], replicated, may hold values from -1.25 to 1.25
- image_qkv: bfloat16 [1024, 3072], replicated, may hold values from -0.1875 to 0.1875
- image_proj: bfloat16 [1024, 1024], replicated, may hold values from -1 to 1
- text_gains: float32 [3, 768], replicated, may hold values from 0.25 to 1.75
- image_gains: float32 [3, 1024], replicated, may hold values from 0.25 to 1.75
- text_upstream: bfloat16 [16, 256, 768], P('dp', 'seq'), may hold values from -6 to 6
- image_upstream: bfloat16 [16, 160, 1024], P('dp', 'seq'), may hold values from -6 to 6
Outputs:
- text_result: bfloat16 [16, 256, 768], P('dp', 'seq')
- image_result: bfloat16 [16, 160, 1024], P('dp', 'seq')
- text_in_grad: float32 [16, 256, 768], P('dp', 'seq')
- image_in_grad: float32 [16, 160, 1024], P('dp', 'seq')
- text_co_in_grad: float32 [768, 3072], P('dp')
- image_co_in_grad: float32 [1024, 3072], P('dp')
- text_co_out_grad: float32 [1024, 768], P('dp')
- image_co_out_grad: float32 [1024, 1024], P('dp')
- text_up_grad: float32 [768, 3072], P('dp')
- text_down_grad: float32 [3072, 768], P('dp')
- image_up_grad: float32 [1024, 1024], P('dp')
- image_down_grad: float32 [1024, 1024], P('dp')
- text_qkv_grad: float32 [768, 2304], P('dp')
- text_proj_grad: float32 [768, 768], P('dp')
- image_qkv_grad: float32 [1024, 3072], P('dp')
- image_proj_grad: float32 [1024, 1024], P('dp')
- text_gains_grad: float32 [3, 768], replicated
- image_gains_grad: float32 [3, 1024], replicated
The draws below stay inside these ranges and needn't reach their ends.
Inputs may be any that keep to these rules, and one draw needn't show every extreme that they name: `text_seg`: in every row the text slots hold four captions in order (ids 0, 1, 2, 3), each non-empty, then padding (id 4), never empty. `image_seg`: in every row the image slots hold the regions of four images in order (ids 0, 1, 2, 3), each non-empty, then padding (id 4), never empty.
All inputs are finite; a program needn't handle non-finite values.
Results may differ from the reference program's by a relative error of at most 0.024.
Values may be sent and summed in bfloat16 or wider, within the bound.
No kernel may reach another device: no remote copies, remote signals or barrier semaphores. Data moves between devices by JAX's collectives and lax.ppermute only.
A program may use at most 256 MiB of HBM per device.

```python
import functools
import jax
import jax.numpy as jnp
from jax import lax

DT = 768
HT = 12
FT = 3072
DI = 1024
HI = 8
FI = 1024
DC = 1024
HC = 8
TSLOTS = 256
ISLOTS = 160
ROWS_DEV = 2
ROWS = 16


def segment_ids(key, slot_count, shortest, longest):
    lengths = jax.random.randint(key, (ROWS, 4), shortest, longest + 1)
    ends = jnp.cumsum(lengths, axis=1)
    positions = jnp.arange(slot_count, dtype=jnp.int32)[None, :, None]
    return jnp.sum((positions >= ends[:, None, :]).astype(jnp.int32), axis=-1).astype(jnp.int32)


def draw_text_seg(key, part):
    return segment_ids(jax.random.fold_in(key, 11), TSLOTS, 16, 60)


def draw_image_seg(key, part):
    return segment_ids(jax.random.fold_in(key, 23), ISLOTS, 10, 36)


def steps_of(stream_key, extent, split, smallest, high):
    gain = 1.0
    for axis_at, blocks in split:
        draws = jax.random.uniform(jax.random.fold_in(jax.random.fold_in(stream_key, 6), axis_at), (blocks,), jnp.float32, smallest / len(split), high / len(split))
        gain = gain * jnp.repeat(jnp.exp(draws), extent[axis_at] // blocks).reshape((-1,) + (1,) * (len(extent) - 1 - axis_at))
    return gain


def scatter_about(key, shape, scale, limit, pieces=(), held_as=jnp.bfloat16):
    drawn = scale * jax.random.normal(key, shape, jnp.float32)
    if pieces:
        drawn = drawn * steps_of(key, shape, pieces, -0.22, 0.18)
    return jnp.clip(drawn, -limit, limit).astype(held_as)


def setup_inputs(seed: int = 0) -> dict:
    splits = jax.random.split(jax.random.key(seed), 21)
    text_in = scatter_about(splits[0], (ROWS, TSLOTS, DT), 1.0, 6.0, ((0, 8), (1, 4)))
    image_in = scatter_about(splits[1], (ROWS, ISLOTS, DI), 1.0, 6.0, ((0, 8), (1, 4)))
    text_seg = draw_text_seg(jax.random.fold_in(splits[20], 71), 0)
    image_seg = draw_image_seg(jax.random.fold_in(splits[20], 71), 0)
    text_co_in = scatter_about(splits[4], (DT, 3 * DC), DT ** -0.5, 0.21875)
    image_co_in = scatter_about(splits[5], (DI, 3 * DC), DI ** -0.5, 0.1875)
    text_co_out = scatter_about(splits[6], (DC, DT), (DC // 32) ** -0.5, 1.0)
    image_co_out = scatter_about(splits[7], (DC, DI), (DC // 32) ** -0.5, 1.0)
    text_up = scatter_about(splits[8], (DT, FT), DT ** -0.5, 0.21875)
    text_down = scatter_about(splits[9], (FT, DT), (FT // 2) ** -0.5, 0.15625)
    image_up = scatter_about(splits[10], (DI, FI), DI ** -0.5, 0.1875)
    image_down = scatter_about(splits[11], (FI, DI), (FI // 2) ** -0.5, 0.25)
    text_qkv = scatter_about(splits[12], (DT, 3 * DT), DT ** -0.5, 0.21875)
    text_proj = scatter_about(splits[13], (DT, DT), (DT // 32) ** -0.5, 1.25)
    image_qkv = scatter_about(splits[14], (DI, 3 * DI), DI ** -0.5, 0.1875)
    image_proj = scatter_about(splits[15], (DI, DI), (DI // 32) ** -0.5, 1.0)
    text_gains = jnp.clip(1.0 + 0.15 * jax.random.normal(splits[16], (3, DT), jnp.float32), 0.25, 1.75)
    image_gains = jnp.clip(1.0 + 0.15 * jax.random.normal(splits[17], (3, DI), jnp.float32), 0.25, 1.75)
    text_upstream = scatter_about(splits[18], (ROWS, TSLOTS, DT), 1.0, 6.0, ((0, 8), (1, 4)))
    image_upstream = scatter_about(splits[19], (ROWS, ISLOTS, DI), 1.0, 6.0, ((0, 8), (1, 4)))
    return {"text_in": text_in, "image_in": image_in, "text_seg": text_seg, "image_seg": image_seg, "text_co_in": text_co_in, "image_co_in": image_co_in, "text_co_out": text_co_out, "image_co_out": image_co_out, "text_up": text_up, "text_down": text_down, "image_up": image_up, "image_down": image_down, "text_qkv": text_qkv, "text_proj": text_proj, "image_qkv": image_qkv, "image_proj": image_proj, "text_gains": text_gains, "image_gains": image_gains, "text_upstream": text_upstream, "image_upstream": image_upstream}


@jax.custom_vjp
def low(v):
    return lax.optimization_barrier(v.astype(jnp.bfloat16)).astype(jnp.float32)

@jax.custom_vjp
def low_back(v):
    return v

def low_keep(v):
    return (low(v), None)

def low_pass(kept, grad):
    return (grad,)

def back_keep(v):
    return (v, None)

def back_low(kept, grad):
    return (low(grad),)
low.defvjp(low_keep, low_pass)
low_back.defvjp(back_keep, back_low)
NEG_FILL = -1000000000.0
NORM_EPS = 1e-05
EXACT = lax.Precision.HIGHEST

def project(acts, weight):
    return jnp.einsum('rld,de->rle', acts, weight, precision=EXACT)

def layer_norm(summed, gain_row):
    center = summed - lax.optimization_barrier(jnp.mean(summed, axis=-1, keepdims=True))
    spread = lax.optimization_barrier(jnp.mean(center * center, axis=-1, keepdims=True))
    return center * lax.rsqrt(spread + NORM_EPS) * gain_row

def rounded_three(merged):
    third = merged.shape[-1] // 3
    return (low_back(low(merged[..., :third])), low_back(low(merged[..., third:2 * third])), low_back(low(merged[..., 2 * third:])))

def attention(queries, key_rows, values, allowed, head_count):
    row_count, query_len, full_width = queries.shape
    key_len = key_rows.shape[1]
    head_size = full_width // head_count
    query_heads = queries.reshape(row_count, query_len, head_count, head_size)
    key_heads = key_rows.reshape(row_count, key_len, head_count, head_size)
    value_heads = values.reshape(row_count, key_len, head_count, head_size)
    scores = jnp.einsum('rqhd,rkhd->rhqk', query_heads, key_heads, precision=EXACT) * head_size ** (-0.5)
    scores = low_back(jnp.where(allowed[:, None], scores, NEG_FILL))
    weights = low(jax.nn.softmax(scores, axis=-1))
    context = jnp.einsum('rhqk,rkhd->rqhd', weights, value_heads, precision=EXACT)
    return low_back(low(context.reshape(row_count, query_len, full_width)))

def forward(text_seg, image_seg, text_in, image_in, params):
    text_co_in, image_co_in, text_co_out, image_co_out, text_up, text_down, image_up, image_down, text_qkv, text_proj, image_qkv, image_proj, text_gains, image_gains = params
    text_cross = text_seg[:, :, None] == image_seg[:, None, :]
    image_cross = image_seg[:, :, None] == text_seg[:, None, :]
    text_self = text_seg[:, :, None] == text_seg[:, None, :]
    image_self = image_seg[:, :, None] == image_seg[:, None, :]
    text_query, text_key, text_value = rounded_three(project(low(text_in), text_co_in))
    image_query, image_key, image_value = rounded_three(project(low(image_in), image_co_in))
    text_att = attention(text_query, image_key, image_value, text_cross, HC)
    image_att = attention(image_query, text_key, text_value, image_cross, HC)
    text_first = layer_norm(text_in + low_back(project(text_att, text_co_out)), text_gains[0])
    image_first = layer_norm(image_in + low_back(project(image_att, image_co_out)), image_gains[0])
    text_hidden = low_back(project(low(text_first), text_up))
    image_hidden = low_back(project(low(image_first), image_up))
    text_ffn = low_back(project(low(jax.nn.gelu(text_hidden, approximate=True)), text_down))
    image_ffn = low_back(project(low(jax.nn.gelu(image_hidden, approximate=True)), image_down))
    text_second = layer_norm(text_first + text_ffn, text_gains[1])
    image_second = layer_norm(image_first + image_ffn, image_gains[1])
    self_tq, self_tk, self_tv = rounded_three(project(low(text_second), text_qkv))
    self_iq, self_ik, self_iv = rounded_three(project(low(image_second), image_qkv))
    text_mix = attention(self_tq, self_tk, self_tv, text_self, HT)
    image_mix = attention(self_iq, self_ik, self_iv, image_self, HI)
    text_third = layer_norm(text_second + low_back(project(text_mix, text_proj)), text_gains[2])
    image_third = layer_norm(image_second + low_back(project(image_mix, image_proj)), image_gains[2])
    return (text_third, image_third)

def reference(text_in, image_in, text_seg, image_seg, text_co_in, image_co_in, text_co_out, image_co_out, text_up, text_down, image_up, image_down, text_qkv, text_proj, image_qkv, image_proj, text_gains, image_gains, text_upstream, image_upstream):
    params = tuple((member.astype(jnp.float32) for member in (text_co_in, image_co_in, text_co_out, image_co_out, text_up, text_down, image_up, image_down, text_qkv, text_proj, image_qkv, image_proj, text_gains, image_gains)))
    group_total = ROWS // ROWS_DEV

    def split_rows(source):
        return source.reshape((group_total, ROWS_DEV) + source.shape[1:])
    group_inputs = (split_rows(text_in.astype(jnp.float32)), split_rows(image_in.astype(jnp.float32)), split_rows(text_seg), split_rows(image_seg), split_rows(text_upstream.astype(jnp.float32)), split_rows(image_upstream.astype(jnp.float32)))

    def group_step(totals, group_data):
        text_part, image_part, text_ids, image_ids, text_back, image_back = group_data
        outputs, pullback = jax.vjp(functools.partial(forward, text_ids, image_ids), text_part, image_part, params)
        text_grad, image_grad, weight_grads = pullback((text_back, image_back))
        totals = jax.tree.map(jnp.add, totals, weight_grads)
        return (totals, (outputs[0], outputs[1], text_grad, image_grad))
    zero_grads = jax.tree.map(jnp.zeros_like, params)
    totals, stacked = lax.scan(group_step, zero_grads, group_inputs)

    def join_rows(source):
        return source.reshape((ROWS,) + source.shape[2:])
    return (join_rows(stacked[0]).astype(jnp.bfloat16), join_rows(stacked[1]).astype(jnp.bfloat16), join_rows(stacked[2]), join_rows(stacked[3]), totals[0], totals[1], totals[2], totals[3], totals[4], totals[5], totals[6], totals[7], totals[8], totals[9], totals[10], totals[11], totals[12], totals[13])
```

```python
import functools

import jax
import jax.numpy as jnp
from jax import lax
from jax.experimental import pallas as pl
from jax.experimental.pallas import tpu as pltpu
from jax.sharding import PartitionSpec as P

HT = 12
HI = 8
HC = 8

NORM_EPS = 1e-05

F32 = jnp.float32
BF16 = jnp.bfloat16
LOG2E = 1.4426950408889634
MASKED = -1.0e9 * LOG2E
LANES = 128


def dot_nt(a, b):
    return lax.dot_general(a, b, (((1,), (1,)), ((), ())), preferred_element_type=F32)


def dot_nn(a, b):
    return lax.dot_general(a, b, (((1,), (0,)), ((), ())), preferred_element_type=F32)


def dot_tn(a, b):
    return lax.dot_general(a, b, (((0,), (0,)), ((), ())), preferred_element_type=F32)


def lane_cols(ref, at):
    return ref[0, :, at * LANES : (at + 1) * LANES]


def lane_halves(width):
    lane = lax.broadcasted_iota(jnp.int32, (1, LANES), 1)
    if width == LANES:
        return [None]
    return [(lane // width) == i for i in range(LANES // width)]


def keep_lanes(x, sel):
    return x if sel is None else jnp.where(sel, x, jnp.zeros_like(x))


def attend_heads(q_ref, q_at, k_ref, k_at, v_ref, v_at, bias, o_ref, o_at, p_ref, width, count):
    scale = width**-0.5 * LOG2E
    sels = lane_halves(width)
    for t in range(count):
        q = lane_cols(q_ref, q_at + t)
        k = lane_cols(k_ref, k_at + t)
        v = lane_cols(v_ref, v_at + t)
        out = None
        for i, sel in enumerate(sels):
            s = dot_nt(k, keep_lanes(q, sel)) * scale + bias
            e = jnp.exp2(s - jnp.max(s, axis=0, keepdims=True))
            p = (e * (1.0 / jnp.sum(e, axis=0, keepdims=True))).astype(BF16)
            p_ref[0, t * len(sels) + i] = p
            o = dot_tn(p, v)
            out = o if out is None else jnp.where(sel, o, out)
        o_ref[0, :, (o_at + t) * LANES : (o_at + t + 1) * LANES] = out.astype(BF16)


def attend_heads_back(
    q_ref, q_at, k_ref, k_at, v_ref, v_at, da_ref, p_ref, dq_ref, dk_ref, dv_ref, width, count
):
    scale = width**-0.5
    sels = lane_halves(width)
    for t in range(count):
        q = lane_cols(q_ref, q_at + t)
        k = lane_cols(k_ref, k_at + t)
        v = lane_cols(v_ref, v_at + t)
        da = lane_cols(da_ref, t)
        dq = dk = dv = None
        for i, sel in enumerate(sels):
            p = p_ref[0, t * len(sels) + i]
            da_h = keep_lanes(da, sel)
            dp = dot_nt(v, da_h)
            pf = p.astype(F32)
            w = pf * dp
            ds = (w - pf * jnp.sum(w, axis=0, keepdims=True)).astype(BF16)
            dv_h = dot_nn(p, da_h)
            dk_h = dot_nn(ds, keep_lanes(q, sel))
            dq_h = dot_tn(ds, keep_lanes(k, sel))
            dq = dq_h if dq is None else dq + dq_h
            dk = dk_h if dk is None else dk + dk_h
            dv = dv_h if dv is None else dv + dv_h
        for ref, at, val in (
            (dq_ref, q_at, dq * scale),
            (dk_ref, k_at, dk * scale),
            (dv_ref, v_at, dv),
        ):
            ref[0, :, (at + t) * LANES : (at + t + 1) * LANES] = val.astype(BF16)


def bias_of(key_col, query_row):
    return jnp.where(key_col == query_row, 0.0, MASKED).astype(F32)


def co_fwd_body(t_ref, i_ref, tc_ref, tr_ref, ic_ref, ir_ref, ot_ref, oi_ref, pt_ref, pi_ref, *, width):
    n = ot_ref.shape[2] // LANES
    bias_t = bias_of(ic_ref[0], tr_ref[0])
    attend_heads(t_ref, 0, i_ref, n, i_ref, 2 * n, bias_t, ot_ref, 0, pt_ref, width, n)
    bias_i = bias_of(tc_ref[0], ir_ref[0])
    attend_heads(i_ref, 0, t_ref, n, t_ref, 2 * n, bias_i, oi_ref, 0, pi_ref, width, n)


def self_fwd_body(t_ref, i_ref, tc_ref, tr_ref, ic_ref, ir_ref, ot_ref, oi_ref, pt_ref, pi_ref, *, tw, iw):
    nt = ot_ref.shape[2] // LANES
    ni = oi_ref.shape[2] // LANES
    attend_heads(t_ref, 0, t_ref, nt, t_ref, 2 * nt, bias_of(tc_ref[0], tr_ref[0]), ot_ref, 0, pt_ref, tw, nt)
    attend_heads(i_ref, 0, i_ref, ni, i_ref, 2 * ni, bias_of(ic_ref[0], ir_ref[0]), oi_ref, 0, pi_ref, iw, ni)


def co_bwd_body(t_ref, i_ref, dt_ref, di_ref, pt_ref, pi_ref, gt_ref, gi_ref, *, width):
    n = dt_ref.shape[2] // LANES
    attend_heads_back(t_ref, 0, i_ref, n, i_ref, 2 * n, dt_ref, pt_ref, gt_ref, gi_ref, gi_ref, width, n)
    attend_heads_back(i_ref, 0, t_ref, n, t_ref, 2 * n, di_ref, pi_ref, gi_ref, gt_ref, gt_ref, width, n)


def self_bwd_body(t_ref, i_ref, dt_ref, di_ref, pt_ref, pi_ref, gt_ref, gi_ref, *, tw, iw):
    nt = dt_ref.shape[2] // LANES
    ni = di_ref.shape[2] // LANES
    attend_heads_back(t_ref, 0, t_ref, nt, t_ref, 2 * nt, dt_ref, pt_ref, gt_ref, gt_ref, gt_ref, tw, nt)
    attend_heads_back(i_ref, 0, i_ref, ni, i_ref, 2 * ni, di_ref, pi_ref, gi_ref, gi_ref, gi_ref, iw, ni)


def row_spec(shape):
    return pl.BlockSpec((1,) + tuple(shape[1:]), lambda r: (r,) + (0,) * (len(shape) - 1))


def by_rows(body, ins, outs, name):
    rows = ins[0].shape[0]
    return pl.pallas_call(
        body,
        grid=(rows,),
        in_specs=[row_spec(a.shape) for a in ins],
        out_specs=[row_spec(o.shape) for o in outs],
        out_shape=outs,
        compiler_params=pltpu.CompilerParams(
            vmem_limit_bytes=grant([((1,) + a.shape[1:], a.dtype) for a in (*ins, *outs)], [], 4)
        ),
        name=name,
    )(*ins)


def seg_views(tseg, iseg):
    return (tseg[:, :, None], tseg[:, None, :], iseg[:, :, None], iseg[:, None, :])


def co_attention(tqkv, iqkv, segs, heads):
    r, lt, w = tqkv.shape
    li = iqkv.shape[1]
    w //= 3
    outs = [
        jax.ShapeDtypeStruct((r, lt, w), BF16),
        jax.ShapeDtypeStruct((r, li, w), BF16),
        jax.ShapeDtypeStruct((r, heads, li, lt), BF16),
        jax.ShapeDtypeStruct((r, heads, lt, li), BF16),
    ]
    return by_rows(functools.partial(co_fwd_body, width=w // heads), (tqkv, iqkv) + segs, outs, "co_fwd")


def self_attention(tqkv, iqkv, segs, theads, iheads):
    r, lt, wt = tqkv.shape
    li, wi = iqkv.shape[1:]
    wt //= 3
    wi //= 3
    outs = [
        jax.ShapeDtypeStruct((r, lt, wt), BF16),
        jax.ShapeDtypeStruct((r, li, wi), BF16),
        jax.ShapeDtypeStruct((r, theads, lt, lt), BF16),
        jax.ShapeDtypeStruct((r, iheads, li, li), BF16),
    ]
    body = functools.partial(self_fwd_body, tw=wt // theads, iw=wi // iheads)
    return by_rows(body, (tqkv, iqkv) + segs, outs, "self_fwd")


def co_attention_back(tqkv, iqkv, dt, di, pt, pi, heads):
    outs = [jax.ShapeDtypeStruct(tqkv.shape, BF16), jax.ShapeDtypeStruct(iqkv.shape, BF16)]
    body = functools.partial(co_bwd_body, width=dt.shape[2] // heads)
    return by_rows(body, (tqkv, iqkv, dt, di, pt, pi), outs, "co_bwd")


def self_attention_back(tqkv, iqkv, dt, di, pt, pi, theads, iheads):
    outs = [jax.ShapeDtypeStruct(tqkv.shape, BF16), jax.ShapeDtypeStruct(iqkv.shape, BF16)]
    body = functools.partial(self_bwd_body, tw=dt.shape[2] // theads, iw=di.shape[2] // iheads)
    return by_rows(body, (tqkv, iqkv, dt, di, pt, pi), outs, "self_bwd")


TILE = 256
GAIN_ROWS = 32


def wgrad_body(scal_ref, *refs, plan, ndp, gains, gains_at):
    n = len(plan)
    xs, ys = refs[:n], refs[n : 2 * n]
    gain_refs = refs[2 * n : 2 * n + gains]
    keep_ref, send_ref = refs[2 * n + gains : 2 * n + gains + 2]
    if gains:
        rows_ref = refs[-1]
        at = 0
        for ref in gain_refs:
            total = jnp.sum(ref[...], axis=0, keepdims=True)
            for c in range(0, ref.shape[1], TILE):
                rows_ref[at : at + 1] = total[:, c : c + TILE]
                at += 1
        for at in range(at, GAIN_ROWS):
            rows_ref[at : at + 1] = jnp.zeros((1, TILE), F32)
        low = rows_ref[...].astype(BF16)
        for j in range(ndp // 2):
            keep_ref[j, gains_at : gains_at + GAIN_ROWS] = low
            send_ref[j, gains_at : gains_at + GAIN_ROWS] = low
    odd = scal_ref[0] == 1
    for (x_ref, y_ref), (tiles, total, split, off) in zip(zip(xs, ys), plan):
        xt = jnp.transpose(x_ref[...])
        rows = xt.shape[0] // ndp
        for t in range(tiles):
            if split:
                first = jnp.minimum(scal_ref[1] * tiles, total - tiles) + t
                dy = y_ref[:, pl.ds(pl.multiple_of(first * TILE, TILE), TILE)]
            else:
                dy = y_ref[:, t * TILE : (t + 1) * TILE]
            g = dot_nn(xt, dy).astype(BF16)
            at = off + t * rows
            for j in range(ndp // 2):
                even_rows = g[2 * j * rows : (2 * j + 1) * rows]
                odd_rows = g[(2 * j + 1) * rows : (2 * j + 2) * rows]
                keep_ref[j, at : at + rows] = jnp.where(odd, odd_rows, even_rows)
                send_ref[j, at : at + rows] = jnp.where(odd, even_rows, odd_rows)


def unpack_body(scal_ref, *refs, plan, nseq, gains_at):
    z = scal_ref[1]
    all_refs, own_ref = refs[:nseq], refs[nseq]
    refs = refs[nseq - 1 :]
    outs = refs[2 : 2 + len(plan)]
    if len(refs) > 2 + len(plan):
        low = own_ref[gains_at : gains_at + GAIN_ROWS].astype(F32)
        at = 0
        for out in refs[2 + len(plan) :]:
            for k in range(out.shape[0]):
                for c in range(0, out.shape[1], TILE):
                    out[k : k + 1, c : c + TILE] = low[at : at + 1]
                    at += 1
    for out, (tiles, total, split, off, rows) in zip(outs, plan):
        if split:
            for k, ref in enumerate(all_refs):
                first = jnp.minimum((z ^ k) * tiles, total - tiles)
                for t in range(tiles):
                    c = pl.multiple_of((first + t) * TILE, TILE)
                    out[:, pl.ds(c, TILE)] = ref[off + t * rows : off + (t + 1) * rows].astype(F32)
        else:
            for t in range(tiles):
                out[:, t * TILE : (t + 1) * TILE] = own_ref[off + t * rows : off + (t + 1) * rows].astype(F32)


def whole(memory_space=None):
    return pl.BlockSpec(memory_space=memory_space or pltpu.VMEM)


def pick(at, values):
    out = values[0]
    for k in range(1, len(values)):
        out = jnp.where(at == k, values[k], out)
    return out


def join_body(scal_ref, *refs, nseq):
    z = scal_ref[1]
    for ref, parts in ((refs[2 * nseq], refs[:nseq]), (refs[2 * nseq + 1], refs[nseq : 2 * nseq])):
        count = parts[0].shape[1]
        for r in range(ref.shape[0]):
            values = [p[r] for p in parts]
            for k in range(nseq):
                ref[r, k * count : (k + 1) * count] = pick(z ^ k, values)


def pack_body(t_ref, i_ref, o_ref):
    at = 0
    for ref in (t_ref, i_ref):
        for c in range(0, ref.shape[2], TILE):
            for r in range(ref.shape[0]):
                part = ref[r, :, c : c + TILE]
                for k in range(o_ref.shape[0]):
                    o_ref[k, at : at + part.shape[0]] = part
                at += part.shape[0]


def unpack_pair_body(g_ref, t_ref, i_ref, *, nseq, lt, li):
    at = 0
    for ref, count in ((t_ref, lt), (i_ref, li)):
        for c in range(0, ref.shape[2], TILE):
            for r in range(ref.shape[0]):
                for k in range(nseq):
                    ref[r, k * count : (k + 1) * count, c : c + TILE] = g_ref[k, at : at + count]
                at += count


class Comm:
    def __init__(self):
        self.nseq = lax.axis_size("seq")
        self.ndp = lax.axis_size("dp")
        self.z = lax.axis_index("seq")
        self.d = lax.axis_index("dp")
        self.scal = jnp.stack([self.d % 2, self.z]).astype(jnp.int32)

    def spread(self, copies):
        return lax.all_to_all(copies, "seq", split_axis=0, concat_axis=0, tiled=True)

    def pieces(self, x):
        n = self.nseq
        return [x] + [lax.ppermute(x, "seq", [(i, i ^ k) for i in range(n)]) for k in range(1, n)]

    def gather_pair(self, text, image):
        n = self.nseq
        rows, lt, wt = text.shape
        li, wi = image.shape[1:]
        parts = self.pieces(text) + self.pieces(image)
        return pl.pallas_call(
            functools.partial(join_body, nseq=n),
            in_specs=[whole(pltpu.SMEM)] + [whole()] * (2 * n),
            out_specs=[whole(), whole()],
            out_shape=[
                jax.ShapeDtypeStruct((rows, n * lt, wt), BF16),
                jax.ShapeDtypeStruct((rows, n * li, wi), BF16),
            ],
            name="join",
        )(self.scal, *parts)

    def gather_pair_later(self, text, image):
        n = self.nseq
        rows, lt, wt = text.shape
        li, wi = image.shape[1:]
        total = rows * (lt * (wt // TILE) + li * (wi // TILE))
        packed = pl.pallas_call(
            pack_body,
            in_specs=[whole(), whole()],
            out_specs=whole(),
            out_shape=jax.ShapeDtypeStruct((n, total, TILE), BF16),
            name="pack",
        )(text, image)
        got = self.spread(packed)
        return pl.pallas_call(
            functools.partial(unpack_pair_body, nseq=n, lt=lt, li=li),
            in_specs=[whole()],
            out_specs=[whole(), whole()],
            out_shape=[
                jax.ShapeDtypeStruct((rows, n * lt, wt), BF16),
                jax.ShapeDtypeStruct((rows, n * li, wi), BF16),
            ],
            name="unpack_pair",
        )(got)

    def own_slots(self, x, count):
        return lax.dynamic_slice_in_dim(x, self.z * count, count, 1)

    def plan_of(self, members):
        plan = {}
        off = 0
        for want in (True, False):
            for at, (x, y, split) in enumerate(members):
                if split != want:
                    continue
                total = y.shape[-1] // TILE
                tiles = -(-total // self.nseq) if split else total
                rows = x.shape[-1] // self.ndp
                plan[at] = (tiles, total, split, off, rows)
                off += tiles * rows
            if want:
                split_rows = off
        return [plan[i] for i in range(len(members))], split_rows, off

    def weight_grads(self, members, gains=()):
        members = [(x.reshape(-1, x.shape[-1]), y.reshape(-1, y.shape[-1]), s) for x, y, s in members]
        plan, split_rows, rows = self.plan_of(members)
        gains_at = rows
        if gains:
            rows += GAIN_ROWS
        flat_gains = [g for stream in gains for g in stream]
        half = jax.ShapeDtypeStruct((self.ndp // 2, rows, TILE), BF16)
        keep, send = pl.pallas_call(
            functools.partial(wgrad_body, plan=[p[:4] for p in plan], ndp=self.ndp, gains=len(flat_gains), gains_at=gains_at),
            in_specs=[whole(pltpu.SMEM)] + [whole()] * (2 * len(members) + len(flat_gains)),
            out_specs=[whole(), whole()],
            out_shape=[half, half],
            compiler_params=pltpu.CompilerParams(vmem_limit_bytes=12 * 1024 * 1024),
            scratch_shapes=[pltpu.VMEM((GAIN_ROWS, TILE), F32)] if gains else [],
            name="wgrad",
        )(self.scal, *[m[0] for m in members], *[m[1] for m in members], *flat_gains)
        return Group(self, plan, split_rows, rows, keep, send, gains, gains_at)


class Group:
    def __init__(self, comm, plan, split_rows, rows, keep, send, gains, gains_at):
        self.gain_shapes = [(len(stream), stream[0].shape[1]) for stream in gains]
        self.gains_at = gains_at - split_rows
        self.comm, self.plan, self.split_rows, self.rows = comm, plan, split_rows, rows
        self.keep = keep
        self.got = lax.ppermute(send, "dp", [(i, i ^ 1) for i in range(comm.ndp)])

    def cross(self):
        pair = (self.keep.astype(F32) + self.got.astype(F32)).astype(BF16)
        groups = [list(range(b, self.comm.ndp, 2)) for b in range(2)]
        self.parts = lax.all_to_all(
            pair, "dp", split_axis=0, concat_axis=0, tiled=True, axis_index_groups=groups
        )

    def along(self):
        mine = jnp.sum(self.parts.astype(F32), axis=0).astype(BF16)
        self.everyone = self.comm.pieces(mine[: self.split_rows])
        self.own = mine[self.split_rows :] if self.split_rows < self.rows else mine[:8]

    def unpack(self):
        plan = [(p[0], p[1], p[2], p[3] if p[2] else p[3] - self.split_rows, p[4]) for p in self.plan]
        outs = [jax.ShapeDtypeStruct((p[4], p[1] * TILE), F32) for p in plan]
        outs += [jax.ShapeDtypeStruct(shape, F32) for shape in self.gain_shapes]
        return pl.pallas_call(
            functools.partial(
                unpack_body, plan=plan, nseq=self.comm.nseq, gains_at=self.gains_at
            ),
            in_specs=[whole(pltpu.SMEM)] + [whole()] * (self.comm.nseq + 1),
            out_specs=[whole()] * len(outs),
            out_shape=outs,
            compiler_params=pltpu.CompilerParams(vmem_limit_bytes=12 * 1024 * 1024),
            name="unpack",
        )(self.comm.scal, *self.everyone, self.own)


def tie(*xs):
    return lax.optimization_barrier(xs)


SQRT_2_PI = 0.7978845608028654
GELU_CUBE = 0.044715


def spec(shape, index=None, memory_space=None):
    if index is None:
        zeros = (0,) * len(shape)
        return pl.BlockSpec(shape, lambda i: zeros)
    return pl.BlockSpec(shape, index)


def nbytes(shape, dtype):
    total = jnp.dtype(dtype).itemsize
    dims = list(shape)
    dims[-1] = -(-dims[-1] // 128) * 128
    dims[-2] = -(-dims[-2] // 16) * 16
    for d in dims:
        total *= d
    return total


def grant(blocks, scratch, extra):
    total = sum(2 * nbytes(b, d) for b, d in blocks) + sum(nbytes(x.shape, x.dtype) for x in scratch)
    return total + extra * 1024 * 1024


def call(body, grid, ins, in_specs, outs, out_specs, scratch, name, extra=6):
    many = isinstance(outs, list)
    blocks = [(b.block_shape, x.dtype) for b, x in zip(in_specs, ins)]
    blocks += [
        (b.block_shape, x.dtype)
        for b, x in zip(out_specs if many else [out_specs], outs if many else [outs])
    ]
    limit = grant(blocks, scratch, extra)
    return pl.pallas_call(
        body,
        grid=grid,
        in_specs=in_specs,
        out_specs=out_specs,
        out_shape=outs,
        scratch_shapes=scratch,
        compiler_params=pltpu.CompilerParams(vmem_limit_bytes=limit),
        name=name,
    )(*ins)


def chunk_of(rows):
    return 32 if rows % 32 == 0 else 16


def row_chunks(rows, body):
    size = chunk_of(rows)

    def step(i, carry):
        body(pl.ds(pl.multiple_of(i * size, size), size))
        return carry

    lax.fori_loop(0, rows // size, step, 0, unroll=2)


def normalize(z):
    center = z - jnp.mean(z, axis=-1, keepdims=True)
    inv = lax.rsqrt(jnp.mean(center * center, axis=-1, keepdims=True) + NORM_EPS)
    return center * inv, inv


def denormalize(dy, n, inv, gain):
    dn = dy * gain
    m1 = jnp.mean(dn, axis=-1, keepdims=True)
    m2 = jnp.mean(dn * n, axis=-1, keepdims=True)
    return inv * (dn - m1 - n * m2)


def fold_rows(x):
    return jnp.sum(x.reshape(x.shape[0] // 8, 8, x.shape[1]), axis=0)


def mm_body(x_ref, w_ref, o_ref):
    o_ref[...] = dot_nn(x_ref[...], w_ref[...]).astype(BF16)


def matmul(x, w, name, tile=512):
    t, k = x.shape
    n = w.shape[1]
    if n % tile:
        tile = n // 3
    return call(
        mm_body,
        (n // tile,),
        (x, w),
        [spec((t, k)), spec((k, tile), lambda i: (0, i))],
        jax.ShapeDtypeStruct((t, n), BF16),
        spec((t, tile), lambda i: (0, i)),
        [],
        name,
    )


def out_norm_body(x_ref, w_ref, res_ref, g_ref, n_ref, inv_ref, low_ref, acc_ref):
    i = pl.program_id(0)
    width = w_ref.shape[1]
    acc_ref[i] = dot_nn(x_ref[...], w_ref[...])
    steps = acc_ref.shape[0]

    @pl.when(i == steps - 1)
    def _():
        gain = g_ref[...]

        def chunk(rows):
            z = jnp.concatenate([acc_ref[s, rows] for s in range(steps)], axis=-1)
            n, inv = normalize(z + res_ref[rows].astype(F32))
            n_ref[rows] = n
            inv_ref[rows] = inv
            low_ref[rows] = (n * gain).astype(BF16)

        row_chunks(x_ref.shape[0], chunk)


def out_norm(x, w, res, gain, name):
    t, k = x.shape
    d = w.shape[1]
    return call(
        out_norm_body,
        (d // TILE,),
        (x, w, res, gain),
        [spec((t, k)), spec((k, TILE), lambda i: (0, i)), spec((t, d)), spec((1, d))],
        [
            jax.ShapeDtypeStruct((t, d), F32),
            jax.ShapeDtypeStruct((t, 1), F32),
            jax.ShapeDtypeStruct((t, d), BF16),
        ],
        [spec((t, d)), spec((t, 1)), spec((t, d))],
        [pltpu.VMEM((d // TILE, t, TILE), F32)],
        name,
    )


def gelu_pair(v):
    v2 = v * v
    s = 0.5 + 0.5 * jnp.tanh(v * (SQRT_2_PI + (SQRT_2_PI * GELU_CUBE) * v2))
    a = v * s
    return a, s + a * (1.0 - s) * (2.0 * SQRT_2_PI + (6.0 * SQRT_2_PI * GELU_CUBE) * v2)


def ffn_body(low_ref, up_ref, down_ref, n1_ref, g1_ref, g2_ref, a_ref, slope_ref, n_ref, inv_ref, o_ref, acc_ref):
    i = pl.program_id(0)
    a, slope = gelu_pair(dot_nn(low_ref[...], up_ref[...]))
    a = a.astype(BF16)
    a_ref[...] = a
    slope_ref[...] = slope.astype(BF16)
    part = dot_nn(a, down_ref[...])

    @pl.when(i == 0)
    def _():
        acc_ref[...] = part

    @pl.when(i > 0)
    def _():
        acc_ref[...] += part

    @pl.when(i == pl.num_programs(0) - 1)
    def _():
        g1 = g1_ref[...]
        g2 = g2_ref[...]

        def chunk(rows):
            n, inv = normalize(n1_ref[rows] * g1 + acc_ref[rows])
            n_ref[rows] = n
            inv_ref[rows] = inv
            o_ref[rows] = (n * g2).astype(BF16)

        row_chunks(low_ref.shape[0], chunk)


def ffn(low, up, down, n1, g1, g2, name):
    t, d = low.shape
    f = up.shape[1]
    tile = 512
    return call(
        ffn_body,
        (f // tile,),
        (low, up, down, n1, g1, g2),
        [
            spec((t, d)),
            spec((d, tile), lambda i: (0, i)),
            spec((tile, d), lambda i: (i, 0)),
            spec((t, d)),
            spec((1, d)),
            spec((1, d)),
        ],
        [
            jax.ShapeDtypeStruct((t, f), BF16),
            jax.ShapeDtypeStruct((t, f), BF16),
            jax.ShapeDtypeStruct((t, d), F32),
            jax.ShapeDtypeStruct((t, 1), F32),
            jax.ShapeDtypeStruct((t, d), BF16),
        ],
        [
            spec((t, tile), lambda i: (0, i)),
            spec((t, tile), lambda i: (0, i)),
            spec((t, d)),
            spec((t, 1)),
            spec((t, d)),
        ],
        [pltpu.VMEM((t, d), F32)],
        name,
    )


def turn_body(
    z_ref, mix_ref, w_ref, n2_ref, g2_ref, g3_ref, up_ref, res_ref, d_ref, low_ref, dmix_ref, dg_ref, acc_ref, n_ref, *, rows_of, count
):
    acc_ref[...] = dot_nn(mix_ref[...], w_ref[...])
    g2 = g2_ref[...]
    g3 = g3_ref[...]
    dg_ref[...] = jnp.zeros_like(dg_ref)

    def chunk(rows):
        n, inv = normalize(n2_ref[rows] * g2 + acc_ref[rows])
        n_ref[rows] = n
        dy = up_ref[rows].astype(F32)
        d = denormalize(dy, n, inv, g3)
        d_ref[rows] = d
        low_ref[rows] = d.astype(BF16)
        dg_ref[...] += fold_rows(dy * n)

    row_chunks(mix_ref.shape[0], chunk)
    dmix_ref[...] = dot_nt(low_ref[...], w_ref[...]).astype(BF16)
    for r in range(res_ref.shape[0]):
        own = n_ref[pl.ds(pl.multiple_of(r * rows_of + z_ref[0] * count, 8), count)]
        res_ref[r] = (own * g3).astype(BF16)


def turn(z, mix, w, n2, g2, g3, upstream, rows, count, name):
    t, k = mix.shape
    d = w.shape[1]
    ins = (z, mix, w, n2, g2, g3, upstream)
    return pl.pallas_call(
        functools.partial(turn_body, rows_of=t // rows, count=count),
        in_specs=[whole(pltpu.SMEM)] + [whole()] * 6,
        out_specs=[whole()] * 5,
        out_shape=[
            jax.ShapeDtypeStruct((rows, count, d), BF16),
            jax.ShapeDtypeStruct((t, d), F32),
            jax.ShapeDtypeStruct((t, d), BF16),
            jax.ShapeDtypeStruct((t, k), BF16),
            jax.ShapeDtypeStruct((8, d), F32),
        ],
        scratch_shapes=[pltpu.VMEM((t, d), F32), pltpu.VMEM((t, d), F32)],
        compiler_params=pltpu.CompilerParams(vmem_limit_bytes=12 * 1024 * 1024),
        name=name,
    )(*ins)


def norm_back(acc_ref, dres_ref, n_ref, inv_ref, gain, d_ref, low_ref, dg_ref):
    dg_ref[...] = jnp.zeros_like(dg_ref)

    def chunk(rows):
        dy = dres_ref[rows] + acc_ref[rows]
        n = n_ref[rows]
        d = denormalize(dy, n, inv_ref[rows], gain)
        d_ref[rows] = d
        low_ref[rows] = d.astype(BF16)
        dg_ref[...] += fold_rows(dy * n)

    row_chunks(n_ref.shape[0], chunk)


def qkv_back_body(dx_ref, w_ref, dres_ref, n_ref, inv_ref, g_ref, d_ref, low_ref, dg_ref, acc_ref):
    i = pl.program_id(0)
    part = dot_nt(dx_ref[...], w_ref[...])

    @pl.when(i == 0)
    def _():
        acc_ref[...] = part

    @pl.when(i > 0)
    def _():
        acc_ref[...] += part

    @pl.when(i == pl.num_programs(0) - 1)
    def _():
        norm_back(acc_ref, dres_ref, n_ref, inv_ref, g_ref[...], d_ref, low_ref, dg_ref)


def qkv_back(dx, w, dres, n, inv, gain, name):
    t, m = dx.shape
    d = w.shape[0]
    tile = m // 3
    return call(
        qkv_back_body,
        (3,),
        (dx, w, dres, n, inv, gain),
        [
            spec((t, tile), lambda i: (0, i)),
            spec((d, tile), lambda i: (0, i)),
            spec((t, d)),
            spec((t, d)),
            spec((t, 1)),
            spec((1, d)),
        ],
        [
            jax.ShapeDtypeStruct((t, d), F32),
            jax.ShapeDtypeStruct((t, d), BF16),
            jax.ShapeDtypeStruct((8, d), F32),
        ],
        [spec((t, d)), spec((t, d)), spec((8, d))],
        [pltpu.VMEM((t, d), F32)],
        name,
    )


def ffn_back_body(
    low_ref, down_ref, slope_ref, up_ref, dres_ref, n_ref, inv_ref, g_ref, wo_ref, dh_ref, d_ref, dlow_ref, datt_ref, dg_ref, acc_ref
):
    i = pl.program_id(0)
    dh = (dot_nt(low_ref[...], down_ref[...]) * slope_ref[...].astype(F32)).astype(BF16)
    dh_ref[...] = dh
    part = dot_nt(dh, up_ref[...])

    @pl.when(i == 0)
    def _():
        acc_ref[...] = part

    @pl.when(i > 0)
    def _():
        acc_ref[...] += part

    @pl.when(i == pl.num_programs(0) - 1)
    def _():
        norm_back(acc_ref, dres_ref, n_ref, inv_ref, g_ref[...], d_ref, dlow_ref, dg_ref)
        datt_ref[...] = dot_nt(dlow_ref[...], wo_ref[...]).astype(BF16)


def ffn_back(low, down, slope, up, dres, n, inv, gain, wo, name):
    t, d = low.shape
    f = up.shape[1]
    tile = 512
    return call(
        ffn_back_body,
        (f // tile,),
        (low, down, slope, up, dres, n, inv, gain, wo),
        [
            spec((t, d)),
            spec((tile, d), lambda i: (i, 0)),
            spec((t, tile), lambda i: (0, i)),
            spec((d, tile), lambda i: (0, i)),
            spec((t, d)),
            spec((t, d)),
            spec((t, 1)),
            spec((1, d)),
            spec(wo.shape),
        ],
        [
            jax.ShapeDtypeStruct((t, f), BF16),
            jax.ShapeDtypeStruct((t, d), F32),
            jax.ShapeDtypeStruct((t, d), BF16),
            jax.ShapeDtypeStruct((t, wo.shape[0]), BF16),
            jax.ShapeDtypeStruct((8, d), F32),
        ],
        [
            spec((t, tile), lambda i: (0, i)),
            spec((t, d)),
            spec((t, d)),
            spec((t, wo.shape[0])),
            spec((8, d)),
        ],
        [pltpu.VMEM((t, d), F32)],
        name,
    )


def in_back_body(z_ref, dx_ref, w_ref, d_ref, o_ref):
    i = pl.program_id(0)
    dx = dx_ref[...]
    part = dot_nt(dx.reshape(dx.shape[0] * dx.shape[1], dx.shape[2]), w_ref[...]).reshape(o_ref.shape)

    @pl.when(i == 0)
    def _():
        o_ref[...] = d_ref[...] + part

    @pl.when(i > 0)
    def _():
        o_ref[...] += part


def in_back(z, dx, w, d1, count, name):
    r, _, m = dx.shape
    d = w.shape[0]
    tile = 1024
    return pl.pallas_call(
        in_back_body,
        grid_spec=pltpu.PrefetchScalarGridSpec(
            num_scalar_prefetch=1,
            grid=(m // tile,),
            in_specs=[
                pl.BlockSpec((r, count, tile), lambda i, z: (0, z[0], i)),
                pl.BlockSpec((d, tile), lambda i, z: (0, i)),
                pl.BlockSpec((r, count, d), lambda i, z: (0, z[0], 0)),
            ],
            out_specs=pl.BlockSpec((r, count, d), lambda i, z: (0, 0, 0)),
        ),
        out_shape=jax.ShapeDtypeStruct((r, count, d), F32),
        compiler_params=pltpu.CompilerParams(vmem_limit_bytes=12 * 1024 * 1024),
        name=name,
    )(z, dx, w, d1)


def per_device(
    text_in,
    image_in,
    text_seg,
    image_seg,
    text_co_in,
    image_co_in,
    text_co_out,
    image_co_out,
    text_up,
    text_down,
    image_up,
    image_down,
    text_qkv,
    text_proj,
    image_qkv,
    image_proj,
    text_gains,
    image_gains,
    text_upstream,
    image_upstream,
):
    comm = Comm()
    nt = text_in.shape[1]
    ni = image_in.shape[1]
    text_full, image_full = comm.gather_pair(text_in, image_in)
    text_upstream, image_upstream, text_full, image_full = tie(
        text_upstream, image_upstream, text_full, image_full
    )
    text_up_full, image_up_full = comm.gather_pair_later(text_upstream, image_upstream)
    segs = seg_views(text_seg, image_seg)

    zs = comm.z.reshape(1).astype(jnp.int32)
    rows = text_in.shape[0]
    tg = [text_gains[k : k + 1] for k in range(3)]
    ig = [image_gains[k : k + 1] for k in range(3)]

    def flat(x):
        return x.reshape(-1, x.shape[-1])

    def deep(x):
        return x.reshape(rows, -1, x.shape[-1])

    tx = flat(text_full)
    ix = flat(image_full)
    tqkv = deep(matmul(tx, text_co_in, "t_co"))
    iqkv = deep(matmul(ix, image_co_in, "i_co"))
    text_att, image_att, co_pt, co_pi = co_attention(tqkv, iqkv, segs, HC)
    text_att = flat(text_att)
    image_att = flat(image_att)
    tn1, tr1, t1 = out_norm(text_att, text_co_out, tx, tg[0], "t_norm1")
    in1, ir1, i1 = out_norm(image_att, image_co_out, ix, ig[0], "i_norm1")
    ta, tslope, tn2, tr2, t2 = ffn(t1, text_up, text_down, tn1, tg[0], tg[1], "t_ffn")
    ia, islope, in2, ir2, i2 = ffn(i1, image_up, image_down, in1, ig[0], ig[1], "i_ffn")
    sqkv = deep(matmul(t2, text_qkv, "t_qkv"))
    uqkv = deep(matmul(i2, image_qkv, "i_qkv"))
    text_mix, image_mix, self_pt, self_pi = self_attention(sqkv, uqkv, segs, HT, HI)
    text_mix = flat(text_mix)
    image_mix = flat(image_mix)
    text_result, d3, d3b, dmt, tdg3 = turn(
        zs, text_mix, text_proj, tn2, tg[1], tg[2], flat(text_up_full), rows, nt, "t_turn"
    )
    image_result, e3, e3b, dmi, idg3 = turn(
        zs, image_mix, image_proj, in2, ig[1], ig[2], flat(image_up_full), rows, ni, "i_turn"
    )
    dsqkv, duqkv = self_attention_back(
        sqkv, uqkv, deep(dmt), deep(dmi), self_pt, self_pi, HT, HI
    )
    group_1 = comm.weight_grads(
        [(text_mix, d3b, False), (image_mix, e3b, True), (t2, dsqkv, True), (i2, duqkv, True)]
    )
    d2, d2b, tdg2 = qkv_back(flat(dsqkv), text_qkv, d3, tn2, tr2, tg[1], "t_qkv_back")
    e2, e2b, idg2 = qkv_back(flat(duqkv), image_qkv, e3, in2, ir2, ig[1], "i_qkv_back")
    group_1.got, d2b, e2b = tie(group_1.got, d2b, e2b)
    group_1.cross()
    dht, d1, d1b, dat, tdg1 = ffn_back(
        d2b, text_down, tslope, text_up, d2, tn1, tr1, tg[0], text_co_out, "t_ffn_back"
    )
    dhi, e1, e1b, dai, idg1 = ffn_back(
        e2b, image_down, islope, image_up, e2, in1, ir1, ig[0], image_co_out, "i_ffn_back"
    )
    group_1.parts, dht, dhi = tie(group_1.parts, dht, dhi)
    group_1.along()
    group_2 = comm.weight_grads(
        [(ta, d2b, False), (ia, e2b, True), (t1, dht, True), (i1, dhi, True)]
    )
    dt, di = co_attention_back(tqkv, iqkv, deep(dat), deep(dai), co_pt, co_pi, HC)
    group_2.got, dt, di = tie(group_2.got, dt, di)
    group_2.cross()
    group_3 = comm.weight_grads(
        [(text_att, d1b, False), (image_att, e1b, True), (tx, dt, True), (ix, di, True)],
        [(tdg1, tdg2, tdg3), (idg1, idg2, idg3)],
    )
    text_in_grad = in_back(zs, dt, text_co_in, deep(d1), nt, "t_in_back")
    image_in_grad = in_back(zs, di, image_co_in, deep(e1), ni, "i_in_back")
    group_2.parts, group_3.got, text_in_grad, image_in_grad = tie(
        group_2.parts, group_3.got, text_in_grad, image_in_grad
    )
    group_2.along()
    group_3.cross()
    *group_1.everyone, group_3.parts = tie(*group_1.everyone, group_3.parts)
    group_3.along()
    text_proj_grad, image_proj_grad, text_qkv_grad, image_qkv_grad = group_1.unpack()
    text_down_grad, image_down_grad, text_up_grad, image_up_grad = group_2.unpack()
    (
        text_co_out_grad,
        image_co_out_grad,
        text_co_in_grad,
        image_co_in_grad,
        text_gains_grad,
        image_gains_grad,
    ) = group_3.unpack()
    return (
        text_result,
        image_result,
        text_in_grad,
        image_in_grad,
        text_co_in_grad,
        image_co_in_grad,
        text_co_out_grad,
        image_co_out_grad,
        text_up_grad,
        text_down_grad,
        image_up_grad,
        image_down_grad,
        text_qkv_grad,
        text_proj_grad,
        image_qkv_grad,
        image_proj_grad,
        text_gains_grad,
        image_gains_grad,
    )


def solution(mesh):
    slots = P("dp", "seq", None)
    rows = P("dp", None)
    return jax.shard_map(
        per_device,
        mesh=mesh,
        in_specs=(slots, slots, rows, rows) + (P(),) * 14 + (slots, slots),
        out_specs=(slots,) * 4 + (rows,) * 12 + (P(), P()),
        check_vma=False,
    )
```

```python
import functools
import types

import jax
import jax.numpy as jnp
from jax import lax
from jax.experimental import pallas as pl
from jax.experimental.pallas import tpu as pltpu
from jax.sharding import PartitionSpec as P

HT = 12
HI = 8
HC = 8

NORM_EPS = 1e-05

F32 = jnp.float32
BF16 = jnp.bfloat16
LOG2E = 1.4426950408889634
MASKED = -1.0e9 * LOG2E
SQRT_2_PI = 0.7978845608028654
GELU_CUBE = 0.044715
LANES = 128
TILE = 256
WIDE = 1536
GAIN_ROWS = 32
MIB = 1024 * 1024


def dot_nt(a, b):
    return lax.dot_general(a, b, (((1,), (1,)), ((), ())), preferred_element_type=F32)


def dot_nn(a, b):
    return lax.dot_general(a, b, (((1,), (0,)), ((), ())), preferred_element_type=F32)


def dot_tn(a, b):
    return lax.dot_general(a, b, (((0,), (0,)), ((), ())), preferred_element_type=F32)


class Copies:
    def __init__(self, sems):
        self.sems, self.used, self.leaving = sems, 0, []

    def fetch(self, src, dst):
        copy = pltpu.make_async_copy(src, dst, self.sems.at[self.used])
        self.used += 1
        copy.start()
        return copy

    def flush(self, src, dst):
        self.leaving.append(self.fetch(src, dst))

    def finish(self):
        for copy in self.leaving:
            copy.wait()


def nbytes(shape, dtype):
    total = jnp.dtype(dtype).itemsize
    dims = list(shape)
    dims[-1] = -(-dims[-1] // 128) * 128
    if len(dims) > 1:
        dims[-2] = -(-dims[-2] // 16) * 16
    for d in dims:
        total *= d
    return total


def kernel_call(name, body, scal, ins, outs, scratch, copies=64, extra=8):
    names = list(ins) + list(outs) + list(scratch)

    def kernel(scal_ref, *refs):
        k = types.SimpleNamespace(**dict(zip(names, refs)))
        moves = Copies(refs[-1])
        body(scal_ref, k, moves)
        moves.finish()

    def place(where):
        return pl.BlockSpec(memory_space=pltpu.HBM if where == "h" else pltpu.VMEM)

    def shape_of(shape, dtype, where):
        return pltpu.HBM(tuple(shape), dtype) if where == "h" else jax.ShapeDtypeStruct(shape, dtype)

    args = [
        pltpu.with_memory_space_constraint(x, pltpu.HBM) if where == "h" else x for x, where in ins.values()
    ]
    total = sum(nbytes(s, d) for s, d in scratch.values()) + extra * MIB
    got = pl.pallas_call(
        kernel,
        in_specs=[pl.BlockSpec(memory_space=pltpu.SMEM)] + [place(w) for _, w in ins.values()],
        out_specs=[place(w) for _, _, w in outs.values()],
        out_shape=[shape_of(*o) for o in outs.values()],
        scratch_shapes=[pltpu.VMEM(tuple(s), d) for s, d in scratch.values()]
        + [pltpu.SemaphoreType.DMA((copies,))],
        compiler_params=pltpu.CompilerParams(vmem_limit_bytes=total),
        name=name,
    )(scal, *args)
    return types.SimpleNamespace(**dict(zip(outs, got)))


def loop(count, body, unroll=1):
    def step(i, carry):
        body(i)
        return carry

    lax.fori_loop(0, count, step, 0, unroll=unroll)


def at(i, size):
    return pl.ds(pl.multiple_of(i * size, size), size)


def row_chunks(rows, body):
    size = next(c for c in (128, 80, 64, 32, 16) if rows % c == 0)
    loop(rows // size, lambda i: body(at(i, size)))


def tile_of(width, limit):
    parts = -(-width // limit)
    while width % (parts * TILE):
        parts += 1
    return width // parts


def pick(i, values):
    out = values[0]
    for k in range(1, len(values)):
        out = jnp.where(i == k, values[k], out)
    return out


def lane_halves(width):
    if width == LANES:
        return [None]
    lane = lax.broadcasted_iota(jnp.int32, (1, LANES), 1)
    return [(lane // width) == i for i in range(LANES // width)]


def keep_lanes(x, sel):
    return x if sel is None else jnp.where(sel, x, jnp.zeros_like(x))


def cols(ref, rows, tile):
    return ref[rows, tile * LANES : (tile + 1) * LANES]


def store_bias(bias_ref, down_ref, along_ref):
    for r in range(bias_ref.shape[0]):
        row = down_ref[r : r + 1].astype(F32)
        col = jnp.transpose(jnp.broadcast_to(row, (8, row.shape[1])))[:, :1]
        bias_ref[r] = jnp.where(col == along_ref[r : r + 1].astype(F32), 0.0, MASKED).astype(F32)


def attend(r, q_ref, kv_ref, bias, o_ref, p_ref, lq, lk, width):
    scale = width**-0.5 * LOG2E
    sels = lane_halves(width)
    n = o_ref.shape[1] // LANES
    qs, ks = at(r, lq), at(r, lk)
    for t in range(n):
        q, k, v = cols(q_ref, qs, t), cols(kv_ref, ks, n + t), cols(kv_ref, ks, 2 * n + t)
        out = None
        for i, sel in enumerate(sels):
            s = dot_nt(k, keep_lanes(q, sel)) * scale + bias
            e = jnp.exp2(s - jnp.max(s, axis=0, keepdims=True))
            p = (e * (1.0 / jnp.sum(e, axis=0, keepdims=True))).astype(BF16)
            p_ref[r, t * len(sels) + i] = p
            o = dot_tn(p, v)
            out = o if out is None else jnp.where(sel, o, out)
        o_ref[qs, t * LANES : (t + 1) * LANES] = out.astype(BF16)


def attend_wide(r, q_ref, kv_ref, bias, o_ref, p_ref, lq, lk):
    scale = LANES**-0.5 * LOG2E
    n = o_ref.shape[1] // LANES
    qs, ks = at(r, lq), at(r, lk)
    for t in range(n):
        q, k, v = cols(q_ref, qs, t), cols(kv_ref, ks, n + t), cols(kv_ref, ks, 2 * n + t)
        s = dot_nt(q, k) * scale + bias
        e = jnp.exp2(s - jnp.max(s, axis=1, keepdims=True))
        p = (e * (1.0 / jnp.sum(e, axis=1, keepdims=True))).astype(BF16)
        p_ref[r, t] = p
        o_ref[qs, t * LANES : (t + 1) * LANES] = dot_nn(p, v).astype(BF16)


def attend_wide_back(r, q_ref, kv_ref, da_ref, p_ref, dq_ref, dkv_ref, lq, lk):
    scale = LANES**-0.5
    n = da_ref.shape[1] // LANES
    qs, ks = at(r, lq), at(r, lk)
    for t in range(n):
        q, k, v = cols(q_ref, qs, t), cols(kv_ref, ks, n + t), cols(kv_ref, ks, 2 * n + t)
        da = cols(da_ref, qs, t)
        p = p_ref[r, t]
        pf = p.astype(F32)
        w = pf * dot_nt(da, v)
        ds = (w - pf * jnp.sum(w, axis=1, keepdims=True)).astype(BF16)
        dq_ref[qs, t * LANES : (t + 1) * LANES] = (dot_nn(ds, k) * scale).astype(BF16)
        dkv_ref[ks, (n + t) * LANES : (n + t + 1) * LANES] = (dot_tn(ds, q) * scale).astype(BF16)
        dkv_ref[ks, (2 * n + t) * LANES : (2 * n + t + 1) * LANES] = dot_tn(p, da).astype(BF16)


def attend_back(r, q_ref, kv_ref, da_ref, p_ref, dq_ref, dkv_ref, lq, lk, width):
    scale = width**-0.5
    sels = lane_halves(width)
    n = da_ref.shape[1] // LANES
    qs, ks = at(r, lq), at(r, lk)
    for t in range(n):
        q, k, v = cols(q_ref, qs, t), cols(kv_ref, ks, n + t), cols(kv_ref, ks, 2 * n + t)
        da = cols(da_ref, qs, t)
        dq = dk = dv = None
        for i, sel in enumerate(sels):
            p = p_ref[r, t * len(sels) + i]
            da_h = keep_lanes(da, sel)
            pf = p.astype(F32)
            w = pf * dot_nt(v, da_h)
            ds = (w - pf * jnp.sum(w, axis=0, keepdims=True)).astype(BF16)
            dv_h = dot_nn(p, da_h)
            dk_h = dot_nn(ds, keep_lanes(q, sel))
            dq_h = dot_tn(ds, keep_lanes(k, sel))
            dq = dq_h if dq is None else dq + dq_h
            dk = dk_h if dk is None else dk + dk_h
            dv = dv_h if dv is None else dv + dv_h
        dq_ref[qs, t * LANES : (t + 1) * LANES] = (dq * scale).astype(BF16)
        dkv_ref[ks, (n + t) * LANES : (n + t + 1) * LANES] = (dk * scale).astype(BF16)
        dkv_ref[ks, (2 * n + t) * LANES : (2 * n + t + 1) * LANES] = dv.astype(BF16)


def normalize(z):
    center = z - jnp.mean(z, axis=-1, keepdims=True)
    inv = lax.rsqrt(jnp.mean(center * center, axis=-1, keepdims=True) + NORM_EPS)
    return center * inv, inv


def fold_rows(x):
    return jnp.sum(x.reshape(x.shape[0] // 8, 8, x.shape[1]), axis=0)


def matmul_tiles(x_ref, w_ref, o_ref):
    n = o_ref.shape[1]
    tile = tile_of(n, WIDE)

    def step(i):
        o_ref[:, at(i, tile)] = dot_nn(x_ref[...], w_ref[:, at(i, tile)]).astype(o_ref.dtype)

    loop(n // tile, step)


def norm_rows(acc_ref, res, gain, n_ref, inv_ref, low_ref=None):
    def chunk(rows):
        n, inv = normalize(acc_ref[rows] + res(rows))
        n_ref[rows] = n
        inv_ref[rows] = jnp.broadcast_to(inv, (inv.shape[0], LANES))
        if low_ref is not None:
            low_ref[rows] = (n * gain).astype(BF16)

    row_chunks(acc_ref.shape[0], chunk)


def norm_back_rows(dy_of, n_ref, inv_ref, gain, d_ref, low_ref, dg_ref):
    dg_ref[...] = jnp.zeros_like(dg_ref)

    def chunk(rows):
        dy = dy_of(rows)
        n = n_ref[rows]
        dn = dy * gain
        m1 = jnp.mean(dn, axis=-1, keepdims=True)
        m2 = jnp.mean(dn * n, axis=-1, keepdims=True)
        d = inv_ref[rows][:, :1] * (dn - m1 - n * m2)
        d_ref[rows] = d
        low_ref[rows] = d.astype(BF16)
        dg_ref[...] += fold_rows(dy * n)

    row_chunks(n_ref.shape[0], chunk)


def gelu_pair(v):
    v2 = v * v
    s = 0.5 + 0.5 * jnp.tanh(v * (SQRT_2_PI + (SQRT_2_PI * GELU_CUBE) * v2))
    a = v * s
    return a, s + a * (1.0 - s) * (2.0 * SQRT_2_PI + (6.0 * SQRT_2_PI * GELU_CUBE) * v2)


def ffn_tiles(x_ref, up_ref, down_ref, a_ref, slope_ref, acc_ref):
    width = tile_of(a_ref.shape[1], WIDE)

    def step(i):
        tile = at(i, width)
        a, slope = gelu_pair(dot_nn(x_ref[...], up_ref[:, tile]))
        a = a.astype(BF16)
        a_ref[:, tile] = a
        slope_ref[:, tile] = slope.astype(BF16)
        acc_ref[...] += dot_nn(a, down_ref[tile])

    acc_ref[...] = jnp.zeros_like(acc_ref)
    loop(a_ref.shape[1] // width, step)


def ffn_back_tiles(low_ref, down_ref, slope_ref, up_ref, dh_ref, acc_ref):
    width = tile_of(dh_ref.shape[1], WIDE)

    def step(i):
        tile = at(i, width)
        dh = (dot_nt(low_ref[...], down_ref[tile]) * slope_ref[:, tile].astype(F32)).astype(BF16)
        dh_ref[:, tile] = dh
        acc_ref[...] += dot_nt(dh, up_ref[:, tile])

    loop(dh_ref.shape[1] // width, step)


def send_packed(cp, keep, send, far_keep, far_send, first, last):
    for near, far in ((send, far_send), (keep, far_keep)):
        cp.flush(near.at[:, first:last], far.at[:, first:last])


def wgrad_group(scal, cp, xs, ys, plan, ndp, keep, send, far_keep, far_send):
    by_member = all(off % 16 == 0 and (tiles * rows) % 16 == 0 for tiles, _, _, off, rows in plan)
    for x, y, p in zip(xs, ys, plan):
        wgrad_member(scal, x, y, keep, send, p, ndp)
        if by_member:
            send_packed(cp, keep, send, far_keep, far_send, p[3], p[3] + p[0] * p[4])
    if not by_member:
        send_packed(cp, keep, send, far_keep, far_send, 0, keep.shape[1])


def wgrad_member(scal_ref, x_ref, y_ref, keep_ref, send_ref, plan, ndp):
    tiles, total, split, off, rows = plan
    odd = scal_ref[0] == 1
    xt = jnp.transpose(x_ref[...])
    first = jnp.minimum(scal_ref[1] * tiles, total - tiles) if split else 0
    for t in range(tiles):
        g = dot_nn(xt, y_ref[:, at(first + t, TILE)]).astype(BF16)
        base = off + t * rows
        for j in range(ndp // 2):
            even_rows = g[2 * j * rows : (2 * j + 1) * rows]
            odd_rows = g[(2 * j + 1) * rows : (2 * j + 2) * rows]
            keep_ref[j, base : base + rows] = jnp.where(odd, odd_rows, even_rows)
            send_ref[j, base : base + rows] = jnp.where(odd, even_rows, odd_rows)


def pack_gains(gain_refs, rows_ref, keep_ref, send_ref, base):
    row = 0
    for ref in gain_refs:
        total = jnp.sum(ref[...], axis=0, keepdims=True)
        for c in range(0, ref.shape[1], TILE):
            rows_ref[row : row + 1] = total[:, c : c + TILE]
            row += 1
    for row in range(row, GAIN_ROWS):
        rows_ref[row : row + 1] = jnp.zeros((1, TILE), F32)
    low = rows_ref[...].astype(BF16)
    for j in range(keep_ref.shape[0]):
        keep_ref[j, base : base + GAIN_ROWS] = low
        send_ref[j, base : base + GAIN_ROWS] = low


def co_stage_body(scal, k, cp, *, rows, parts, count_t, count_i):
    pieces = [cp.fetch(getattr(k, f"part{i}"), k.staged.at[i]) for i in range(parts)]
    wa = cp.fetch(k.co_t, k.wa)
    wb = cp.fetch(k.co_i, k.wb)
    wo = cp.fetch(k.out_t, k.wo)
    wd = cp.fetch(k.down_t, k.wd)
    lt, li = parts * count_t, parts * count_i
    store_bias(k.bias, k.iseg, k.tseg)
    for piece in pieces:
        piece.wait()
    base = join_tiles(scal[1], k.staged, k.tx, count_t, rows, 0)
    wa.wait()
    matmul_tiles(k.tx, k.wa, k.tqkv)
    up_t = cp.fetch(k.up_t, k.wa)
    cp.flush(k.tx, k.o_tx)
    cp.flush(k.tqkv, k.o_tqkv)
    join_tiles(scal[1], k.staged, k.ix, count_i, rows, base)
    wb.wait()
    matmul_tiles(k.ix, k.wb, k.iqkv)
    wi = k.ix.shape[1]
    up_i = cp.fetch(k.up_i, k.wb.at[:, 0:wi])
    down_i = cp.fetch(k.down_i, k.wb.at[:, wi : 2 * wi])
    out_i = cp.fetch(k.out_i, k.wb.at[:, 2 * wi : 3 * wi])
    cp.flush(k.ix, k.o_ix)
    cp.flush(k.iqkv, k.o_iqkv)
    assert k.tatt.shape[1] == HC * LANES

    def heads(r):
        attend(r, k.tqkv, k.iqkv, k.bias[r], k.tatt, k.pt, lt, li, LANES)
        attend_wide(r, k.iqkv, k.tqkv, k.bias[r], k.iatt, k.pi, li, lt)

    loop(rows, heads)
    cp.flush(k.tatt, k.o_tatt)
    cp.flush(k.iatt, k.o_iatt)
    cp.flush(k.pt, k.o_pt)
    cp.flush(k.pi, k.o_pi)
    out_i.wait()
    matmul_tiles(k.iatt, k.wb.at[:, 2 * wi : 3 * wi], k.acc_i)
    ig = k.ig[...]
    norm_rows(k.acc_i, lambda r: k.ix[r].astype(F32), ig[0:1], k.in1, k.ir1, k.i1)
    up_i.wait()
    down_i.wait()
    ffn_tiles(k.i1, k.wb.at[:, 0:wi], k.wb.at[:, wi : 2 * wi], k.ia, k.isl, k.acc_i)
    norm_rows(k.acc_i, lambda r: k.in1[r] * ig[0:1], ig[1:2], k.in2, k.ir2, k.i2)
    for name in ("in1", "ir1", "i1", "ia", "isl", "in2", "ir2", "i2"):
        cp.flush(getattr(k, name), getattr(k, "o_" + name))
    wo.wait()
    matmul_tiles(k.tatt, k.wo, k.acc_t)
    tg = k.tg[...]
    norm_rows(k.acc_t, lambda r: k.tx[r].astype(F32), tg[0:1], k.tn1, k.tr1, k.t1)
    up_t.wait()
    wd.wait()
    for name in ("tn1", "tr1", "t1"):
        cp.flush(getattr(k, name), getattr(k, "o_" + name))
    ffn_tiles(k.t1, k.wa, k.wd, k.ta, k.tsl, k.acc_t)
    cp.flush(k.ta, k.o_ta)
    cp.flush(k.tsl, k.o_tsl)
    norm_rows(k.acc_t, lambda r: k.tn1[r] * tg[0:1], tg[1:2], k.tn2, k.tr2, k.t2)
    for name in ("t2", "tn2", "tr2"):
        cp.flush(getattr(k, name), getattr(k, "o_" + name))


def self_stage_body(scal, k, cp, *, rows, count_t, count_i):
    t2 = cp.fetch(k.h_t2, k.t2)
    wa = cp.fetch(k.qkv_t, k.wa)
    i2 = cp.fetch(k.h_i2, k.i2)
    wb = cp.fetch(k.qkv_i, k.wb)
    pa = cp.fetch(k.proj_t, k.pa)
    pb = cp.fetch(k.proj_i, k.pb)
    tn2 = cp.fetch(k.h_tn2, k.tn2)
    in2 = cp.fetch(k.h_in2, k.in2)
    store_bias(k.tbias, k.tseg, k.tseg)
    store_bias(k.ibias, k.iseg, k.iseg)
    lt = k.t2.shape[0] // rows
    li = k.i2.shape[0] // rows
    t2.wait()
    wa.wait()
    matmul_tiles(k.t2, k.wa, k.sqkv)
    cp.flush(k.sqkv, k.o_sqkv)
    i2.wait()
    wb.wait()
    matmul_tiles(k.i2, k.wb, k.uqkv)
    cp.flush(k.uqkv, k.o_uqkv)
    wt = k.tmix.shape[1] // HT
    wi = k.imix.shape[1] // HI

    def heads(r):
        attend(r, k.sqkv, k.sqkv, k.tbias[r], k.tmix, k.spt, lt, lt, wt)
        attend(r, k.uqkv, k.uqkv, k.ibias[r], k.imix, k.spi, li, li, wi)

    loop(rows, heads)
    for name in ("tmix", "imix", "spt", "spi"):
        cp.flush(getattr(k, name), getattr(k, "o_" + name))
    tn2.wait()
    in2.wait()
    z = scal[1]
    for mix, w, ready, acc, n2, g, n3, r3, res, count in (
        (k.tmix, k.pa, pa, k.acc_t, k.tn2, k.tg, k.tn3, k.tr3, k.o_tres, count_t),
        (k.imix, k.pb, pb, k.acc_i, k.in2, k.ig, k.in3, k.ir3, k.o_ires, count_i),
    ):
        ready.wait()
        matmul_tiles(mix, w, acc)
        gain = g[...]
        norm_rows(acc, lambda r, n2=n2, gain=gain: n2[r] * gain[1:2], None, n3, r3)
        length = mix.shape[0] // rows
        for r in range(rows):
            own = n3[pl.ds(pl.multiple_of(r * length + z * count, 8), count)]
            res[r] = (own * gain[2:3]).astype(BF16)
    for name in ("tn3", "in3", "tr3", "ir3"):
        cp.flush(getattr(k, name), getattr(k, "o_" + name))


def self_back_body(scal, k, cp, *, rows, count_t, count_i, plan, ndp):
    ups = [cp.fetch(getattr(k, f"h_up{i}"), k.up.at[i]) for i in range(k.up.shape[0])]
    names = ("tn3", "tr3", "proj_t", "in3", "ir3", "proj_i", "sqkv", "spt", "uqkv", "spi")
    names += ("tmix", "imix", "t2", "i2")
    moves = {n: cp.fetch(getattr(k, "h_" + n), getattr(k, n)) for n in names}

    def ready(*which):
        for n in which:
            moves[n].wait()

    for copy in ups:
        copy.wait()
    base = join_tiles(scal[1], k.up, k.tup, count_t, rows, 0)
    join_tiles(scal[1], k.up, k.iup, count_i, rows, base)
    ready("tn3", "tr3", "proj_t")
    norm_back_rows(
        lambda r: k.tup[r].astype(F32), k.tn3, k.tr3, k.tg[2:3], k.o_d3, k.d3b, k.tdg
    )
    k.dmt[...] = dot_nt(k.d3b[...], k.proj_t[...]).astype(BF16)
    ready("in3", "ir3", "proj_i")
    norm_back_rows(
        lambda r: k.iup[r].astype(F32), k.in3, k.ir3, k.ig[2:3], k.o_e3, k.e3b, k.idg
    )
    k.dmi[...] = dot_nt(k.e3b[...], k.proj_i[...]).astype(BF16)
    ready("sqkv", "spt", "uqkv", "spi")
    lt, li = k.tup.shape[0] // rows, k.iup.shape[0] // rows
    wt = k.dmt.shape[1] // HT
    wi = k.dmi.shape[1] // HI

    def heads(r):
        attend_back(r, k.sqkv, k.sqkv, k.dmt, k.spt, k.o_dsqkv, k.o_dsqkv, lt, lt, wt)
        attend_back(r, k.uqkv, k.uqkv, k.dmi, k.spi, k.o_duqkv, k.o_duqkv, li, li, wi)

    loop(rows, heads)
    ready("tmix", "imix", "t2", "i2")
    xs, ys = (k.tmix, k.imix, k.t2, k.i2), (k.d3b, k.e3b, k.o_dsqkv, k.o_duqkv)
    wgrad_group(scal, cp, xs, ys, plan, ndp, k.keep, k.send, k.o_keep, k.o_send)
    for name in ("tdg", "idg"):
        cp.flush(getattr(k, name), getattr(k, "o_" + name))


def chunked(cp, src, dst, axis, count=3):
    size = src.shape[axis] // count
    out = []
    for i in range(count):
        part = slice(i * size, (i + 1) * size)
        part = (slice(None), part) if axis == 1 else (part, slice(None))
        out.append((cp.fetch(src.at[part], dst.at[part]), part))
    return out


def qkv_back_body(scal, k, cp):
    wa = cp.fetch(k.qkv_t, k.wa)
    extra_t = [cp.fetch(k.h_tn2, k.tn2), cp.fetch(k.h_tr2, k.tr2)]
    wb = cp.fetch(k.qkv_i, k.wb)
    extra_i = [cp.fetch(k.h_in2, k.in2), cp.fetch(k.h_ir2, k.ir2)]
    for dx, w, ready, extra, acc, d3, n, inv, g, outs in (
        (k.dsqkv, k.wa, wa, extra_t, k.acc_t, k.d3, k.tn2, k.tr2, k.tg, ("d2", "d2b", "tdg")),
        (k.duqkv, k.wb, wb, extra_i, k.acc_i, k.e3, k.in2, k.ir2, k.ig, ("e2", "e2b", "idg")),
    ):
        ready.wait()
        acc[...] = dot_nt(dx[...], w[...])
        for copy in extra:
            copy.wait()
        d2, low, dg = (getattr(k, name) for name in outs)
        norm_back_rows(lambda r, acc=acc, d3=d3: d3[r] + acc[r], n, inv, g[1:2], d2, low, dg)
        for name in outs:
            cp.flush(getattr(k, name), getattr(k, "o_" + name))


def ffn_back_body(scal, k, cp, *, plan, ndp):
    def start(*names):
        return [cp.fetch(getattr(k, "h_" + n), getattr(k, n)) for n in names]

    moves = start("e2b", "down_i", "isl", "up_i")
    y1 = cp.fetch(k.h_e2, k.y1)
    later = start("d2b", "down_t", "tsl", "up_t")
    x1 = cp.fetch(k.h_d2, k.x1)
    last = start("ta", "ia", "t1", "i1")
    for copy in (*moves, y1):
        copy.wait()
    ffn_back_tiles(k.e2b, k.down_i, k.isl, k.up_i, k.dhi, k.y1)
    cp.flush(k.y1, k.o_y1)
    for copy in (*later, x1):
        copy.wait()
    ffn_back_tiles(k.d2b, k.down_t, k.tsl, k.up_t, k.dht, k.x1)
    cp.flush(k.x1, k.o_x1)
    for copy in last:
        copy.wait()
    xs, ys = (k.ta, k.ia, k.t1, k.i1), (k.d2b, k.e2b, k.dht, k.dhi)
    wgrad_group(scal, cp, xs, ys, plan, ndp, k.keep, k.send, k.o_keep, k.o_send)


def first_norm_back_body(scal, k, cp, *, rows, count_t, count_i):
    moves_t = [cp.fetch(getattr(k, "h_" + n), getattr(k, n)) for n in ("x1", "tn1", "tr1", "out_t")]
    moves_i = [cp.fetch(getattr(k, "h_" + n), getattr(k, n)) for n in ("y1", "in1", "ir1", "out_i")]
    z = scal[1]
    for moves, x1, n, inv, g, d1, low, dg, w, da, own, count in (
        (moves_t, k.x1, k.tn1, k.tr1, k.tg, k.d1, k.d1b, k.tdg, k.out_t, k.dat, k.own_t, count_t),
        (moves_i, k.y1, k.in1, k.ir1, k.ig, k.e1, k.e1b, k.idg, k.out_i, k.dai, k.own_i, count_i),
    ):
        for copy in moves:
            copy.wait()
        norm_back_rows(lambda r, x1=x1: x1[r], n, inv, g[0:1], d1, low, dg)
        da[...] = dot_nt(low[...], w[...]).astype(BF16)
        length = x1.shape[0] // rows
        for r in range(rows):
            own[r] = d1[pl.ds(pl.multiple_of(r * length + z * count, 8), count)]
    for name in ("dat", "dai", "d1b", "e1b", "own_t", "own_i", "tdg", "idg"):
        cp.flush(getattr(k, name), getattr(k, "o_" + name))


def co_back_body(scal, k, cp, *, rows, parts, count_t, count_i, plan, last_plan, ndp, gains_at):
    names = ("tqkv", "pt", "dat", "iqkv", "pi", "dai", "iatt", "e1b", "tatt", "d1b", "ix", "tx")
    names += ("tdg1", "tdg2", "tdg3", "idg1", "idg2", "idg3")
    moves = [cp.fetch(getattr(k, "h_" + n), getattr(k, n)) for n in names]
    for copy in moves[:6]:
        copy.wait()
    lt, li = parts * count_t, parts * count_i
    def heads(r):
        attend_back(r, k.tqkv, k.iqkv, k.dat, k.pt, k.dt, k.di, lt, li, LANES)
        attend_wide_back(r, k.iqkv, k.tqkv, k.dai, k.pi, k.di, k.dt, li, lt)

    loop(rows, heads)
    for copy in moves[6:]:
        copy.wait()
    xs, ys = (k.iatt, k.ix, k.tatt), (k.e1b, k.di, k.d1b)
    wgrad_group(scal, cp, xs, ys, plan, ndp, k.keep, k.send, k.o_keep, k.o_send)
    gains = (k.tdg1, k.tdg2, k.tdg3, k.idg1, k.idg2, k.idg3)
    pack_gains(gains, k.gain_rows, k.keep_last, k.send_last, gains_at)
    wgrad_member(scal, k.tx, k.dt, k.keep_last, k.send_last, last_plan, ndp)
    cp.flush(k.send_last, k.o_send_last)
    cp.flush(k.keep_last, k.o_keep_last)
    z = scal[1]
    for full, own, count in ((k.dt, k.o_dt, count_t), (k.di, k.o_di, count_i)):
        for r in range(rows):
            values = [
                full[(r * parts + i) * count : (r * parts + i + 1) * count] for i in range(parts)
            ]
            own[r] = pick(z, values)


def in_back_body(scal, k, cp):
    own_t = cp.fetch(k.h_d1, k.d1)
    own_i = cp.fetch(k.h_e1, k.e1)
    wa = chunked(cp, k.co_t, k.wa, 1)
    wb = chunked(cp, k.co_i, k.wb, 1)
    for dx, w, chunks, d1, out, own in (
        (k.dt, k.wa, wa, k.d1, k.o_dt, own_t),
        (k.di, k.wb, wb, k.e1, k.o_di, own_i),
    ):
        own.wait()
        r, count, m = dx.shape
        flat = dx[...].reshape(r * count, m)
        total = d1[...].reshape(r * count, d1.shape[2])
        for copy, part in chunks:
            copy.wait()
            total = total + dot_nt(flat[part], w[part])
        out[...] = total.reshape(out.shape)


def pack_body(scal, k, cp, *, count):
    for i in range(count):
        packed = getattr(k, f"s{i}")
        base = 0
        for ref in (getattr(k, f"t{i}"), getattr(k, f"i{i}")):
            for c in range(0, ref.shape[2], TILE):
                for r in range(ref.shape[0]):
                    part = ref[r, :, c : c + TILE]
                    packed[base : base + part.shape[0]] = part
                    base += part.shape[0]
        cp.flush(packed, getattr(k, f"o{i}"))


def join_tiles(z, staged, full, count, rows, base):
    parts = staged.shape[0]
    for c in range(0, full.shape[1], TILE):
        for r in range(rows):
            values = [staged[i, base : base + count] for i in range(parts)]
            for i in range(parts):
                to = (r * parts + i) * count
                full[to : to + count, c : c + TILE] = pick(z ^ i, values)
            base += count
    return base


def unpack_body(scal, k, cp, *, plan, nseq, gains_at, gain_shapes):
    z = scal[1]
    pieces = [cp.fetch(getattr(k, f"h{i}"), getattr(k, f"p{i}")) for i in range(nseq)]
    low = None
    if hasattr(k, "own"):
        cp.fetch(k.h_own, k.own).wait()
        low = k.own
    if gain_shapes:
        sums = low[gains_at : gains_at + GAIN_ROWS].astype(F32)
        row = 0
        for i, (count, width) in enumerate(gain_shapes):
            out = getattr(k, f"o_gain{i}")
            for g in range(count):
                for c in range(0, width, TILE):
                    out[g : g + 1, c : c + TILE] = sums[row : row + 1]
                    row += 1
    for i, (tiles, total, split, off, rows) in enumerate(plan):
        if not split:
            buf = getattr(k, f"b{i}")
            for t in range(tiles):
                buf[:, t * TILE : (t + 1) * TILE] = low[off + t * rows : off + (t + 1) * rows].astype(F32)
            cp.flush(buf, getattr(k, f"o{i}"))
    for piece in pieces:
        piece.wait()
    for i, (tiles, total, split, off, rows) in enumerate(plan):
        if split:
            buf = getattr(k, f"b{i}")
            for s in range(nseq):
                ref = getattr(k, f"p{s}")
                first = jnp.minimum((z ^ s) * tiles, total - tiles)
                for t in range(tiles):
                    buf[:, at(first + t, TILE)] = ref[off + t * rows : off + (t + 1) * rows].astype(F32)
            cp.flush(buf, getattr(k, f"o{i}"))


class Comm:
    def __init__(self):
        self.nseq = lax.axis_size("seq")
        self.ndp = lax.axis_size("dp")
        self.z = lax.axis_index("seq")
        self.d = lax.axis_index("dp")
        self.scal = jnp.stack([self.d % 2, self.z]).astype(jnp.int32)

    def pieces(self, x):
        n = self.nseq
        return [x] + [lax.ppermute(x, "seq", [(i, i ^ k) for i in range(n)]) for k in range(1, n)]

    def pack(self, *pairs):
        ins, outs, scratch = {}, {}, {}
        for i, (text, image) in enumerate(pairs):
            total = sum(x.shape[0] * x.shape[1] * (x.shape[2] // TILE) for x in (text, image))
            ins.update({f"t{i}": (text, "v"), f"i{i}": (image, "v")})
            outs[f"o{i}"] = ((total, TILE), BF16, "h")
            scratch[f"s{i}"] = ((total, TILE), BF16)
        got = kernel_call(
            "pack",
            functools.partial(pack_body, count=len(pairs)),
            self.scal,
            ins,
            outs,
            scratch,
            copies=len(pairs),
            extra=2,
        )
        return [getattr(got, name) for name in outs]

    def plan_of(self, members):
        plan = {}
        off = 0
        for want in (True, False):
            for i, (din, dout, split) in enumerate(members):
                if split != want:
                    continue
                total = dout // TILE
                tiles = -(-total // self.nseq) if split else total
                rows = din // self.ndp
                plan[i] = (tiles, total, split, off, rows)
                off += tiles * rows
            if want:
                split_rows = off
        return Plan(self, [plan[i] for i in range(len(members))], split_rows, off)


class Plan:
    def __init__(self, comm, members, split_rows, rows, gain_shapes=()):
        self.comm, self.members, self.split_rows, self.rows = comm, members, split_rows, rows
        self.gain_shapes = gain_shapes
        self.gains_at = rows

    def with_gains(self, shapes):
        self.gain_shapes = shapes
        self.rows += GAIN_ROWS
        return self

    def half(self):
        return (self.comm.ndp // 2, self.rows, TILE)

    def swap(self, keep, send):
        self.keep = keep
        self.got = lax.ppermute(send, "dp", [(i, i ^ 1) for i in range(self.comm.ndp)])

    def cross(self):
        pair = (self.keep.astype(F32) + self.got.astype(F32)).astype(BF16)
        groups = [list(range(b, self.comm.ndp, 2)) for b in range(2)]
        self.parts = lax.all_to_all(
            pair, "dp", split_axis=0, concat_axis=0, tiled=True, axis_index_groups=groups
        )

    def along(self):
        def total(part):
            return jnp.sum(part.astype(F32), axis=0).astype(BF16)

        self.everyone = []
        if self.split_rows:
            self.everyone = self.comm.pieces(total(self.parts[:, : self.split_rows]))
        self.own = total(self.parts[:, self.split_rows :]) if self.rows > self.split_rows else None

    def unpack(self):
        plan = [(p[0], p[1], p[2], p[3] if p[2] else p[3] - self.split_rows, p[4]) for p in self.members]
        ins = {f"h{i}": (x, "h") for i, x in enumerate(self.everyone)}
        if self.rows > self.split_rows:
            ins["h_own"] = (self.own, "h")
        outs = {f"o{i}": ((p[4], p[1] * TILE), F32, "h") for i, p in enumerate(plan)}
        outs.update({f"o_gain{i}": (s, F32, "v") for i, s in enumerate(self.gain_shapes)})
        scratch = {f"p{i}": (x.shape, BF16) for i, x in enumerate(self.everyone)}
        if self.rows > self.split_rows:
            scratch["own"] = (self.own.shape, BF16)
        scratch.update({f"b{i}": ((p[4], p[1] * TILE), F32) for i, p in enumerate(plan)})
        got = kernel_call(
            "unpack",
            functools.partial(
                unpack_body,
                plan=plan,
                nseq=len(self.everyone),
                gains_at=self.gains_at - self.split_rows,
                gain_shapes=self.gain_shapes,
            ),
            self.comm.scal,
            ins,
            outs,
            scratch,
            copies=16,
        )
        return [getattr(got, name) for name in outs]


def tie(*xs):
    return lax.optimization_barrier(xs)


def per_device(
    text_in,
    image_in,
    text_seg,
    image_seg,
    text_co_in,
    image_co_in,
    text_co_out,
    image_co_out,
    text_up,
    text_down,
    image_up,
    image_down,
    text_qkv,
    text_proj,
    image_qkv,
    image_proj,
    text_gains,
    image_gains,
    text_upstream,
    image_upstream,
):
    comm = Comm()
    scal = comm.scal
    n = comm.nseq
    rows, nt, dt = text_in.shape
    ni, di = image_in.shape[1:]
    lt, li = n * nt, n * ni
    tt, ti = rows * lt, rows * li
    dc = text_co_out.shape[0]
    ft, fi = text_up.shape[1], image_up.shape[1]
    segs = {"tseg": (text_seg, "v"), "iseg": (image_seg, "v")}
    gains = {"tg": (text_gains, "v"), "ig": (image_gains, "v")}

    inputs, upstream = comm.pack((text_in, image_in), (text_upstream, image_upstream))
    inputs = comm.pieces(inputs)
    upstream, *inputs = tie(upstream, *inputs)
    upstream = comm.pieces(upstream)

    def saved(**shapes):
        return (
            {"o_" + name: (shape, dtype, "h") for name, (shape, dtype) in shapes.items()},
            {name: (shape, dtype) for name, (shape, dtype) in shapes.items()},
        )

    outs, scratch = saved(
        tx=((tt, dt), BF16),
        ix=((ti, di), BF16),
        tqkv=((tt, 3 * dc), BF16),
        iqkv=((ti, 3 * dc), BF16),
        tatt=((tt, dc), BF16),
        iatt=((ti, dc), BF16),
        pt=((rows, HC, li, lt), BF16),
        pi=((rows, HC, li, lt), BF16),
        tn1=((tt, dt), F32),
        tr1=((tt, LANES), F32),
        t1=((tt, dt), BF16),
        in1=((ti, di), F32),
        ir1=((ti, LANES), F32),
        i1=((ti, di), BF16),
        ta=((tt, ft), BF16),
        tsl=((tt, ft), BF16),
        ia=((ti, fi), BF16),
        isl=((ti, fi), BF16),
        tr2=((tt, LANES), F32),
        ir2=((ti, LANES), F32),
        tn2=((tt, dt), F32),
        t2=((tt, dt), BF16),
        in2=((ti, di), F32),
        i2=((ti, di), BF16),
    )
    scratch.update(
        staged=((n,) + inputs[0].shape, BF16),
        bias=((rows, li, lt), F32),
        wa=((dt, 3 * dc), BF16),
        wb=((di, 3 * dc), BF16),
        wo=((dc, dt), BF16),
        wd=((ft, dt), BF16),
        acc_t=((tt, dt), F32),
        acc_i=((ti, di), F32),
    )
    ins = {f"part{i}": (x, "h") for i, x in enumerate(inputs)}
    ins.update(
        co_t=(text_co_in, "h"),
        co_i=(image_co_in, "h"),
        out_t=(text_co_out, "h"),
        out_i=(image_co_out, "h"),
        up_t=(text_up, "h"),
        down_t=(text_down, "h"),
        up_i=(image_up, "h"),
        down_i=(image_down, "h"),
        **segs,
        **gains,
    )
    f1 = kernel_call(
        "co_stage",
        functools.partial(co_stage_body, rows=rows, parts=n, count_t=nt, count_i=ni),
        scal,
        ins,
        outs,
        scratch,
    )

    outs, scratch = saved(
        sqkv=((tt, 3 * dt), BF16),
        uqkv=((ti, 3 * di), BF16),
        tmix=((tt, dt), BF16),
        imix=((ti, di), BF16),
        spt=((rows, HT, lt, lt), BF16),
        spi=((rows, HI, li, li), BF16),
        tn3=((tt, dt), F32),
        tr3=((tt, LANES), F32),
        in3=((ti, di), F32),
        ir3=((ti, LANES), F32),
    )
    outs.update(o_tres=((rows, nt, dt), BF16, "v"), o_ires=((rows, ni, di), BF16, "v"))
    scratch.update(
        wa=(text_qkv.shape, BF16),
        wb=(image_qkv.shape, BF16),
        pa=(text_proj.shape, BF16),
        pb=(image_proj.shape, BF16),
        acc_t=((tt, dt), F32),
        acc_i=((ti, di), F32),
        t2=((tt, dt), BF16),
        i2=((ti, di), BF16),
        tn2=((tt, dt), F32),
        in2=((ti, di), F32),
        tbias=((rows, lt, lt), F32),
        ibias=((rows, li, li), F32),
    )
    f2 = kernel_call(
        "self_stage",
        functools.partial(self_stage_body, rows=rows, count_t=nt, count_i=ni),
        scal,
        dict(
            h_t2=(f1.o_t2, "h"),
            h_i2=(f1.o_i2, "h"),
            h_tn2=(f1.o_tn2, "h"),
            h_in2=(f1.o_in2, "h"),
            qkv_t=(text_qkv, "h"),
            qkv_i=(image_qkv, "h"),
            proj_t=(text_proj, "h"),
            proj_i=(image_proj, "h"),
            **segs,
            **gains,
        ),
        outs,
        scratch,
    )

    group_1 = comm.plan_of([(dt, dt, False), (di, di, True), (dt, 3 * dt, True), (di, 3 * di, True)])
    group_2 = comm.plan_of([(ft, dt, False), (fi, di, True), (dt, ft, True), (di, fi, True)])
    group_3 = comm.plan_of([(dc, di, True), (di, 3 * dc, True), (dc, dt, True)])
    group_4 = comm.plan_of([(dt, 3 * dc, False)]).with_gains([text_gains.shape, image_gains.shape])

    def sources(**arrays):
        return (
            {"h_" + name: (x, "h") for name, x in arrays.items()},
            {name: (x.shape, x.dtype) for name, x in arrays.items()},
        )

    def packed(group, tag=""):
        shape = group.half()
        return (
            {"o_keep" + tag: (shape, BF16, "h"), "o_send" + tag: (shape, BF16, "h")},
            {"keep" + tag: (shape, BF16), "send" + tag: (shape, BF16)},
        )

    ins, scratch = sources(
        tn3=f2.o_tn3,
        tr3=f2.o_tr3,
        proj_t=text_proj,
        in3=f2.o_in3,
        ir3=f2.o_ir3,
        proj_i=image_proj,
        sqkv=f2.o_sqkv,
        spt=f2.o_spt,
        uqkv=f2.o_uqkv,
        spi=f2.o_spi,
        tmix=f2.o_tmix,
        imix=f2.o_imix,
        t2=f1.o_t2,
        i2=f1.o_i2,
    )
    ins.update({f"h_up{i}": (x, "h") for i, x in enumerate(upstream)})
    outs, more = packed(group_1)
    scratch.update(
        **more,
        up=((n,) + upstream[0].shape, BF16),
        tup=((tt, dt), BF16),
        iup=((ti, di), BF16),
        d3b=((tt, dt), BF16),
        e3b=((ti, di), BF16),
        dmt=((tt, dt), BF16),
        dmi=((ti, di), BF16),
        tdg=((8, dt), F32),
        idg=((8, di), F32),
    )
    outs.update(
        o_d3=((tt, dt), F32, "v"),
        o_e3=((ti, di), F32, "v"),
        o_dsqkv=((tt, 3 * dt), BF16, "v"),
        o_duqkv=((ti, 3 * di), BF16, "v"),
        o_tdg=((8, dt), F32, "h"),
        o_idg=((8, di), F32, "h"),
    )
    b1 = kernel_call(
        "self_back",
        functools.partial(
            self_back_body, rows=rows, count_t=nt, count_i=ni, plan=group_1.members, ndp=comm.ndp
        ),
        scal,
        {**ins, **gains},
        outs,
        scratch,
    )
    group_1.swap(b1.o_keep, b1.o_send)

    ins, scratch = sources(tn2=f1.o_tn2, tr2=f1.o_tr2, in2=f1.o_in2, ir2=f1.o_ir2)
    outs, more = saved(
        d2=((tt, dt), F32),
        e2=((ti, di), F32),
        d2b=((tt, dt), BF16),
        e2b=((ti, di), BF16),
        tdg=((8, dt), F32),
        idg=((8, di), F32),
    )
    scratch.update(
        **more,
        wa=(text_qkv.shape, BF16),
        wb=(image_qkv.shape, BF16),
        acc_t=((tt, dt), F32),
        acc_i=((ti, di), F32),
    )
    b2 = kernel_call(
        "qkv_back",
        qkv_back_body,
        scal,
        dict(
            **ins,
            qkv_t=(text_qkv, "h"),
            qkv_i=(image_qkv, "h"),
            dsqkv=(b1.o_dsqkv, "v"),
            duqkv=(b1.o_duqkv, "v"),
            d3=(b1.o_d3, "v"),
            e3=(b1.o_e3, "v"),
            **gains,
        ),
        outs,
        scratch,
    )
    group_1.got, d2, e2, d2b, e2b = tie(group_1.got, b2.o_d2, b2.o_e2, b2.o_d2b, b2.o_e2b)
    group_1.cross()

    ins, scratch = sources(
        down_i=image_down,
        isl=f1.o_isl,
        up_i=image_up,
        down_t=text_down,
        tsl=f1.o_tsl,
        up_t=text_up,
        ia=f1.o_ia,
        i1=f1.o_i1,
        ta=f1.o_ta,
        t1=f1.o_t1,
        d2b=d2b,
        e2b=e2b,
    )
    ins.update(h_d2=(d2, "h"), h_e2=(e2, "h"))
    outs, more = packed(group_2)
    scratch.update(x1=((tt, dt), F32), y1=((ti, di), F32))
    scratch.update(**more, dht=((tt, ft), BF16), dhi=((ti, fi), BF16))
    b3 = kernel_call(
        "ffn_back",
        functools.partial(ffn_back_body, plan=group_2.members, ndp=comm.ndp),
        scal,
        ins,
        dict(**outs, o_x1=((tt, dt), F32, "h"), o_y1=((ti, di), F32, "h")),
        scratch,
    )
    group_1.parts, x1, y1, keep, send = tie(
        group_1.parts, b3.o_x1, b3.o_y1, b3.o_keep, b3.o_send
    )
    group_2.swap(keep, send)
    group_1.along()

    ins, scratch = sources(
        x1=x1, y1=y1, tn1=f1.o_tn1, tr1=f1.o_tr1, out_t=text_co_out, in1=f1.o_in1, ir1=f1.o_ir1, out_i=image_co_out
    )
    outs, more = saved(
        d1b=((tt, dt), BF16),
        e1b=((ti, di), BF16),
        dat=((tt, dc), BF16),
        dai=((ti, dc), BF16),
        own_t=((rows, nt, dt), F32),
        own_i=((rows, ni, di), F32),
        tdg=((8, dt), F32),
        idg=((8, di), F32),
    )
    scratch.update(**more, d1=((tt, dt), F32), e1=((ti, di), F32))
    b4 = kernel_call(
        "first_norm_back",
        functools.partial(first_norm_back_body, rows=rows, count_t=nt, count_i=ni),
        scal,
        dict(**ins, **gains),
        outs,
        scratch,
    )
    group_2.got, dat, dai = tie(group_2.got, b4.o_dat, b4.o_dai)
    group_2.cross()

    ins, scratch = sources(
        tqkv=f1.o_tqkv,
        pt=f1.o_pt,
        iqkv=f1.o_iqkv,
        pi=f1.o_pi,
        tatt=f1.o_tatt,
        iatt=f1.o_iatt,
        tx=f1.o_tx,
        ix=f1.o_ix,
        dat=dat,
        dai=dai,
        d1b=b4.o_d1b,
        e1b=b4.o_e1b,
        tdg1=b4.o_tdg,
        tdg2=b2.o_tdg,
        tdg3=b1.o_tdg,
        idg1=b4.o_idg,
        idg2=b2.o_idg,
        idg3=b1.o_idg,
    )
    outs, more = packed(group_3)
    outs_last, more_last = packed(group_4, "_last")
    outs.update(outs_last)
    scratch.update(
        **more, **more_last, dt=((tt, 3 * dc), BF16), di=((ti, 3 * dc), BF16), gain_rows=((GAIN_ROWS, TILE), F32)
    )
    b5 = kernel_call(
        "co_back",
        functools.partial(
            co_back_body,
            rows=rows,
            parts=n,
            count_t=nt,
            count_i=ni,
            plan=group_3.members,
            last_plan=group_4.members[0],
            ndp=comm.ndp,
            gains_at=group_4.gains_at,
        ),
        scal,
        ins,
        dict(
            **outs,
            o_dt=((rows, nt, 3 * dc), BF16, "v"),
            o_di=((rows, ni, 3 * dc), BF16, "v"),
        ),
        scratch,
    )
    group_1.everyone[1], group_1.everyone[2], dt_own, di_own, keep, send, keep_last, send_last = tie(
        *group_1.everyone[1:3],
        b5.o_dt,
        b5.o_di,
        b5.o_keep,
        b5.o_send,
        b5.o_keep_last,
        b5.o_send_last,
    )
    group_3.swap(keep, send)
    group_4.swap(keep_last, send_last)
    b6 = kernel_call(
        "in_back",
        in_back_body,
        scal,
        dict(
            co_t=(text_co_in, "h"),
            co_i=(image_co_in, "h"),
            dt=(dt_own, "v"),
            di=(di_own, "v"),
            h_d1=(b4.o_own_t, "h"),
            h_e1=(b4.o_own_i, "h"),
        ),
        dict(o_dt=((rows, nt, dt), F32, "v"), o_di=((rows, ni, di), F32, "v")),
        dict(
            wa=(text_co_in.shape, BF16),
            wb=(image_co_in.shape, BF16),
            d1=((rows, nt, dt), F32),
            e1=((rows, ni, di), F32),
        ),
    )
    (
        group_1.everyone[3],
        group_3.got,
        group_4.got,
        group_2.parts,
        text_in_grad,
        image_in_grad,
    ) = tie(group_1.everyone[3], group_3.got, group_4.got, group_2.parts, b6.o_dt, b6.o_di)
    group_2.along()
    group_3.cross()
    *group_2.everyone, group_3.parts, group_4.got = tie(
        *group_2.everyone, group_3.parts, group_4.got
    )
    group_3.along()
    group_4.cross()
    text_proj_grad, image_proj_grad, text_qkv_grad, image_qkv_grad = group_1.unpack()
    text_down_grad, image_down_grad, text_up_grad, image_up_grad = group_2.unpack()
    image_co_out_grad, image_co_in_grad, text_co_out_grad = group_3.unpack()
    group_4.along()
    text_co_in_grad, text_gains_grad, image_gains_grad = group_4.unpack()
    return (
        f2.o_tres,
        f2.o_ires,
        text_in_grad,
        image_in_grad,
        text_co_in_grad,
        image_co_in_grad,
        text_co_out_grad,
        image_co_out_grad,
        text_up_grad,
        text_down_grad,
        image_up_grad,
        image_down_grad,
        text_qkv_grad,
        text_proj_grad,
        image_qkv_grad,
        image_proj_grad,
        text_gains_grad,
        image_gains_grad,
    )


def solution(mesh):
    slots = P("dp", "seq", None)
    rows = P("dp", None)
    return jax.shard_map(
        per_device,
        mesh=mesh,
        in_specs=(slots, slots, rows, rows) + (P(),) * 14 + (slots, slots),
        out_specs=(slots,) * 4 + (rows,) * 12 + (P(), P()),
        check_vma=False,
    )
```

```python
import functools
import types

import jax
import jax.numpy as jnp
from jax import lax
from jax.experimental import pallas as pl
from jax.experimental.pallas import tpu as pltpu
from jax.sharding import PartitionSpec as P

HT = 12
HI = 8
HC = 8

NORM_EPS = 1e-05

F32 = jnp.float32
BF16 = jnp.bfloat16
LOG2E = 1.4426950408889634
MASKED = -1.0e9 * LOG2E
SQRT_2_PI = 0.7978845608028654
GELU_CUBE = 0.044715
LANES = 128
TILE = 256
WIDE = 1536
GAIN_ROWS = 32
MIB = 1024 * 1024


def dot_nt(a, b):
    return lax.dot_general(a, b, (((1,), (1,)), ((), ())), preferred_element_type=F32)


def dot_nn(a, b):
    return lax.dot_general(a, b, (((1,), (0,)), ((), ())), preferred_element_type=F32)


def dot_tn(a, b):
    return lax.dot_general(a, b, (((0,), (0,)), ((), ())), preferred_element_type=F32)


class Copies:
    def __init__(self, sems):
        self.sems, self.used, self.leaving = sems, 0, []

    def fetch(self, src, dst):
        copy = pltpu.make_async_copy(src, dst, self.sems.at[self.used])
        self.used += 1
        copy.start()
        return copy

    def flush(self, src, dst):
        self.leaving.append(self.fetch(src, dst))

    def finish(self):
        for copy in self.leaving:
            copy.wait()


def nbytes(shape, dtype):
    total = jnp.dtype(dtype).itemsize
    dims = list(shape)
    dims[-1] = -(-dims[-1] // 128) * 128
    if len(dims) > 1:
        dims[-2] = -(-dims[-2] // 16) * 16
    for d in dims:
        total *= d
    return total


def kernel_call(name, body, scal, ins, outs, scratch, copies=64, extra=8):
    names = list(ins) + list(outs) + list(scratch)

    def kernel(scal_ref, *refs):
        k = types.SimpleNamespace(**dict(zip(names, refs)))
        moves = Copies(refs[-1])
        body(scal_ref, k, moves)
        moves.finish()

    def place(where):
        return pl.BlockSpec(memory_space=pltpu.HBM if where == "h" else pltpu.VMEM)

    def shape_of(shape, dtype, where):
        return pltpu.HBM(tuple(shape), dtype) if where == "h" else jax.ShapeDtypeStruct(shape, dtype)

    args = [
        pltpu.with_memory_space_constraint(x, pltpu.HBM) if where == "h" else x for x, where in ins.values()
    ]
    total = sum(nbytes(s, d) for s, d in scratch.values()) + extra * MIB
    got = pl.pallas_call(
        kernel,
        in_specs=[pl.BlockSpec(memory_space=pltpu.SMEM)] + [place(w) for _, w in ins.values()],
        out_specs=[place(w) for _, _, w in outs.values()],
        out_shape=[shape_of(*o) for o in outs.values()],
        scratch_shapes=[pltpu.VMEM(tuple(s), d) for s, d in scratch.values()]
        + [pltpu.SemaphoreType.DMA((copies,))],
        compiler_params=pltpu.CompilerParams(vmem_limit_bytes=total),
        name=name,
    )(scal, *args)
    return types.SimpleNamespace(**dict(zip(outs, got)))


def loop(count, body, unroll=1):
    def step(i, carry):
        body(i)
        return carry

    lax.fori_loop(0, count, step, 0, unroll=unroll)


def at(i, size):
    return pl.ds(pl.multiple_of(i * size, size), size)


def row_chunks(rows, body):
    size = next(c for c in (128, 80, 64, 32, 16) if rows % c == 0)
    loop(rows // size, lambda i: body(at(i, size)))


def tile_of(width, limit):
    parts = -(-width // limit)
    while width % (parts * TILE):
        parts += 1
    return width // parts


def pick(i, values):
    out = values[0]
    for k in range(1, len(values)):
        out = jnp.where(i == k, values[k], out)
    return out


def lane_halves(width):
    if width == LANES:
        return [None]
    lane = lax.broadcasted_iota(jnp.int32, (1, LANES), 1)
    return [(lane // width) == i for i in range(LANES // width)]


def keep_lanes(x, sel):
    return x if sel is None else jnp.where(sel, x, jnp.zeros_like(x))


def cols(ref, rows, tile):
    return ref[rows, tile * LANES : (tile + 1) * LANES]


def store_bias(bias_ref, down_ref, along_ref):
    for r in range(bias_ref.shape[0]):
        row = down_ref[r : r + 1].astype(F32)
        col = jnp.transpose(jnp.broadcast_to(row, (8, row.shape[1])))[:, :1]
        bias_ref[r] = jnp.where(col == along_ref[r : r + 1].astype(F32), 0.0, MASKED).astype(F32)


def attend(r, q_ref, kv_ref, bias, o_ref, p_ref, lq, lk, width):
    scale = width**-0.5 * LOG2E
    sels = lane_halves(width)
    n = o_ref.shape[1] // LANES
    qs, ks = at(r, lq), at(r, lk)
    for t in range(n):
        q, k, v = cols(q_ref, qs, t), cols(kv_ref, ks, n + t), cols(kv_ref, ks, 2 * n + t)
        out = None
        for i, sel in enumerate(sels):
            s = dot_nt(k, keep_lanes(q, sel)) * scale + bias
            e = jnp.exp2(s - jnp.max(s, axis=0, keepdims=True))
            p = (e * (1.0 / jnp.sum(e, axis=0, keepdims=True))).astype(BF16)
            p_ref[r, t * len(sels) + i] = p
            o = dot_tn(p, v)
            out = o if out is None else jnp.where(sel, o, out)
        o_ref[qs, t * LANES : (t + 1) * LANES] = out.astype(BF16)


def attend_wide(r, q_ref, kv_ref, bias, o_ref, p_ref, lq, lk):
    scale = LANES**-0.5 * LOG2E
    n = o_ref.shape[1] // LANES
    qs, ks = at(r, lq), at(r, lk)
    for t in range(n):
        q, k, v = cols(q_ref, qs, t), cols(kv_ref, ks, n + t), cols(kv_ref, ks, 2 * n + t)
        s = dot_nt(q, k) * scale + bias
        e = jnp.exp2(s - jnp.max(s, axis=1, keepdims=True))
        p = (e * (1.0 / jnp.sum(e, axis=1, keepdims=True))).astype(BF16)
        p_ref[r, t] = p
        o_ref[qs, t * LANES : (t + 1) * LANES] = dot_nn(p, v).astype(BF16)


def attend_wide_back(r, q_ref, kv_ref, da_ref, p_ref, dq_ref, dkv_ref, lq, lk):
    scale = LANES**-0.5
    n = da_ref.shape[1] // LANES
    qs, ks = at(r, lq), at(r, lk)
    for t in range(n):
        q, k, v = cols(q_ref, qs, t), cols(kv_ref, ks, n + t), cols(kv_ref, ks, 2 * n + t)
        da = cols(da_ref, qs, t)
        p = p_ref[r, t]
        pf = p.astype(F32)
        w = pf * dot_nt(da, v)
        ds = (w - pf * jnp.sum(w, axis=1, keepdims=True)).astype(BF16)
        dq_ref[qs, t * LANES : (t + 1) * LANES] = (dot_nn(ds, k) * scale).astype(BF16)
        dkv_ref[ks, (n + t) * LANES : (n + t + 1) * LANES] = (dot_tn(ds, q) * scale).astype(BF16)
        dkv_ref[ks, (2 * n + t) * LANES : (2 * n + t + 1) * LANES] = dot_tn(p, da).astype(BF16)


def attend_back(r, q_ref, kv_ref, da_ref, p_ref, dq_ref, dkv_ref, lq, lk, width):
    scale = width**-0.5
    sels = lane_halves(width)
    n = da_ref.shape[1] // LANES
    qs, ks = at(r, lq), at(r, lk)
    for t in range(n):
        q, k, v = cols(q_ref, qs, t), cols(kv_ref, ks, n + t), cols(kv_ref, ks, 2 * n + t)
        da = cols(da_ref, qs, t)
        dq = dk = dv = None
        for i, sel in enumerate(sels):
            p = p_ref[r, t * len(sels) + i]
            da_h = keep_lanes(da, sel)
            pf = p.astype(F32)
            w = pf * dot_nt(v, da_h)
            ds = (w - pf * jnp.sum(w, axis=0, keepdims=True)).astype(BF16)
            dv_h = dot_nn(p, da_h)
            dk_h = dot_nn(ds, keep_lanes(q, sel))
            dq_h = dot_tn(ds, keep_lanes(k, sel))
            dq = dq_h if dq is None else dq + dq_h
            dk = dk_h if dk is None else dk + dk_h
            dv = dv_h if dv is None else dv + dv_h
        dq_ref[qs, t * LANES : (t + 1) * LANES] = (dq * scale).astype(BF16)
        dkv_ref[ks, (n + t) * LANES : (n + t + 1) * LANES] = (dk * scale).astype(BF16)
        dkv_ref[ks, (2 * n + t) * LANES : (2 * n + t + 1) * LANES] = dv.astype(BF16)


def normalize(z):
    center = z - jnp.mean(z, axis=-1, keepdims=True)
    inv = lax.rsqrt(jnp.mean(center * center, axis=-1, keepdims=True) + NORM_EPS)
    return center * inv, inv


def fold_rows(x):
    return jnp.sum(x.reshape(x.shape[0] // 8, 8, x.shape[1]), axis=0)


def matmul_tiles(x_ref, w_ref, o_ref):
    n = o_ref.shape[1]
    tile = tile_of(n, WIDE)

    def step(i):
        o_ref[:, at(i, tile)] = dot_nn(x_ref[...], w_ref[:, at(i, tile)]).astype(o_ref.dtype)

    loop(n // tile, step)


def norm_rows(acc_ref, res, gain, n_ref, inv_ref, low_ref=None):
    def chunk(rows):
        n, inv = normalize(acc_ref[rows] + res(rows))
        n_ref[rows] = n
        inv_ref[rows] = jnp.broadcast_to(inv, (inv.shape[0], LANES))
        if low_ref is not None:
            low_ref[rows] = (n * gain).astype(BF16)

    row_chunks(acc_ref.shape[0], chunk)


def norm_back_rows(dy_of, n_ref, inv_ref, gain, d_ref, low_ref, dg_ref):
    dg_ref[...] = jnp.zeros_like(dg_ref)

    def chunk(rows):
        dy = dy_of(rows)
        n = n_ref[rows]
        dn = dy * gain
        m1 = jnp.mean(dn, axis=-1, keepdims=True)
        m2 = jnp.mean(dn * n, axis=-1, keepdims=True)
        d = inv_ref[rows][:, :1] * (dn - m1 - n * m2)
        d_ref[rows] = d
        low_ref[rows] = d.astype(BF16)
        dg_ref[...] += fold_rows(dy * n)

    row_chunks(n_ref.shape[0], chunk)


def gelu_pair(v):
    v2 = v * v
    s = 0.5 + 0.5 * jnp.tanh(v * (SQRT_2_PI + (SQRT_2_PI * GELU_CUBE) * v2))
    a = v * s
    return a, s + a * (1.0 - s) * (2.0 * SQRT_2_PI + (6.0 * SQRT_2_PI * GELU_CUBE) * v2)


def ffn_tiles(x_ref, up_ref, down_ref, a_ref, slope_ref, acc_ref):
    width = tile_of(a_ref.shape[1], WIDE)

    def step(i):
        tile = at(i, width)
        a, slope = gelu_pair(dot_nn(x_ref[...], up_ref[:, tile]))
        a = a.astype(BF16)
        a_ref[:, tile] = a
        slope_ref[:, tile] = slope.astype(BF16)
        acc_ref[...] += dot_nn(a, down_ref[tile])

    acc_ref[...] = jnp.zeros_like(acc_ref)
    loop(a_ref.shape[1] // width, step)


def ffn_back_tiles(low_ref, down_ref, slope_ref, up_ref, dh_ref, acc_ref):
    width = tile_of(dh_ref.shape[1], WIDE)

    def step(i):
        tile = at(i, width)
        dh = (dot_nt(low_ref[...], down_ref[tile]) * slope_ref[:, tile].astype(F32)).astype(BF16)
        dh_ref[:, tile] = dh
        acc_ref[...] += dot_nt(dh, up_ref[:, tile])

    loop(dh_ref.shape[1] // width, step)


def send_packed(cp, keep, send, far_keep, far_send, first, last):
    for near, far in ((send, far_send), (keep, far_keep)):
        cp.flush(near.at[:, first:last], far.at[:, first:last])


def wgrad_group(scal, cp, xs, ys, plan, ndp, keep, send, far_keep, far_send):
    by_member = all(off % 16 == 0 and (tiles * rows) % 16 == 0 for tiles, _, _, off, rows in plan)
    for x, y, p in zip(xs, ys, plan):
        wgrad_member(scal, x, y, keep, send, p, ndp)
        if by_member:
            send_packed(cp, keep, send, far_keep, far_send, p[3], p[3] + p[0] * p[4])
    if not by_member:
        send_packed(cp, keep, send, far_keep, far_send, 0, keep.shape[1])


def wgrad_member(scal_ref, x_ref, y_ref, keep_ref, send_ref, plan, ndp):
    tiles, total, split, off, rows = plan
    odd = scal_ref[0] == 1
    xt = jnp.transpose(x_ref[...])
    first = jnp.minimum(scal_ref[1] * tiles, total - tiles) if split else 0
    for t in range(tiles):
        g = dot_nn(xt, y_ref[:, at(first + t, TILE)]).astype(BF16)
        base = off + t * rows
        for j in range(ndp // 2):
            even_rows = g[2 * j * rows : (2 * j + 1) * rows]
            odd_rows = g[(2 * j + 1) * rows : (2 * j + 2) * rows]
            keep_ref[j, base : base + rows] = jnp.where(odd, odd_rows, even_rows)
            send_ref[j, base : base + rows] = jnp.where(odd, even_rows, odd_rows)


def pack_gains(gain_refs, rows_ref, keep_ref, send_ref, base):
    row = 0
    for ref in gain_refs:
        total = jnp.sum(ref[...], axis=0, keepdims=True)
        for c in range(0, ref.shape[1], TILE):
            rows_ref[row : row + 1] = total[:, c : c + TILE]
            row += 1
    for row in range(row, GAIN_ROWS):
        rows_ref[row : row + 1] = jnp.zeros((1, TILE), F32)
    low = rows_ref[...].astype(BF16)
    for j in range(keep_ref.shape[0]):
        keep_ref[j, base : base + GAIN_ROWS] = low
        send_ref[j, base : base + GAIN_ROWS] = low


def co_stage_body(scal, k, cp, *, rows, parts, count_t, count_i):
    pieces = [cp.fetch(getattr(k, f"part{i}"), k.staged.at[i]) for i in range(parts)]
    wa = cp.fetch(k.co_t, k.wa)
    wb = cp.fetch(k.co_i, k.wb)
    wo = cp.fetch(k.out_t, k.wo)
    wd = cp.fetch(k.down_t, k.wd)
    lt, li = parts * count_t, parts * count_i
    store_bias(k.bias, k.iseg, k.tseg)
    for piece in pieces:
        piece.wait()
    base = join_tiles(scal[1], k.staged, k.tx, count_t, rows, 0)
    wa.wait()
    matmul_tiles(k.tx, k.wa, k.tqkv)
    up_t = cp.fetch(k.up_t, k.wa)
    cp.flush(k.tx, k.o_tx)
    cp.flush(k.tqkv, k.o_tqkv)
    join_tiles(scal[1], k.staged, k.ix, count_i, rows, base)
    wb.wait()
    matmul_tiles(k.ix, k.wb, k.iqkv)
    wi = k.ix.shape[1]
    up_i = cp.fetch(k.up_i, k.wb.at[:, 0:wi])
    down_i = cp.fetch(k.down_i, k.wb.at[:, wi : 2 * wi])
    out_i = cp.fetch(k.out_i, k.wb.at[:, 2 * wi : 3 * wi])
    cp.flush(k.ix, k.o_ix)
    cp.flush(k.iqkv, k.o_iqkv)
    assert k.tatt.shape[1] == HC * LANES

    def heads(r):
        attend(r, k.tqkv, k.iqkv, k.bias[r], k.tatt, k.pt, lt, li, LANES)
        attend_wide(r, k.iqkv, k.tqkv, k.bias[r], k.iatt, k.pi, li, lt)

    loop(rows, heads)
    cp.flush(k.tatt, k.o_tatt)
    cp.flush(k.iatt, k.o_iatt)
    cp.flush(k.pt, k.o_pt)
    cp.flush(k.pi, k.o_pi)
    out_i.wait()
    matmul_tiles(k.iatt, k.wb.at[:, 2 * wi : 3 * wi], k.acc_i)
    ig = k.ig[...]
    norm_rows(k.acc_i, lambda r: k.ix[r].astype(F32), ig[0:1], k.in1, k.ir1, k.i1)
    up_i.wait()
    down_i.wait()
    ffn_tiles(k.i1, k.wb.at[:, 0:wi], k.wb.at[:, wi : 2 * wi], k.ia, k.isl, k.acc_i)
    norm_rows(k.acc_i, lambda r: k.in1[r] * ig[0:1], ig[1:2], k.in2, k.ir2, k.i2)
    for name in ("in1", "ir1", "i1", "ia", "isl", "in2", "ir2", "i2"):
        cp.flush(getattr(k, name), getattr(k, "o_" + name))
    wo.wait()
    matmul_tiles(k.tatt, k.wo, k.acc_t)
    tg = k.tg[...]
    norm_rows(k.acc_t, lambda r: k.tx[r].astype(F32), tg[0:1], k.tn1, k.tr1, k.t1)
    up_t.wait()
    wd.wait()
    for name in ("tn1", "tr1", "t1"):
        cp.flush(getattr(k, name), getattr(k, "o_" + name))
    ffn_tiles(k.t1, k.wa, k.wd, k.ta, k.tsl, k.acc_t)
    cp.flush(k.ta, k.o_ta)
    cp.flush(k.tsl, k.o_tsl)
    norm_rows(k.acc_t, lambda r: k.tn1[r] * tg[0:1], tg[1:2], k.tn2, k.tr2, k.t2)
    for name in ("t2", "tn2", "tr2"):
        cp.flush(getattr(k, name), getattr(k, "o_" + name))


def self_stage_body(scal, k, cp, *, rows, count_t, count_i):
    t2 = cp.fetch(k.h_t2, k.t2)
    wa = cp.fetch(k.qkv_t, k.wa)
    i2 = cp.fetch(k.h_i2, k.i2)
    wb = cp.fetch(k.qkv_i, k.wb)
    pa = cp.fetch(k.proj_t, k.pa)
    pb = cp.fetch(k.proj_i, k.pb)
    tn2 = cp.fetch(k.h_tn2, k.tn2)
    in2 = cp.fetch(k.h_in2, k.in2)
    store_bias(k.tbias, k.tseg, k.tseg)
    store_bias(k.ibias, k.iseg, k.iseg)
    lt = k.t2.shape[0] // rows
    li = k.i2.shape[0] // rows
    t2.wait()
    wa.wait()
    matmul_tiles(k.t2, k.wa, k.sqkv)
    cp.flush(k.sqkv, k.o_sqkv)
    i2.wait()
    wb.wait()
    matmul_tiles(k.i2, k.wb, k.uqkv)
    cp.flush(k.uqkv, k.o_uqkv)
    wt = k.tmix.shape[1] // HT
    wi = k.imix.shape[1] // HI

    def heads(r):
        attend(r, k.sqkv, k.sqkv, k.tbias[r], k.tmix, k.spt, lt, lt, wt)
        attend(r, k.uqkv, k.uqkv, k.ibias[r], k.imix, k.spi, li, li, wi)

    loop(rows, heads)
    for name in ("tmix", "imix", "spt", "spi"):
        cp.flush(getattr(k, name), getattr(k, "o_" + name))
    tn2.wait()
    in2.wait()
    z = scal[1]
    for mix, w, ready, acc, n2, g, n3, r3, res, count in (
        (k.tmix, k.pa, pa, k.acc_t, k.tn2, k.tg, k.tn3, k.tr3, k.o_tres, count_t),
        (k.imix, k.pb, pb, k.acc_i, k.in2, k.ig, k.in3, k.ir3, k.o_ires, count_i),
    ):
        ready.wait()
        matmul_tiles(mix, w, acc)
        gain = g[...]
        norm_rows(acc, lambda r, n2=n2, gain=gain: n2[r] * gain[1:2], None, n3, r3)
        length = mix.shape[0] // rows
        for r in range(rows):
            own = n3[pl.ds(pl.multiple_of(r * length + z * count, 8), count)]
            res[r] = (own * gain[2:3]).astype(BF16)
    for name in ("tn3", "in3", "tr3", "ir3"):
        cp.flush(getattr(k, name), getattr(k, "o_" + name))


def self_back_body(scal, k, cp, *, rows, count_t, count_i, plan, ndp):
    ups = [cp.fetch(getattr(k, f"h_up{i}"), k.up.at[i]) for i in range(k.up.shape[0])]
    names = ("tn3", "tr3", "proj_t", "in3", "ir3", "proj_i", "sqkv", "spt", "uqkv", "spi")
    names += ("tmix", "imix", "t2", "i2")
    moves = {n: cp.fetch(getattr(k, "h_" + n), getattr(k, n)) for n in names}

    def ready(*which):
        for n in which:
            moves[n].wait()

    for copy in ups:
        copy.wait()
    base = join_tiles(scal[1], k.up, k.tup, count_t, rows, 0)
    join_tiles(scal[1], k.up, k.iup, count_i, rows, base)
    ready("tn3", "tr3", "proj_t")
    norm_back_rows(
        lambda r: k.tup[r].astype(F32), k.tn3, k.tr3, k.tg[2:3], k.o_d3, k.d3b, k.tdg
    )
    k.dmt[...] = dot_nt(k.d3b[...], k.proj_t[...]).astype(BF16)
    ready("in3", "ir3", "proj_i")
    norm_back_rows(
        lambda r: k.iup[r].astype(F32), k.in3, k.ir3, k.ig[2:3], k.o_e3, k.e3b, k.idg
    )
    k.dmi[...] = dot_nt(k.e3b[...], k.proj_i[...]).astype(BF16)
    ready("sqkv", "spt", "uqkv", "spi")
    lt, li = k.tup.shape[0] // rows, k.iup.shape[0] // rows
    wt = k.dmt.shape[1] // HT
    wi = k.dmi.shape[1] // HI

    def heads(r):
        attend_back(r, k.sqkv, k.sqkv, k.dmt, k.spt, k.o_dsqkv, k.o_dsqkv, lt, lt, wt)
        attend_back(r, k.uqkv, k.uqkv, k.dmi, k.spi, k.o_duqkv, k.o_duqkv, li, li, wi)

    loop(rows, heads)
    ready("tmix", "imix", "t2", "i2")
    xs, ys = (k.tmix, k.imix, k.t2, k.i2), (k.d3b, k.e3b, k.o_dsqkv, k.o_duqkv)
    wgrad_group(scal, cp, xs, ys, plan, ndp, k.keep, k.send, k.o_keep, k.o_send)
    for name in ("tdg", "idg"):
        cp.flush(getattr(k, name), getattr(k, "o_" + name))


def chunked(cp, src, dst, axis, count=3):
    size = src.shape[axis] // count
    out = []
    for i in range(count):
        part = slice(i * size, (i + 1) * size)
        part = (slice(None), part) if axis == 1 else (part, slice(None))
        out.append((cp.fetch(src.at[part], dst.at[part]), part))
    return out


def qkv_back_body(scal, k, cp):
    wa = cp.fetch(k.qkv_t, k.wa)
    extra_t = [cp.fetch(k.h_tn2, k.tn2), cp.fetch(k.h_tr2, k.tr2)]
    wb = cp.fetch(k.qkv_i, k.wb)
    extra_i = [cp.fetch(k.h_in2, k.in2), cp.fetch(k.h_ir2, k.ir2)]
    for dx, w, ready, extra, acc, d3, n, inv, g, outs in (
        (k.dsqkv, k.wa, wa, extra_t, k.acc_t, k.d3, k.tn2, k.tr2, k.tg, ("d2", "d2b", "tdg")),
        (k.duqkv, k.wb, wb, extra_i, k.acc_i, k.e3, k.in2, k.ir2, k.ig, ("e2", "e2b", "idg")),
    ):
        ready.wait()
        acc[...] = dot_nt(dx[...], w[...])
        for copy in extra:
            copy.wait()
        d2, low, dg = (getattr(k, name) for name in outs)
        norm_back_rows(lambda r, acc=acc, d3=d3: d3[r] + acc[r], n, inv, g[1:2], d2, low, dg)
        for name in outs:
            cp.flush(getattr(k, name), getattr(k, "o_" + name))


def ffn_back_body(scal, k, cp, *, plan, ndp):
    def start(*names):
        return [cp.fetch(getattr(k, "h_" + n), getattr(k, n)) for n in names]

    moves = start("e2b", "down_i", "isl", "up_i")
    y1 = cp.fetch(k.h_e2, k.y1)
    later = start("d2b", "down_t", "tsl", "up_t")
    x1 = cp.fetch(k.h_d2, k.x1)
    last = start("ta", "ia", "t1", "i1")
    for copy in (*moves, y1):
        copy.wait()
    ffn_back_tiles(k.e2b, k.down_i, k.isl, k.up_i, k.dhi, k.y1)
    cp.flush(k.y1, k.o_y1)
    for copy in (*later, x1):
        copy.wait()
    ffn_back_tiles(k.d2b, k.down_t, k.tsl, k.up_t, k.dht, k.x1)
    cp.flush(k.x1, k.o_x1)
    for copy in last:
        copy.wait()
    xs, ys = (k.ta, k.ia, k.t1, k.i1), (k.d2b, k.e2b, k.dht, k.dhi)
    wgrad_group(scal, cp, xs, ys, plan, ndp, k.keep, k.send, k.o_keep, k.o_send)


def first_norm_back_body(scal, k, cp, *, rows, count_t, count_i):
    moves_t = [cp.fetch(getattr(k, "h_" + n), getattr(k, n)) for n in ("x1", "tn1", "tr1", "out_t")]
    moves_i = [cp.fetch(getattr(k, "h_" + n), getattr(k, n)) for n in ("y1", "in1", "ir1", "out_i")]
    z = scal[1]
    for moves, x1, n, inv, g, d1, low, dg, w, da, own, count in (
        (moves_t, k.x1, k.tn1, k.tr1, k.tg, k.d1, k.d1b, k.tdg, k.out_t, k.dat, k.own_t, count_t),
        (moves_i, k.y1, k.in1, k.ir1, k.ig, k.e1, k.e1b, k.idg, k.out_i, k.dai, k.own_i, count_i),
    ):
        for copy in moves:
            copy.wait()
        norm_back_rows(lambda r, x1=x1: x1[r], n, inv, g[0:1], d1, low, dg)
        da[...] = dot_nt(low[...], w[...]).astype(BF16)
        length = x1.shape[0] // rows
        for r in range(rows):
            own[r] = d1[pl.ds(pl.multiple_of(r * length + z * count, 8), count)]
    for name in ("dat", "dai", "d1b", "e1b", "own_t", "own_i", "tdg", "idg"):
        cp.flush(getattr(k, name), getattr(k, "o_" + name))


def co_back_body(scal, k, cp, *, rows, parts, count_t, count_i, plan, last_plan, ndp, gains_at):
    names = ("tqkv", "pt", "dat", "iqkv", "pi", "dai", "iatt", "e1b", "tatt", "d1b", "ix", "tx")
    names += ("tdg1", "tdg2", "tdg3", "idg1", "idg2", "idg3")
    moves = [cp.fetch(getattr(k, "h_" + n), getattr(k, n)) for n in names]
    for copy in moves[:6]:
        copy.wait()
    lt, li = parts * count_t, parts * count_i
    def heads(r):
        attend_back(r, k.tqkv, k.iqkv, k.dat, k.pt, k.dt, k.di, lt, li, LANES)
        attend_wide_back(r, k.iqkv, k.tqkv, k.dai, k.pi, k.di, k.dt, li, lt)

    loop(rows, heads)
    for copy in moves[6:]:
        copy.wait()
    xs, ys = (k.iatt, k.ix, k.tatt), (k.e1b, k.di, k.d1b)
    wgrad_group(scal, cp, xs, ys, plan, ndp, k.keep, k.send, k.o_keep, k.o_send)
    gains = (k.tdg1, k.tdg2, k.tdg3, k.idg1, k.idg2, k.idg3)
    pack_gains(gains, k.gain_rows, k.keep_last, k.send_last, gains_at)
    wgrad_member(scal, k.tx, k.dt, k.keep_last, k.send_last, last_plan, ndp)
    cp.flush(k.send_last, k.o_send_last)
    cp.flush(k.keep_last, k.o_keep_last)
    z = scal[1]
    for full, own, count in ((k.dt, k.o_dt, count_t), (k.di, k.o_di, count_i)):
        for r in range(rows):
            values = [
                full[(r * parts + i) * count : (r * parts + i + 1) * count] for i in range(parts)
            ]
            own[r] = pick(z, values)


def in_back_body(scal, k, cp):
    own_t = cp.fetch(k.h_d1, k.d1)
    own_i = cp.fetch(k.h_e1, k.e1)
    wa = chunked(cp, k.co_t, k.wa, 1)
    wb = chunked(cp, k.co_i, k.wb, 1)
    for dx, w, chunks, d1, out, own in (
        (k.dt, k.wa, wa, k.d1, k.o_dt, own_t),
        (k.di, k.wb, wb, k.e1, k.o_di, own_i),
    ):
        own.wait()
        r, count, m = dx.shape
        flat = dx[...].reshape(r * count, m)
        total = d1[...].reshape(r * count, d1.shape[2])
        for copy, part in chunks:
            copy.wait()
            total = total + dot_nt(flat[part], w[part])
        out[...] = total.reshape(out.shape)


def pack_body(scal, k, cp, *, count):
    names = [f"{stream}{i}" for i in range(count) for stream in "ti"]
    moves = {name: cp.fetch(getattr(k, "h_" + name), getattr(k, name)) for name in names}
    for i in range(count):
        packed = getattr(k, f"s{i}")
        base = 0
        for name in (f"t{i}", f"i{i}"):
            moves[name].wait()
            ref = getattr(k, name)
            for c in range(0, ref.shape[2], TILE):
                for r in range(ref.shape[0]):
                    part = ref[r, :, c : c + TILE]
                    packed[base : base + part.shape[0]] = part
                    base += part.shape[0]
        cp.flush(packed, getattr(k, f"o{i}"))


def join_tiles(z, staged, full, count, rows, base):
    parts = staged.shape[0]
    for c in range(0, full.shape[1], TILE):
        for r in range(rows):
            values = [staged[i, base : base + count] for i in range(parts)]
            for i in range(parts):
                to = (r * parts + i) * count
                full[to : to + count, c : c + TILE] = pick(z ^ i, values)
            base += count
    return base


def unpack_body(scal, k, cp, *, plan, nseq, gains_at, gain_shapes):
    z = scal[1]
    pieces = [cp.fetch(getattr(k, f"h{i}"), getattr(k, f"p{i}")) for i in range(nseq)]
    low = None
    if hasattr(k, "own"):
        cp.fetch(k.h_own, k.own).wait()
        low = k.own
    if gain_shapes:
        sums = low[gains_at : gains_at + GAIN_ROWS].astype(F32)
        row = 0
        for i, (count, width) in enumerate(gain_shapes):
            out = getattr(k, f"o_gain{i}")
            for g in range(count):
                for c in range(0, width, TILE):
                    out[g : g + 1, c : c + TILE] = sums[row : row + 1]
                    row += 1
    for i, (tiles, total, split, off, rows) in enumerate(plan):
        if not split:
            buf = getattr(k, f"b{i}")
            for t in range(tiles):
                buf[:, t * TILE : (t + 1) * TILE] = low[off + t * rows : off + (t + 1) * rows].astype(F32)
            cp.flush(buf, getattr(k, f"o{i}"))
    for piece in pieces:
        piece.wait()
    for i, (tiles, total, split, off, rows) in enumerate(plan):
        if split:
            buf = getattr(k, f"b{i}")
            for s in range(nseq):
                ref = getattr(k, f"p{s}")
                first = jnp.minimum((z ^ s) * tiles, total - tiles)
                for t in range(tiles):
                    buf[:, at(first + t, TILE)] = ref[off + t * rows : off + (t + 1) * rows].astype(F32)
            cp.flush(buf, getattr(k, f"o{i}"))


class Comm:
    def __init__(self):
        self.nseq = lax.axis_size("seq")
        self.ndp = lax.axis_size("dp")
        self.z = lax.axis_index("seq")
        self.d = lax.axis_index("dp")
        self.scal = jnp.stack([self.d % 2, self.z]).astype(jnp.int32)

    def pieces_at_once(self, x):
        n = self.nseq
        return [x] + [lax.ppermute(x, "seq", [(i, i ^ k) for i in range(n)]) for k in range(1, n)]

    def pieces(self, x):
        n = self.nseq
        got = [x]
        for k in range(1, n):
            step = k & -k
            got.append(lax.ppermute(got[k ^ step], "seq", [(i, i ^ step) for i in range(n)]))
        return got

    def pack(self, *pairs):
        ins, outs, scratch = {}, {}, {}
        for i, (text, image) in enumerate(pairs):
            total = sum(x.shape[0] * x.shape[1] * (x.shape[2] // TILE) for x in (text, image))
            ins.update({f"h_t{i}": (text, "h"), f"h_i{i}": (image, "h")})
            scratch.update({f"t{i}": (text.shape, BF16), f"i{i}": (image.shape, BF16)})
            outs[f"o{i}"] = ((total, TILE), BF16, "h")
            scratch[f"s{i}"] = ((total, TILE), BF16)
        got = kernel_call(
            "pack",
            functools.partial(pack_body, count=len(pairs)),
            self.scal,
            ins,
            outs,
            scratch,
            copies=3 * len(pairs),
            extra=2,
        )
        return [getattr(got, name) for name in outs]

    def plan_of(self, members):
        plan = {}
        off = 0
        for want in (True, False):
            for i, (din, dout, split) in enumerate(members):
                if split != want:
                    continue
                total = dout // TILE
                tiles = -(-total // self.nseq) if split else total
                rows = din // self.ndp
                plan[i] = (tiles, total, split, off, rows)
                off += tiles * rows
            if want:
                split_rows = off
        return Plan(self, [plan[i] for i in range(len(members))], split_rows, off)


class Plan:
    def __init__(self, comm, members, split_rows, rows, gain_shapes=()):
        self.comm, self.members, self.split_rows, self.rows = comm, members, split_rows, rows
        self.gain_shapes = gain_shapes
        self.gains_at = rows

    def with_gains(self, shapes):
        self.gain_shapes = shapes
        self.rows += GAIN_ROWS
        return self

    def half(self):
        return (self.comm.ndp // 2, self.rows, TILE)

    def swap(self, keep, send):
        self.keep = keep
        self.got = lax.ppermute(send, "dp", [(i, i ^ 1) for i in range(self.comm.ndp)])

    def add(self):
        self.pair = (self.keep.astype(F32) + self.got.astype(F32)).astype(BF16)

    def cross(self):
        groups = [list(range(b, self.comm.ndp, 2)) for b in range(2)]
        self.parts = lax.all_to_all(
            self.pair, "dp", split_axis=0, concat_axis=0, tiled=True, axis_index_groups=groups
        )

    def along(self):
        def total(part):
            return jnp.sum(part.astype(F32), axis=0).astype(BF16)

        self.everyone = []
        if self.split_rows:
            self.everyone = self.comm.pieces(total(self.parts[:, : self.split_rows]))
        self.own = total(self.parts[:, self.split_rows :]) if self.rows > self.split_rows else None

    def unpack(self):
        plan = [(p[0], p[1], p[2], p[3] if p[2] else p[3] - self.split_rows, p[4]) for p in self.members]
        ins = {f"h{i}": (x, "h") for i, x in enumerate(self.everyone)}
        if self.rows > self.split_rows:
            ins["h_own"] = (self.own, "h")
        outs = {f"o{i}": ((p[4], p[1] * TILE), F32, "h") for i, p in enumerate(plan)}
        outs.update({f"o_gain{i}": (s, F32, "v") for i, s in enumerate(self.gain_shapes)})
        scratch = {f"p{i}": (x.shape, BF16) for i, x in enumerate(self.everyone)}
        if self.rows > self.split_rows:
            scratch["own"] = (self.own.shape, BF16)
        scratch.update({f"b{i}": ((p[4], p[1] * TILE), F32) for i, p in enumerate(plan)})
        got = kernel_call(
            "unpack",
            functools.partial(
                unpack_body,
                plan=plan,
                nseq=len(self.everyone),
                gains_at=self.gains_at - self.split_rows,
                gain_shapes=self.gain_shapes,
            ),
            self.comm.scal,
            ins,
            outs,
            scratch,
            copies=16,
        )
        return [getattr(got, name) for name in outs]


def tie(*xs):
    return lax.optimization_barrier(xs)


def per_device(
    text_in,
    image_in,
    text_seg,
    image_seg,
    text_co_in,
    image_co_in,
    text_co_out,
    image_co_out,
    text_up,
    text_down,
    image_up,
    image_down,
    text_qkv,
    text_proj,
    image_qkv,
    image_proj,
    text_gains,
    image_gains,
    text_upstream,
    image_upstream,
):
    comm = Comm()
    scal = comm.scal
    n = comm.nseq
    rows, nt, dt = text_in.shape
    ni, di = image_in.shape[1:]
    lt, li = n * nt, n * ni
    tt, ti = rows * lt, rows * li
    dc = text_co_out.shape[0]
    ft, fi = text_up.shape[1], image_up.shape[1]
    segs = {"tseg": (text_seg, "v"), "iseg": (image_seg, "v")}
    gains = {"tg": (text_gains, "v"), "ig": (image_gains, "v")}

    inputs, upstream = comm.pack((text_in, image_in), (text_upstream, image_upstream))
    inputs = comm.pieces(inputs)
    upstream, *inputs = tie(upstream, *inputs)
    upstream = comm.pieces_at_once(upstream)

    def saved(**shapes):
        return (
            {"o_" + name: (shape, dtype, "h") for name, (shape, dtype) in shapes.items()},
            {name: (shape, dtype) for name, (shape, dtype) in shapes.items()},
        )

    outs, scratch = saved(
        tx=((tt, dt), BF16),
        ix=((ti, di), BF16),
        tqkv=((tt, 3 * dc), BF16),
        iqkv=((ti, 3 * dc), BF16),
        tatt=((tt, dc), BF16),
        iatt=((ti, dc), BF16),
        pt=((rows, HC, li, lt), BF16),
        pi=((rows, HC, li, lt), BF16),
        tn1=((tt, dt), F32),
        tr1=((tt, LANES), F32),
        t1=((tt, dt), BF16),
        in1=((ti, di), F32),
        ir1=((ti, LANES), F32),
        i1=((ti, di), BF16),
        ta=((tt, ft), BF16),
        tsl=((tt, ft), BF16),
        ia=((ti, fi), BF16),
        isl=((ti, fi), BF16),
        tr2=((tt, LANES), F32),
        ir2=((ti, LANES), F32),
        tn2=((tt, dt), F32),
        t2=((tt, dt), BF16),
        in2=((ti, di), F32),
        i2=((ti, di), BF16),
    )
    scratch.update(
        staged=((n,) + inputs[0].shape, BF16),
        bias=((rows, li, lt), F32),
        wa=((dt, 3 * dc), BF16),
        wb=((di, 3 * dc), BF16),
        wo=((dc, dt), BF16),
        wd=((ft, dt), BF16),
        acc_t=((tt, dt), F32),
        acc_i=((ti, di), F32),
    )
    ins = {f"part{i}": (x, "h") for i, x in enumerate(inputs)}
    ins.update(
        co_t=(text_co_in, "h"),
        co_i=(image_co_in, "h"),
        out_t=(text_co_out, "h"),
        out_i=(image_co_out, "h"),
        up_t=(text_up, "h"),
        down_t=(text_down, "h"),
        up_i=(image_up, "h"),
        down_i=(image_down, "h"),
        **segs,
        **gains,
    )
    f1 = kernel_call(
        "co_stage",
        functools.partial(co_stage_body, rows=rows, parts=n, count_t=nt, count_i=ni),
        scal,
        ins,
        outs,
        scratch,
    )

    outs, scratch = saved(
        sqkv=((tt, 3 * dt), BF16),
        uqkv=((ti, 3 * di), BF16),
        tmix=((tt, dt), BF16),
        imix=((ti, di), BF16),
        spt=((rows, HT, lt, lt), BF16),
        spi=((rows, HI, li, li), BF16),
        tn3=((tt, dt), F32),
        tr3=((tt, LANES), F32),
        in3=((ti, di), F32),
        ir3=((ti, LANES), F32),
    )
    outs.update(o_tres=((rows, nt, dt), BF16, "v"), o_ires=((rows, ni, di), BF16, "v"))
    scratch.update(
        wa=(text_qkv.shape, BF16),
        wb=(image_qkv.shape, BF16),
        pa=(text_proj.shape, BF16),
        pb=(image_proj.shape, BF16),
        acc_t=((tt, dt), F32),
        acc_i=((ti, di), F32),
        t2=((tt, dt), BF16),
        i2=((ti, di), BF16),
        tn2=((tt, dt), F32),
        in2=((ti, di), F32),
        tbias=((rows, lt, lt), F32),
        ibias=((rows, li, li), F32),
    )
    f2 = kernel_call(
        "self_stage",
        functools.partial(self_stage_body, rows=rows, count_t=nt, count_i=ni),
        scal,
        dict(
            h_t2=(f1.o_t2, "h"),
            h_i2=(f1.o_i2, "h"),
            h_tn2=(f1.o_tn2, "h"),
            h_in2=(f1.o_in2, "h"),
            qkv_t=(text_qkv, "h"),
            qkv_i=(image_qkv, "h"),
            proj_t=(text_proj, "h"),
            proj_i=(image_proj, "h"),
            **segs,
            **gains,
        ),
        outs,
        scratch,
    )

    group_1 = comm.plan_of([(dt, dt, True), (di, di, True), (dt, 3 * dt, True), (di, 3 * di, True)])
    group_2 = comm.plan_of([(ft, dt, True), (fi, di, True), (dt, ft, True), (di, fi, True)])
    group_3 = comm.plan_of([(dc, di, True), (di, 3 * dc, True), (dc, dt, True)])
    group_4 = comm.plan_of([(dt, 3 * dc, False)]).with_gains([text_gains.shape, image_gains.shape])

    def sources(**arrays):
        return (
            {"h_" + name: (x, "h") for name, x in arrays.items()},
            {name: (x.shape, x.dtype) for name, x in arrays.items()},
        )

    def packed(group, tag=""):
        shape = group.half()
        return (
            {"o_keep" + tag: (shape, BF16, "h"), "o_send" + tag: (shape, BF16, "h")},
            {"keep" + tag: (shape, BF16), "send" + tag: (shape, BF16)},
        )

    ins, scratch = sources(
        tn3=f2.o_tn3,
        tr3=f2.o_tr3,
        proj_t=text_proj,
        in3=f2.o_in3,
        ir3=f2.o_ir3,
        proj_i=image_proj,
        sqkv=f2.o_sqkv,
        spt=f2.o_spt,
        uqkv=f2.o_uqkv,
        spi=f2.o_spi,
        tmix=f2.o_tmix,
        imix=f2.o_imix,
        t2=f1.o_t2,
        i2=f1.o_i2,
    )
    ins.update({f"h_up{i}": (x, "h") for i, x in enumerate(upstream)})
    outs, more = packed(group_1)
    scratch.update(
        **more,
        up=((n,) + upstream[0].shape, BF16),
        tup=((tt, dt), BF16),
        iup=((ti, di), BF16),
        d3b=((tt, dt), BF16),
        e3b=((ti, di), BF16),
        dmt=((tt, dt), BF16),
        dmi=((ti, di), BF16),
        tdg=((8, dt), F32),
        idg=((8, di), F32),
    )
    outs.update(
        o_d3=((tt, dt), F32, "v"),
        o_e3=((ti, di), F32, "v"),
        o_dsqkv=((tt, 3 * dt), BF16, "v"),
        o_duqkv=((ti, 3 * di), BF16, "v"),
        o_tdg=((8, dt), F32, "h"),
        o_idg=((8, di), F32, "h"),
    )
    b1 = kernel_call(
        "self_back",
        functools.partial(
            self_back_body, rows=rows, count_t=nt, count_i=ni, plan=group_1.members, ndp=comm.ndp
        ),
        scal,
        {**ins, **gains},
        outs,
        scratch,
    )
    group_1.swap(b1.o_keep, b1.o_send)

    ins, scratch = sources(tn2=f1.o_tn2, tr2=f1.o_tr2, in2=f1.o_in2, ir2=f1.o_ir2)
    outs, more = saved(
        d2=((tt, dt), F32),
        e2=((ti, di), F32),
        d2b=((tt, dt), BF16),
        e2b=((ti, di), BF16),
        tdg=((8, dt), F32),
        idg=((8, di), F32),
    )
    scratch.update(
        **more,
        wa=(text_qkv.shape, BF16),
        wb=(image_qkv.shape, BF16),
        acc_t=((tt, dt), F32),
        acc_i=((ti, di), F32),
    )
    b2 = kernel_call(
        "qkv_back",
        qkv_back_body,
        scal,
        dict(
            **ins,
            qkv_t=(text_qkv, "h"),
            qkv_i=(image_qkv, "h"),
            dsqkv=(b1.o_dsqkv, "v"),
            duqkv=(b1.o_duqkv, "v"),
            d3=(b1.o_d3, "v"),
            e3=(b1.o_e3, "v"),
            **gains,
        ),
        outs,
        scratch,
    )
    group_1.got, d2, e2, d2b, e2b = tie(group_1.got, b2.o_d2, b2.o_e2, b2.o_d2b, b2.o_e2b)
    group_1.add()
    group_1.cross()

    ins, scratch = sources(
        down_i=image_down,
        isl=f1.o_isl,
        up_i=image_up,
        down_t=text_down,
        tsl=f1.o_tsl,
        up_t=text_up,
        ia=f1.o_ia,
        i1=f1.o_i1,
        ta=f1.o_ta,
        t1=f1.o_t1,
        d2b=d2b,
        e2b=e2b,
    )
    ins.update(h_d2=(d2, "h"), h_e2=(e2, "h"))
    outs, more = packed(group_2)
    scratch.update(x1=((tt, dt), F32), y1=((ti, di), F32))
    scratch.update(**more, dht=((tt, ft), BF16), dhi=((ti, fi), BF16))
    b3 = kernel_call(
        "ffn_back",
        functools.partial(ffn_back_body, plan=group_2.members, ndp=comm.ndp),
        scal,
        ins,
        dict(**outs, o_x1=((tt, dt), F32, "h"), o_y1=((ti, di), F32, "h")),
        scratch,
    )
    group_1.parts, x1, y1, keep, send = tie(
        group_1.parts, b3.o_x1, b3.o_y1, b3.o_keep, b3.o_send
    )
    group_2.swap(keep, send)
    group_1.along()

    ins, scratch = sources(
        x1=x1, y1=y1, tn1=f1.o_tn1, tr1=f1.o_tr1, out_t=text_co_out, in1=f1.o_in1, ir1=f1.o_ir1, out_i=image_co_out
    )
    outs, more = saved(
        d1b=((tt, dt), BF16),
        e1b=((ti, di), BF16),
        dat=((tt, dc), BF16),
        dai=((ti, dc), BF16),
        own_t=((rows, nt, dt), F32),
        own_i=((rows, ni, di), F32),
        tdg=((8, dt), F32),
        idg=((8, di), F32),
    )
    scratch.update(**more, d1=((tt, dt), F32), e1=((ti, di), F32))
    b4 = kernel_call(
        "first_norm_back",
        functools.partial(first_norm_back_body, rows=rows, count_t=nt, count_i=ni),
        scal,
        dict(**ins, **gains),
        outs,
        scratch,
    )
    group_2.got, dat, dai = tie(group_2.got, b4.o_dat, b4.o_dai)
    group_2.add()
    group_2.cross()

    ins, scratch = sources(
        tqkv=f1.o_tqkv,
        pt=f1.o_pt,
        iqkv=f1.o_iqkv,
        pi=f1.o_pi,
        tatt=f1.o_tatt,
        iatt=f1.o_iatt,
        tx=f1.o_tx,
        ix=f1.o_ix,
        dat=dat,
        dai=dai,
        d1b=b4.o_d1b,
        e1b=b4.o_e1b,
        tdg1=b4.o_tdg,
        tdg2=b2.o_tdg,
        tdg3=b1.o_tdg,
        idg1=b4.o_idg,
        idg2=b2.o_idg,
        idg3=b1.o_idg,
    )
    outs, more = packed(group_3)
    outs_last, more_last = packed(group_4, "_last")
    outs.update(outs_last)
    scratch.update(
        **more, **more_last, dt=((tt, 3 * dc), BF16), di=((ti, 3 * dc), BF16), gain_rows=((GAIN_ROWS, TILE), F32)
    )
    b5 = kernel_call(
        "co_back",
        functools.partial(
            co_back_body,
            rows=rows,
            parts=n,
            count_t=nt,
            count_i=ni,
            plan=group_3.members,
            last_plan=group_4.members[0],
            ndp=comm.ndp,
            gains_at=group_4.gains_at,
        ),
        scal,
        ins,
        dict(
            **outs,
            o_dt=((rows, nt, 3 * dc), BF16, "v"),
            o_di=((rows, ni, 3 * dc), BF16, "v"),
        ),
        scratch,
    )
    (
        group_1.everyone[1],
        group_1.everyone[2],
        group_2.parts,
        dt_own,
        di_own,
        keep,
        send,
        keep_last,
        send_last,
    ) = tie(
        group_1.everyone[1],
        group_1.everyone[2],
        group_2.parts,
        b5.o_dt,
        b5.o_di,
        b5.o_keep,
        b5.o_send,
        b5.o_keep_last,
        b5.o_send_last,
    )
    group_3.swap(keep, send)
    group_4.swap(keep_last, send_last)
    group_2.along()
    b6 = kernel_call(
        "in_back",
        in_back_body,
        scal,
        dict(
            co_t=(text_co_in, "h"),
            co_i=(image_co_in, "h"),
            dt=(dt_own, "v"),
            di=(di_own, "v"),
            h_d1=(b4.o_own_t, "h"),
            h_e1=(b4.o_own_i, "h"),
        ),
        dict(o_dt=((rows, nt, dt), F32, "v"), o_di=((rows, ni, di), F32, "v")),
        dict(
            wa=(text_co_in.shape, BF16),
            wb=(image_co_in.shape, BF16),
            d1=((rows, nt, dt), F32),
            e1=((rows, ni, di), F32),
        ),
    )
    group_1.everyone[3], group_3.got, group_4.got, text_in_grad, image_in_grad = tie(
        group_1.everyone[3], group_3.got, group_4.got, b6.o_dt, b6.o_di
    )
    group_3.add()
    group_3.cross()
    group_4.add()
    group_2.everyone[1], group_2.everyone[2], group_3.parts, group_4.pair = tie(
        group_2.everyone[1], group_2.everyone[2], group_3.parts, group_4.pair
    )
    group_4.cross()
    group_3.along()
    text_proj_grad, image_proj_grad, text_qkv_grad, image_qkv_grad = group_1.unpack()
    text_down_grad, image_down_grad, text_up_grad, image_up_grad = group_2.unpack()
    group_4.along()
    text_co_in_grad, text_gains_grad, image_gains_grad = group_4.unpack()
    *group_3.everyone, text_co_in_grad, text_gains_grad, image_gains_grad = tie(
        *group_3.everyone, text_co_in_grad, text_gains_grad, image_gains_grad
    )
    image_co_out_grad, image_co_in_grad, text_co_out_grad = group_3.unpack()
    return (
        f2.o_tres,
        f2.o_ires,
        text_in_grad,
        image_in_grad,
        text_co_in_grad,
        image_co_in_grad,
        text_co_out_grad,
        image_co_out_grad,
        text_up_grad,
        text_down_grad,
        image_up_grad,
        image_down_grad,
        text_qkv_grad,
        text_proj_grad,
        image_qkv_grad,
        image_proj_grad,
        text_gains_grad,
        image_gains_grad,
    )


def solution(mesh):
    slots = P("dp", "seq", None)
    rows = P("dp", None)
    return jax.shard_map(
        per_device,
        mesh=mesh,
        in_specs=(slots, slots, rows, rows) + (P(),) * 14 + (slots, slots),
        out_specs=(slots,) * 4 + (rows,) * 12 + (P(), P()),
        check_vma=False,
    )
```

```python
import functools
import types

import jax
import jax.numpy as jnp
from jax import lax
from jax.experimental import pallas as pl
from jax.experimental.pallas import tpu as pltpu
from jax.sharding import PartitionSpec as P

HT = 12
HI = 8
HC = 8

NORM_EPS = 1e-05

F32 = jnp.float32
BF16 = jnp.bfloat16
LOG2E = 1.4426950408889634
MASKED = -1.0e9 * LOG2E
SQRT_2_PI = 0.7978845608028654
GELU_CUBE = 0.044715
LANES = 128
TILE = 256
WIDE = 1536
GAIN_ROWS = 32
MIB = 1024 * 1024


def dot_nt(a, b):
    return lax.dot_general(a, b, (((1,), (1,)), ((), ())), preferred_element_type=F32)


def dot_nn(a, b):
    return lax.dot_general(a, b, (((1,), (0,)), ((), ())), preferred_element_type=F32)


def dot_tn(a, b):
    return lax.dot_general(a, b, (((0,), (0,)), ((), ())), preferred_element_type=F32)


class Copies:
    def __init__(self, sems):
        self.sems, self.used, self.leaving = sems, 0, []

    def fetch(self, src, dst):
        copy = pltpu.make_async_copy(src, dst, self.sems.at[self.used])
        self.used += 1
        copy.start()
        return copy

    def flush(self, src, dst):
        self.leaving.append(self.fetch(src, dst))

    def finish(self):
        for copy in self.leaving:
            copy.wait()


def nbytes(shape, dtype):
    total = jnp.dtype(dtype).itemsize
    dims = list(shape)
    dims[-1] = -(-dims[-1] // 128) * 128
    if len(dims) > 1:
        dims[-2] = -(-dims[-2] // 16) * 16
    for d in dims:
        total *= d
    return total


def kernel_call(name, body, scal, ins, outs, scratch, copies=64, extra=8):
    names = list(ins) + list(outs) + list(scratch)

    def kernel(scal_ref, *refs):
        k = types.SimpleNamespace(**dict(zip(names, refs)))
        moves = Copies(refs[-1])
        body(scal_ref, k, moves)
        moves.finish()

    def place(where):
        return pl.BlockSpec(memory_space=pltpu.HBM if where == "h" else pltpu.VMEM)

    def shape_of(shape, dtype, where):
        return pltpu.HBM(tuple(shape), dtype) if where == "h" else jax.ShapeDtypeStruct(shape, dtype)

    args = [
        pltpu.with_memory_space_constraint(x, pltpu.HBM) if where == "h" else x for x, where in ins.values()
    ]
    total = sum(nbytes(s, d) for s, d in scratch.values()) + extra * MIB
    got = pl.pallas_call(
        kernel,
        in_specs=[pl.BlockSpec(memory_space=pltpu.SMEM)] + [place(w) for _, w in ins.values()],
        out_specs=[place(w) for _, _, w in outs.values()],
        out_shape=[shape_of(*o) for o in outs.values()],
        scratch_shapes=[pltpu.VMEM(tuple(s), d) for s, d in scratch.values()]
        + [pltpu.SemaphoreType.DMA((copies,))],
        compiler_params=pltpu.CompilerParams(vmem_limit_bytes=total),
        name=name,
    )(scal, *args)
    return types.SimpleNamespace(**dict(zip(outs, got)))


def loop(count, body, unroll=1):
    def step(i, carry):
        body(i)
        return carry

    lax.fori_loop(0, count, step, 0, unroll=unroll)


def at(i, size):
    return pl.ds(pl.multiple_of(i * size, size), size)


def row_chunks(rows, body):
    size = next(c for c in (128, 80, 64, 32, 16) if rows % c == 0)
    loop(rows // size, lambda i: body(at(i, size)))


def tile_of(width, limit):
    parts = -(-width // limit)
    while width % (parts * TILE):
        parts += 1
    return width // parts


def pick(i, values):
    out = values[0]
    for k in range(1, len(values)):
        out = jnp.where(i == k, values[k], out)
    return out


def lane_halves(width):
    if width == LANES:
        return [None]
    lane = lax.broadcasted_iota(jnp.int32, (1, LANES), 1)
    return [(lane // width) == i for i in range(LANES // width)]


def keep_lanes(x, sel):
    return x if sel is None else jnp.where(sel, x, jnp.zeros_like(x))


def cols(ref, rows, tile):
    return ref[rows, tile * LANES : (tile + 1) * LANES]


def store_bias(bias_ref, down_ref, along_ref):
    for r in range(bias_ref.shape[0]):
        row = down_ref[r : r + 1].astype(F32)
        col = jnp.transpose(jnp.broadcast_to(row, (8, row.shape[1])))[:, :1]
        bias_ref[r] = jnp.where(col == along_ref[r : r + 1].astype(F32), 0.0, MASKED).astype(F32)


def attend(r, q_ref, kv_ref, bias, o_ref, p_ref, lq, lk, width):
    scale = width**-0.5 * LOG2E
    sels = lane_halves(width)
    n = o_ref.shape[1] // LANES
    qs, ks = at(r, lq), at(r, lk)
    for t in range(n):
        q, k, v = cols(q_ref, qs, t), cols(kv_ref, ks, n + t), cols(kv_ref, ks, 2 * n + t)
        out = None
        for i, sel in enumerate(sels):
            s = dot_nt(k, keep_lanes(q, sel)) * scale + bias
            e = jnp.exp2(s - jnp.max(s, axis=0, keepdims=True))
            p = (e * (1.0 / jnp.sum(e, axis=0, keepdims=True))).astype(BF16)
            p_ref[r, t * len(sels) + i] = p
            o = dot_tn(p, v)
            out = o if out is None else jnp.where(sel, o, out)
        o_ref[qs, t * LANES : (t + 1) * LANES] = out.astype(BF16)


def attend_wide(r, q_ref, kv_ref, bias, o_ref, p_ref, lq, lk):
    scale = LANES**-0.5 * LOG2E
    n = o_ref.shape[1] // LANES
    qs, ks = at(r, lq), at(r, lk)
    for t in range(n):
        q, k, v = cols(q_ref, qs, t), cols(kv_ref, ks, n + t), cols(kv_ref, ks, 2 * n + t)
        s = dot_nt(q, k) * scale + bias
        e = jnp.exp2(s - jnp.max(s, axis=1, keepdims=True))
        p = (e * (1.0 / jnp.sum(e, axis=1, keepdims=True))).astype(BF16)
        p_ref[r, t] = p
        o_ref[qs, t * LANES : (t + 1) * LANES] = dot_nn(p, v).astype(BF16)


def attend_wide_back(r, q_ref, kv_ref, da_ref, p_ref, dq_ref, dkv_ref, lq, lk):
    scale = LANES**-0.5
    n = da_ref.shape[1] // LANES
    qs, ks = at(r, lq), at(r, lk)
    for t in range(n):
        q, k, v = cols(q_ref, qs, t), cols(kv_ref, ks, n + t), cols(kv_ref, ks, 2 * n + t)
        da = cols(da_ref, qs, t)
        p = p_ref[r, t]
        pf = p.astype(F32)
        w = pf * dot_nt(da, v)
        ds = (w - pf * jnp.sum(w, axis=1, keepdims=True)).astype(BF16)
        dq_ref[qs, t * LANES : (t + 1) * LANES] = (dot_nn(ds, k) * scale).astype(BF16)
        dkv_ref[ks, (n + t) * LANES : (n + t + 1) * LANES] = (dot_tn(ds, q) * scale).astype(BF16)
        dkv_ref[ks, (2 * n + t) * LANES : (2 * n + t + 1) * LANES] = dot_tn(p, da).astype(BF16)


def attend_back(r, q_ref, kv_ref, da_ref, p_ref, dq_ref, dkv_ref, lq, lk, width):
    scale = width**-0.5
    sels = lane_halves(width)
    n = da_ref.shape[1] // LANES
    qs, ks = at(r, lq), at(r, lk)
    for t in range(n):
        q, k, v = cols(q_ref, qs, t), cols(kv_ref, ks, n + t), cols(kv_ref, ks, 2 * n + t)
        da = cols(da_ref, qs, t)
        dq = dk = dv = None
        for i, sel in enumerate(sels):
            p = p_ref[r, t * len(sels) + i]
            da_h = keep_lanes(da, sel)
            pf = p.astype(F32)
            w = pf * dot_nt(v, da_h)
            ds = (w - pf * jnp.sum(w, axis=0, keepdims=True)).astype(BF16)
            dv_h = dot_nn(p, da_h)
            dk_h = dot_nn(ds, keep_lanes(q, sel))
            dq_h = dot_tn(ds, keep_lanes(k, sel))
            dq = dq_h if dq is None else dq + dq_h
            dk = dk_h if dk is None else dk + dk_h
            dv = dv_h if dv is None else dv + dv_h
        dq_ref[qs, t * LANES : (t + 1) * LANES] = (dq * scale).astype(BF16)
        dkv_ref[ks, (n + t) * LANES : (n + t + 1) * LANES] = (dk * scale).astype(BF16)
        dkv_ref[ks, (2 * n + t) * LANES : (2 * n + t + 1) * LANES] = dv.astype(BF16)


def normalize(z):
    center = z - jnp.mean(z, axis=-1, keepdims=True)
    inv = lax.rsqrt(jnp.mean(center * center, axis=-1, keepdims=True) + NORM_EPS)
    return center * inv, inv


def fold_rows(x):
    return jnp.sum(x.reshape(x.shape[0] // 8, 8, x.shape[1]), axis=0)


def matmul_tiles(x_ref, w_ref, o_ref):
    n = o_ref.shape[1]
    tile = tile_of(n, WIDE)

    def step(i):
        o_ref[:, at(i, tile)] = dot_nn(x_ref[...], w_ref[:, at(i, tile)]).astype(o_ref.dtype)

    loop(n // tile, step)


def norm_rows(acc_ref, res, gain, n_ref, inv_ref, low_ref=None):
    def chunk(rows):
        n, inv = normalize(acc_ref[rows] + res(rows))
        n_ref[rows] = n
        inv_ref[rows] = jnp.broadcast_to(inv, (inv.shape[0], LANES))
        if low_ref is not None:
            low_ref[rows] = (n * gain).astype(BF16)

    row_chunks(acc_ref.shape[0], chunk)


def norm_back_rows(dy_of, n_ref, inv_ref, gain, d_ref, low_ref, dg_ref):
    dg_ref[...] = jnp.zeros_like(dg_ref)

    def chunk(rows):
        dy = dy_of(rows)
        n = n_ref[rows]
        dn = dy * gain
        m1 = jnp.mean(dn, axis=-1, keepdims=True)
        m2 = jnp.mean(dn * n, axis=-1, keepdims=True)
        d = inv_ref[rows][:, :1] * (dn - m1 - n * m2)
        d_ref[rows] = d
        low_ref[rows] = d.astype(BF16)
        dg_ref[...] += fold_rows(dy * n)

    row_chunks(n_ref.shape[0], chunk)


def gelu_pair(v):
    v2 = v * v
    s = 0.5 + 0.5 * jnp.tanh(v * (SQRT_2_PI + (SQRT_2_PI * GELU_CUBE) * v2))
    a = v * s
    return a, s + a * (1.0 - s) * (2.0 * SQRT_2_PI + (6.0 * SQRT_2_PI * GELU_CUBE) * v2)


def ffn_tiles(x_ref, up_ref, down_ref, a_ref, slope_ref, acc_ref):
    width = tile_of(a_ref.shape[1], WIDE)

    def step(i):
        tile = at(i, width)
        a, slope = gelu_pair(dot_nn(x_ref[...], up_ref[:, tile]))
        a = a.astype(BF16)
        a_ref[:, tile] = a
        slope_ref[:, tile] = slope.astype(BF16)
        acc_ref[...] += dot_nn(a, down_ref[tile])

    acc_ref[...] = jnp.zeros_like(acc_ref)
    loop(a_ref.shape[1] // width, step)


def ffn_back_tiles(low_ref, down_ref, slope_ref, up_ref, dh_ref, acc_ref):
    width = tile_of(dh_ref.shape[1], WIDE)

    def step(i):
        tile = at(i, width)
        dh = (dot_nt(low_ref[...], down_ref[tile]) * slope_ref[:, tile].astype(F32)).astype(BF16)
        dh_ref[:, tile] = dh
        acc_ref[...] += dot_nt(dh, up_ref[:, tile])

    loop(dh_ref.shape[1] // width, step)


def send_packed(cp, keep, send, far_keep, far_send, first, last):
    for near, far in ((send, far_send), (keep, far_keep)):
        cp.flush(near.at[:, first:last], far.at[:, first:last])


def wgrad_group(scal, cp, xs, ys, plan, ndp, keep, send, far_keep, far_send):
    by_member = all(off % 16 == 0 and (tiles * rows) % 16 == 0 for tiles, _, _, off, rows in plan)
    for x, y, p in zip(xs, ys, plan):
        wgrad_member(scal, x, y, keep, send, p, ndp)
        if by_member:
            send_packed(cp, keep, send, far_keep, far_send, p[3], p[3] + p[0] * p[4])
    if not by_member:
        send_packed(cp, keep, send, far_keep, far_send, 0, keep.shape[1])


def wgrad_member(scal_ref, x_ref, y_ref, keep_ref, send_ref, plan, ndp):
    tiles, total, split, off, rows = plan
    odd = scal_ref[0] == 1
    xt = jnp.transpose(x_ref[...])
    first = jnp.minimum(scal_ref[1] * tiles, total - tiles) if split else 0
    for t in range(tiles):
        g = dot_nn(xt, y_ref[:, at(first + t, TILE)]).astype(BF16)
        base = off + t * rows
        for j in range(ndp // 2):
            even_rows = g[2 * j * rows : (2 * j + 1) * rows]
            odd_rows = g[(2 * j + 1) * rows : (2 * j + 2) * rows]
            keep_ref[j, base : base + rows] = jnp.where(odd, odd_rows, even_rows)
            send_ref[j, base : base + rows] = jnp.where(odd, even_rows, odd_rows)


def pack_gains(gain_refs, rows_ref, keep_ref, send_ref, base):
    row = 0
    for ref in gain_refs:
        total = jnp.sum(ref[...], axis=0, keepdims=True)
        for c in range(0, ref.shape[1], TILE):
            rows_ref[row : row + 1] = total[:, c : c + TILE]
            row += 1
    for row in range(row, GAIN_ROWS):
        rows_ref[row : row + 1] = jnp.zeros((1, TILE), F32)
    low = rows_ref[...].astype(BF16)
    for j in range(keep_ref.shape[0]):
        keep_ref[j, base : base + GAIN_ROWS] = low
        send_ref[j, base : base + GAIN_ROWS] = low


def co_stage_body(scal, k, cp, *, rows, parts, count_t, count_i):
    pieces = [cp.fetch(getattr(k, f"part{i}"), k.staged.at[i]) for i in range(parts)]
    wa = cp.fetch(k.co_t, k.wa)
    wb = cp.fetch(k.co_i, k.wb)
    wo = cp.fetch(k.out_t, k.wo)
    wd = cp.fetch(k.down_t, k.wd)
    lt, li = parts * count_t, parts * count_i
    store_bias(k.bias, k.iseg, k.tseg)
    for piece in pieces:
        piece.wait()
    base = join_tiles(scal[1], k.staged, k.tx, count_t, rows, 0)
    wa.wait()
    matmul_tiles(k.tx, k.wa, k.tqkv)
    up_t = cp.fetch(k.up_t, k.wa)
    cp.flush(k.tx, k.o_tx)
    cp.flush(k.tqkv, k.o_tqkv)
    join_tiles(scal[1], k.staged, k.ix, count_i, rows, base)
    wb.wait()
    matmul_tiles(k.ix, k.wb, k.iqkv)
    wi = k.ix.shape[1]
    up_i = cp.fetch(k.up_i, k.wb.at[:, 0:wi])
    down_i = cp.fetch(k.down_i, k.wb.at[:, wi : 2 * wi])
    out_i = cp.fetch(k.out_i, k.wb.at[:, 2 * wi : 3 * wi])
    cp.flush(k.ix, k.o_ix)
    cp.flush(k.iqkv, k.o_iqkv)
    assert k.tatt.shape[1] == HC * LANES

    def heads(r):
        attend(r, k.tqkv, k.iqkv, k.bias[r], k.tatt, k.pt, lt, li, LANES)
        attend_wide(r, k.iqkv, k.tqkv, k.bias[r], k.iatt, k.pi, li, lt)

    loop(rows, heads)
    cp.flush(k.tatt, k.o_tatt)
    cp.flush(k.iatt, k.o_iatt)
    cp.flush(k.pt, k.o_pt)
    cp.flush(k.pi, k.o_pi)
    out_i.wait()
    matmul_tiles(k.iatt, k.wb.at[:, 2 * wi : 3 * wi], k.acc_i)
    ig = k.ig[...]
    norm_rows(k.acc_i, lambda r: k.ix[r].astype(F32), ig[0:1], k.in1, k.ir1, k.i1)
    up_i.wait()
    down_i.wait()
    ffn_tiles(k.i1, k.wb.at[:, 0:wi], k.wb.at[:, wi : 2 * wi], k.ia, k.isl, k.acc_i)
    norm_rows(k.acc_i, lambda r: k.in1[r] * ig[0:1], ig[1:2], k.in2, k.ir2, k.i2)
    for name in ("in1", "ir1", "i1", "ia", "isl", "in2", "ir2", "i2"):
        cp.flush(getattr(k, name), getattr(k, "o_" + name))
    wo.wait()
    matmul_tiles(k.tatt, k.wo, k.acc_t)
    tg = k.tg[...]
    norm_rows(k.acc_t, lambda r: k.tx[r].astype(F32), tg[0:1], k.tn1, k.tr1, k.t1)
    up_t.wait()
    wd.wait()
    for name in ("tn1", "tr1", "t1"):
        cp.flush(getattr(k, name), getattr(k, "o_" + name))
    ffn_tiles(k.t1, k.wa, k.wd, k.ta, k.tsl, k.acc_t)
    cp.flush(k.ta, k.o_ta)
    cp.flush(k.tsl, k.o_tsl)
    norm_rows(k.acc_t, lambda r: k.tn1[r] * tg[0:1], tg[1:2], k.tn2, k.tr2, k.t2)
    for name in ("t2", "tn2", "tr2"):
        cp.flush(getattr(k, name), getattr(k, "o_" + name))


def self_stage_body(scal, k, cp, *, rows, count_t, count_i):
    t2 = cp.fetch(k.h_t2, k.t2)
    wa = cp.fetch(k.qkv_t, k.wa)
    i2 = cp.fetch(k.h_i2, k.i2)
    wb = cp.fetch(k.qkv_i, k.wb)
    pa = cp.fetch(k.proj_t, k.pa)
    pb = cp.fetch(k.proj_i, k.pb)
    tn2 = cp.fetch(k.h_tn2, k.tn2)
    in2 = cp.fetch(k.h_in2, k.in2)
    store_bias(k.tbias, k.tseg, k.tseg)
    store_bias(k.ibias, k.iseg, k.iseg)
    lt = k.t2.shape[0] // rows
    li = k.i2.shape[0] // rows
    t2.wait()
    wa.wait()
    matmul_tiles(k.t2, k.wa, k.sqkv)
    cp.flush(k.sqkv, k.o_sqkv)
    i2.wait()
    wb.wait()
    matmul_tiles(k.i2, k.wb, k.uqkv)
    cp.flush(k.uqkv, k.o_uqkv)
    wt = k.tmix.shape[1] // HT
    wi = k.imix.shape[1] // HI

    def heads(r):
        attend(r, k.sqkv, k.sqkv, k.tbias[r], k.tmix, k.spt, lt, lt, wt)
        attend(r, k.uqkv, k.uqkv, k.ibias[r], k.imix, k.spi, li, li, wi)

    loop(rows, heads)
    for name in ("tmix", "imix", "spt", "spi"):
        cp.flush(getattr(k, name), getattr(k, "o_" + name))
    tn2.wait()
    in2.wait()
    z = scal[1]
    for mix, w, ready, acc, n2, g, n3, r3, res, count in (
        (k.tmix, k.pa, pa, k.acc_t, k.tn2, k.tg, k.tn3, k.tr3, k.tres, count_t),
        (k.imix, k.pb, pb, k.acc_i, k.in2, k.ig, k.in3, k.ir3, k.ires, count_i),
    ):
        ready.wait()
        matmul_tiles(mix, w, acc)
        gain = g[...]
        norm_rows(acc, lambda r, n2=n2, gain=gain: n2[r] * gain[1:2], None, n3, r3)
        length = mix.shape[0] // rows
        for r in range(rows):
            own = n3[pl.ds(pl.multiple_of(r * length + z * count, 8), count)]
            res[r] = (own * gain[2:3]).astype(BF16)
        for name in ("tn3", "tr3", "tres") if mix is k.tmix else ("in3", "ir3", "ires"):
            cp.flush(getattr(k, name), getattr(k, "o_" + name))


def self_back_body(scal, k, cp, *, rows, count_t, count_i, plan, ndp):
    ups = [cp.fetch(getattr(k, f"h_up{i}"), k.up.at[i]) for i in range(k.up.shape[0])]
    names = ("tn3", "tr3", "proj_t", "in3", "ir3", "proj_i", "sqkv", "spt", "uqkv", "spi")
    names += ("tmix", "t2", "i2")
    moves = {n: cp.fetch(getattr(k, "h_" + n), getattr(k, n)) for n in names}

    def ready(*which):
        for n in which:
            moves[n].wait()

    for copy in ups:
        copy.wait()
    base = join_tiles(scal[1], k.up, k.tup, count_t, rows, 0)
    join_tiles(scal[1], k.up, k.iup, count_i, rows, base)
    ready("tn3", "tr3", "proj_t")
    norm_back_rows(
        lambda r: k.tup[r].astype(F32), k.tn3, k.tr3, k.tg[2:3], k.o_d3, k.d3b, k.tdg
    )
    k.dmt[...] = dot_nt(k.d3b[...], k.proj_t[...]).astype(BF16)
    ready("in3", "ir3", "proj_i")
    norm_back_rows(
        lambda r: k.iup[r].astype(F32), k.in3, k.ir3, k.ig[2:3], k.o_e3, k.e3b, k.idg
    )
    k.dmi[...] = dot_nt(k.e3b[...], k.proj_i[...]).astype(BF16)
    ready("sqkv", "spt", "uqkv", "spi")
    lt, li = k.tup.shape[0] // rows, k.iup.shape[0] // rows
    wt = k.dmt.shape[1] // HT
    wi = k.dmi.shape[1] // HI

    def heads(r):
        attend_back(r, k.sqkv, k.sqkv, k.dmt, k.spt, k.o_dsqkv, k.o_dsqkv, lt, lt, wt)
        attend_back(r, k.uqkv, k.uqkv, k.dmi, k.spi, k.o_duqkv, k.o_duqkv, li, li, wi)

    loop(rows, heads)
    ready("tmix", "t2", "i2")
    xs, ys = (k.tmix, k.t2, k.i2), (k.d3b, k.o_dsqkv, k.o_duqkv)
    cp.flush(k.e3b, k.o_e3b)
    wgrad_group(scal, cp, xs, ys, plan, ndp, k.keep, k.send, k.o_keep, k.o_send)
    for name in ("tdg", "idg"):
        cp.flush(getattr(k, name), getattr(k, "o_" + name))


def chunked(cp, src, dst, axis, count=3):
    size = src.shape[axis] // count
    out = []
    for i in range(count):
        part = slice(i * size, (i + 1) * size)
        part = (slice(None), part) if axis == 1 else (part, slice(None))
        out.append((cp.fetch(src.at[part], dst.at[part]), part))
    return out


def qkv_back_body(scal, k, cp):
    wa = chunked(cp, k.qkv_t, k.wa, 0, 2)
    extra_t = [cp.fetch(k.h_tn2, k.tn2), cp.fetch(k.h_tr2, k.tr2)]
    wb = chunked(cp, k.qkv_i, k.wb, 0, 2)
    extra_i = [cp.fetch(k.h_in2, k.in2), cp.fetch(k.h_ir2, k.ir2)]
    for dx, w, ready, extra, acc, d3, n, inv, g, outs in (
        (k.dsqkv, k.wa, wa, extra_t, k.acc_t, k.d3, k.tn2, k.tr2, k.tg, ("d2", "d2b", "tdg")),
        (k.duqkv, k.wb, wb, extra_i, k.acc_i, k.e3, k.in2, k.ir2, k.ig, ("e2", "e2b", "idg")),
    ):
        for copy, (part, _) in ready:
            copy.wait()
            acc[:, part] = dot_nt(dx[...], w[part])
        for copy in extra:
            copy.wait()
        d2, low, dg = (getattr(k, name) for name in outs)
        norm_back_rows(lambda r, acc=acc, d3=d3: d3[r] + acc[r], n, inv, g[1:2], d2, low, dg)
        for name in outs:
            cp.flush(getattr(k, name), getattr(k, "o_" + name))


def ffn_back_body(scal, k, cp, *, plan, ndp):
    def start(*names):
        return [cp.fetch(getattr(k, "h_" + n), getattr(k, n)) for n in names]

    moves = start("e2b", "down_i", "isl", "up_i")
    y1 = cp.fetch(k.h_e2, k.y1)
    later = start("d2b", "down_t", "tsl", "up_t")
    x1 = cp.fetch(k.h_d2, k.x1)
    last = start("ta", "ia", "t1", "i1", "imix", "e3b")
    for copy in (*moves, y1):
        copy.wait()
    ffn_back_tiles(k.e2b, k.down_i, k.isl, k.up_i, k.dhi, k.y1)
    cp.flush(k.y1, k.o_y1)
    for copy in (*later, x1):
        copy.wait()
    ffn_back_tiles(k.d2b, k.down_t, k.tsl, k.up_t, k.dht, k.x1)
    cp.flush(k.x1, k.o_x1)
    for copy in last:
        copy.wait()
    xs, ys = (k.ta, k.ia, k.t1, k.i1, k.imix), (k.d2b, k.e2b, k.dht, k.dhi, k.e3b)
    wgrad_group(scal, cp, xs, ys, plan, ndp, k.keep, k.send, k.o_keep, k.o_send)


def first_norm_back_body(scal, k, cp, *, rows, count_t, count_i):
    moves_t = [cp.fetch(getattr(k, "h_" + n), getattr(k, n)) for n in ("x1", "tn1", "tr1", "out_t")]
    moves_i = [cp.fetch(getattr(k, "h_" + n), getattr(k, n)) for n in ("y1", "in1", "ir1", "out_i")]
    z = scal[1]
    for moves, x1, n, inv, g, d1, low, dg, w, da, own, count in (
        (moves_t, k.x1, k.tn1, k.tr1, k.tg, k.d1, k.d1b, k.tdg, k.out_t, k.dat, k.own_t, count_t),
        (moves_i, k.y1, k.in1, k.ir1, k.ig, k.e1, k.e1b, k.idg, k.out_i, k.dai, k.own_i, count_i),
    ):
        for copy in moves:
            copy.wait()
        norm_back_rows(lambda r, x1=x1: x1[r], n, inv, g[0:1], d1, low, dg)
        da[...] = dot_nt(low[...], w[...]).astype(BF16)
        length = x1.shape[0] // rows
        for r in range(rows):
            own[r] = d1[pl.ds(pl.multiple_of(r * length + z * count, 8), count)]
    for name in ("dat", "dai", "d1b", "e1b", "own_t", "own_i", "tdg", "idg"):
        cp.flush(getattr(k, name), getattr(k, "o_" + name))


def co_back_body(scal, k, cp, *, rows, parts, count_t, count_i, plan, last_plan, ndp, gains_at):
    names = ("tqkv", "pt", "dat", "iqkv", "pi", "dai", "iatt", "e1b", "tatt", "d1b", "ix", "tx")
    names += ("tdg1", "tdg2", "tdg3", "idg1", "idg2", "idg3")
    lt, li = parts * count_t, parts * count_i
    first = cp.used
    cp.used += 6 * rows

    def row_copies(r):
        out = []
        for i, name in enumerate(names[:6]):
            far, near = getattr(k, "h_" + name), getattr(k, name)
            part = r if name in ("pt", "pi") else at(r, near.shape[0] // rows)
            out.append(pltpu.make_async_copy(far.at[part], near.at[part], cp.sems.at[first + 6 * r + i]))
        return out

    for r in range(rows):
        for copy in row_copies(r):
            copy.start()
    moves = [cp.fetch(getattr(k, "h_" + n), getattr(k, n)) for n in names[6:]]

    def heads(r):
        for copy in row_copies(r):
            copy.wait()
        attend_back(r, k.tqkv, k.iqkv, k.dat, k.pt, k.dt, k.di, lt, li, LANES)
        attend_wide_back(r, k.iqkv, k.tqkv, k.dai, k.pi, k.di, k.dt, li, lt)

    loop(rows, heads)
    for copy in moves:
        copy.wait()
    xs, ys = (k.iatt, k.ix, k.tatt), (k.e1b, k.di, k.d1b)
    wgrad_group(scal, cp, xs, ys, plan, ndp, k.keep, k.send, k.o_keep, k.o_send)
    gains = (k.tdg1, k.tdg2, k.tdg3, k.idg1, k.idg2, k.idg3)
    pack_gains(gains, k.gain_rows, k.keep_last, k.send_last, gains_at)
    wgrad_member(scal, k.tx, k.dt, k.keep_last, k.send_last, last_plan, ndp)
    cp.flush(k.send_last, k.o_send_last)
    cp.flush(k.keep_last, k.o_keep_last)
    z = scal[1]
    for full, own, count in ((k.dt, k.o_dt, count_t), (k.di, k.o_di, count_i)):
        for r in range(rows):
            values = [
                full[(r * parts + i) * count : (r * parts + i + 1) * count] for i in range(parts)
            ]
            own[r] = pick(z, values)


def in_back_body(scal, k, cp):
    own_t = cp.fetch(k.h_d1, k.d1)
    own_i = cp.fetch(k.h_e1, k.e1)
    wa = chunked(cp, k.co_t, k.wa, 1)
    wb = chunked(cp, k.co_i, k.wb, 1)
    for dx, w, chunks, d1, out, own in (
        (k.dt, k.wa, wa, k.d1, k.gt, own_t),
        (k.di, k.wb, wb, k.e1, k.gi, own_i),
    ):
        own.wait()
        r, count, m = dx.shape
        flat = dx[...].reshape(r * count, m)
        total = d1[...].reshape(r * count, d1.shape[2])
        for copy, part in chunks:
            copy.wait()
            total = total + dot_nt(flat[part], w[part])
        out[...] = total.reshape(out.shape)
        cp.flush(out, k.o_dt if out is k.gt else k.o_di)


def pack_body(scal, k, cp, *, count):
    names = [f"{stream}{i}" for i in range(count) for stream in "ti"]
    moves = {name: cp.fetch(getattr(k, "h_" + name), getattr(k, name)) for name in names}
    for i in range(count):
        packed = getattr(k, f"s{i}")
        base = 0
        for name in (f"t{i}", f"i{i}"):
            moves[name].wait()
            ref = getattr(k, name)
            for c in range(0, ref.shape[2], TILE):
                for r in range(ref.shape[0]):
                    part = ref[r, :, c : c + TILE]
                    packed[base : base + part.shape[0]] = part
                    base += part.shape[0]
        cp.flush(packed, getattr(k, f"o{i}"))


def join_tiles(z, staged, full, count, rows, base):
    parts = staged.shape[0]
    for c in range(0, full.shape[1], TILE):
        for r in range(rows):
            values = [staged[i, base : base + count] for i in range(parts)]
            for i in range(parts):
                to = (r * parts + i) * count
                full[to : to + count, c : c + TILE] = pick(z ^ i, values)
            base += count
    return base


def unpack_body(scal, k, cp, *, plan, nseq, gains_at, gain_shapes):
    z = scal[1]
    pieces = [cp.fetch(getattr(k, f"h{i}"), getattr(k, f"p{i}")) for i in range(nseq)]
    def own_rows(first, last):
        if not hasattr(k, "parts"):
            return k.own[first:last].astype(F32)
        return sum(k.parts[i, first:last].astype(F32) for i in range(k.parts.shape[0]))

    if hasattr(k, "own"):
        cp.fetch(k.h_own, k.own).wait()
    if gain_shapes:
        sums = own_rows(gains_at, gains_at + GAIN_ROWS)
        row = 0
        for i, (count, width) in enumerate(gain_shapes):
            out = getattr(k, f"o_gain{i}")
            for g in range(count):
                for c in range(0, width, TILE):
                    out[g : g + 1, c : c + TILE] = sums[row : row + 1]
                    row += 1
    for i, (tiles, total, split, off, rows) in enumerate(plan):
        if not split:
            buf = getattr(k, f"b{i}")
            for t in range(tiles):
                buf[:, t * TILE : (t + 1) * TILE] = own_rows(off + t * rows, off + (t + 1) * rows)
            cp.flush(buf, getattr(k, f"o{i}"))
    for piece in pieces:
        piece.wait()
    for i, (tiles, total, split, off, rows) in enumerate(plan):
        if split:
            buf = getattr(k, f"b{i}")
            for s in range(nseq):
                ref = getattr(k, f"p{s}")
                first = jnp.minimum((z ^ s) * tiles, total - tiles)
                for t in range(tiles):
                    buf[:, at(first + t, TILE)] = ref[off + t * rows : off + (t + 1) * rows].astype(F32)
            cp.flush(buf, getattr(k, f"o{i}"))


class Comm:
    def __init__(self):
        self.nseq = lax.axis_size("seq")
        self.ndp = lax.axis_size("dp")
        self.z = lax.axis_index("seq")
        self.d = lax.axis_index("dp")
        self.scal = jnp.stack([self.d % 2, self.z]).astype(jnp.int32)

    def pieces_at_once(self, x):
        n = self.nseq
        return [x] + [lax.ppermute(x, "seq", [(i, i ^ k) for i in range(n)]) for k in range(1, n)]

    def pieces(self, x):
        n = self.nseq
        got = [x]
        for k in range(1, n):
            step = k & -k
            got.append(lax.ppermute(got[k ^ step], "seq", [(i, i ^ step) for i in range(n)]))
        return got

    def pack(self, *pairs):
        ins, outs, scratch = {}, {}, {}
        for i, (text, image) in enumerate(pairs):
            total = sum(x.shape[0] * x.shape[1] * (x.shape[2] // TILE) for x in (text, image))
            ins.update({f"h_t{i}": (text, "h"), f"h_i{i}": (image, "h")})
            scratch.update({f"t{i}": (text.shape, BF16), f"i{i}": (image.shape, BF16)})
            outs[f"o{i}"] = ((total, TILE), BF16, "h")
            scratch[f"s{i}"] = ((total, TILE), BF16)
        got = kernel_call(
            "pack",
            functools.partial(pack_body, count=len(pairs)),
            self.scal,
            ins,
            outs,
            scratch,
            copies=3 * len(pairs),
            extra=2,
        )
        return [getattr(got, name) for name in outs]

    def plan_of(self, members):
        plan = {}
        off = 0
        for want in (True, False):
            for i, (din, dout, split) in enumerate(members):
                if split != want:
                    continue
                total = dout // TILE
                tiles = -(-total // self.nseq) if split else total
                rows = din // self.ndp
                plan[i] = (tiles, total, split, off, rows)
                off += tiles * rows
            if want:
                split_rows = off
        return Plan(self, [plan[i] for i in range(len(members))], split_rows, off)


class Plan:
    def __init__(self, comm, members, split_rows, rows, gain_shapes=()):
        self.comm, self.members, self.split_rows, self.rows = comm, members, split_rows, rows
        self.gain_shapes = gain_shapes
        self.gains_at = rows

    def with_gains(self, shapes):
        self.gain_shapes = shapes
        self.rows += GAIN_ROWS
        return self

    def half(self):
        return (self.comm.ndp // 2, self.rows, TILE)

    def swap(self, keep, send):
        self.keep = keep
        self.got = lax.ppermute(send, "dp", [(i, i ^ 1) for i in range(self.comm.ndp)])

    def add(self):
        self.pair = (self.keep.astype(F32) + self.got.astype(F32)).astype(BF16)

    def cross(self):
        groups = [list(range(b, self.comm.ndp, 2)) for b in range(2)]
        self.parts = lax.all_to_all(
            self.pair, "dp", split_axis=0, concat_axis=0, tiled=True, axis_index_groups=groups
        )

    def along(self):
        def total(part):
            return jnp.sum(part.astype(F32), axis=0).astype(BF16)

        self.everyone = []
        if self.split_rows:
            self.everyone = self.comm.pieces(total(self.parts[:, : self.split_rows]))
        self.own = None
        if self.split_rows and self.rows > self.split_rows:
            self.own = total(self.parts[:, self.split_rows :])

    def unpack(self):
        plan = [(p[0], p[1], p[2], p[3] if p[2] else p[3] - self.split_rows, p[4]) for p in self.members]
        ins = {f"h{i}": (x, "h") for i, x in enumerate(self.everyone)}
        if self.own is not None:
            ins["h_own"] = (self.own, "h")
        elif not self.split_rows:
            ins["parts"] = (self.parts, "v")
        outs = {f"o{i}": ((p[4], p[1] * TILE), F32, "h") for i, p in enumerate(plan)}
        outs.update({f"o_gain{i}": (s, F32, "v") for i, s in enumerate(self.gain_shapes)})
        scratch = {f"p{i}": (x.shape, BF16) for i, x in enumerate(self.everyone)}
        if self.own is not None:
            scratch["own"] = (self.own.shape, BF16)
        scratch.update({f"b{i}": ((p[4], p[1] * TILE), F32) for i, p in enumerate(plan)})
        got = kernel_call(
            "unpack",
            functools.partial(
                unpack_body,
                plan=plan,
                nseq=len(self.everyone),
                gains_at=self.gains_at - self.split_rows,
                gain_shapes=self.gain_shapes,
            ),
            self.comm.scal,
            ins,
            outs,
            scratch,
            copies=16,
        )
        return [getattr(got, name) for name in outs]


def tie(*xs):
    return lax.optimization_barrier(xs)


def per_device(
    text_in,
    image_in,
    text_seg,
    image_seg,
    text_co_in,
    image_co_in,
    text_co_out,
    image_co_out,
    text_up,
    text_down,
    image_up,
    image_down,
    text_qkv,
    text_proj,
    image_qkv,
    image_proj,
    text_gains,
    image_gains,
    text_upstream,
    image_upstream,
):
    comm = Comm()
    scal = comm.scal
    n = comm.nseq
    rows, nt, dt = text_in.shape
    ni, di = image_in.shape[1:]
    lt, li = n * nt, n * ni
    tt, ti = rows * lt, rows * li
    dc = text_co_out.shape[0]
    ft, fi = text_up.shape[1], image_up.shape[1]
    segs = {"tseg": (text_seg, "v"), "iseg": (image_seg, "v")}
    gains = {"tg": (text_gains, "v"), "ig": (image_gains, "v")}

    (inputs,) = comm.pack((text_in, image_in))
    inputs = comm.pieces(inputs)
    text_upstream, image_upstream, inputs[1] = tie(text_upstream, image_upstream, inputs[1])
    (upstream,) = comm.pack((text_upstream, image_upstream))
    upstream, *inputs = tie(upstream, *inputs)
    upstream = comm.pieces_at_once(upstream)

    def saved(**shapes):
        return (
            {"o_" + name: (shape, dtype, "h") for name, (shape, dtype) in shapes.items()},
            {name: (shape, dtype) for name, (shape, dtype) in shapes.items()},
        )

    outs, scratch = saved(
        tx=((tt, dt), BF16),
        ix=((ti, di), BF16),
        tqkv=((tt, 3 * dc), BF16),
        iqkv=((ti, 3 * dc), BF16),
        tatt=((tt, dc), BF16),
        iatt=((ti, dc), BF16),
        pt=((rows, HC, li, lt), BF16),
        pi=((rows, HC, li, lt), BF16),
        tn1=((tt, dt), F32),
        tr1=((tt, LANES), F32),
        t1=((tt, dt), BF16),
        in1=((ti, di), F32),
        ir1=((ti, LANES), F32),
        i1=((ti, di), BF16),
        ta=((tt, ft), BF16),
        tsl=((tt, ft), BF16),
        ia=((ti, fi), BF16),
        isl=((ti, fi), BF16),
        tr2=((tt, LANES), F32),
        ir2=((ti, LANES), F32),
        tn2=((tt, dt), F32),
        t2=((tt, dt), BF16),
        in2=((ti, di), F32),
        i2=((ti, di), BF16),
    )
    scratch.update(
        staged=((n,) + inputs[0].shape, BF16),
        bias=((rows, li, lt), F32),
        wa=((dt, 3 * dc), BF16),
        wb=((di, 3 * dc), BF16),
        wo=((dc, dt), BF16),
        wd=((ft, dt), BF16),
        acc_t=((tt, dt), F32),
        acc_i=((ti, di), F32),
    )
    ins = {f"part{i}": (x, "h") for i, x in enumerate(inputs)}
    ins.update(
        co_t=(text_co_in, "h"),
        co_i=(image_co_in, "h"),
        out_t=(text_co_out, "h"),
        out_i=(image_co_out, "h"),
        up_t=(text_up, "h"),
        down_t=(text_down, "h"),
        up_i=(image_up, "h"),
        down_i=(image_down, "h"),
        **segs,
        **gains,
    )
    f1 = kernel_call(
        "co_stage",
        functools.partial(co_stage_body, rows=rows, parts=n, count_t=nt, count_i=ni),
        scal,
        ins,
        outs,
        scratch,
    )

    outs, scratch = saved(
        sqkv=((tt, 3 * dt), BF16),
        uqkv=((ti, 3 * di), BF16),
        tmix=((tt, dt), BF16),
        imix=((ti, di), BF16),
        spt=((rows, HT, lt, lt), BF16),
        spi=((rows, HI, li, li), BF16),
        tn3=((tt, dt), F32),
        tr3=((tt, LANES), F32),
        in3=((ti, di), F32),
        ir3=((ti, LANES), F32),
        tres=((rows, nt, dt), BF16),
        ires=((rows, ni, di), BF16),
    )
    scratch.update(
        wa=(text_qkv.shape, BF16),
        wb=(image_qkv.shape, BF16),
        pa=(text_proj.shape, BF16),
        pb=(image_proj.shape, BF16),
        acc_t=((tt, dt), F32),
        acc_i=((ti, di), F32),
        t2=((tt, dt), BF16),
        i2=((ti, di), BF16),
        tn2=((tt, dt), F32),
        in2=((ti, di), F32),
        tbias=((rows, lt, lt), F32),
        ibias=((rows, li, li), F32),
    )
    f2 = kernel_call(
        "self_stage",
        functools.partial(self_stage_body, rows=rows, count_t=nt, count_i=ni),
        scal,
        dict(
            h_t2=(f1.o_t2, "h"),
            h_i2=(f1.o_i2, "h"),
            h_tn2=(f1.o_tn2, "h"),
            h_in2=(f1.o_in2, "h"),
            qkv_t=(text_qkv, "h"),
            qkv_i=(image_qkv, "h"),
            proj_t=(text_proj, "h"),
            proj_i=(image_proj, "h"),
            **segs,
            **gains,
        ),
        outs,
        scratch,
    )

    group_1 = comm.plan_of([(dt, dt, True), (dt, 3 * dt, True), (di, 3 * di, True)])
    group_2 = comm.plan_of([(ft, dt, True), (fi, di, True), (dt, ft, True), (di, fi, True), (di, di, True)])
    group_3 = comm.plan_of([(dc, di, True), (di, 3 * dc, True), (dc, dt, True)])
    group_4 = comm.plan_of([(dt, 3 * dc, False)]).with_gains([text_gains.shape, image_gains.shape])

    def sources(**arrays):
        return (
            {"h_" + name: (x, "h") for name, x in arrays.items()},
            {name: (x.shape, x.dtype) for name, x in arrays.items()},
        )

    def packed(group, tag=""):
        shape = group.half()
        return (
            {"o_keep" + tag: (shape, BF16, "h"), "o_send" + tag: (shape, BF16, "h")},
            {"keep" + tag: (shape, BF16), "send" + tag: (shape, BF16)},
        )

    ins, scratch = sources(
        tn3=f2.o_tn3,
        tr3=f2.o_tr3,
        proj_t=text_proj,
        in3=f2.o_in3,
        ir3=f2.o_ir3,
        proj_i=image_proj,
        sqkv=f2.o_sqkv,
        spt=f2.o_spt,
        uqkv=f2.o_uqkv,
        spi=f2.o_spi,
        tmix=f2.o_tmix,
        t2=f1.o_t2,
        i2=f1.o_i2,
    )
    ins.update({f"h_up{i}": (x, "h") for i, x in enumerate(upstream)})
    outs, more = packed(group_1)
    scratch.update(
        **more,
        up=((n,) + upstream[0].shape, BF16),
        tup=((tt, dt), BF16),
        iup=((ti, di), BF16),
        d3b=((tt, dt), BF16),
        e3b=((ti, di), BF16),
        dmt=((tt, dt), BF16),
        dmi=((ti, di), BF16),
        tdg=((8, dt), F32),
        idg=((8, di), F32),
    )
    outs.update(
        o_e3b=((ti, di), BF16, "h"),
        o_d3=((tt, dt), F32, "v"),
        o_e3=((ti, di), F32, "v"),
        o_dsqkv=((tt, 3 * dt), BF16, "v"),
        o_duqkv=((ti, 3 * di), BF16, "v"),
        o_tdg=((8, dt), F32, "h"),
        o_idg=((8, di), F32, "h"),
    )
    b1 = kernel_call(
        "self_back",
        functools.partial(
            self_back_body, rows=rows, count_t=nt, count_i=ni, plan=group_1.members, ndp=comm.ndp
        ),
        scal,
        {**ins, **gains},
        outs,
        scratch,
    )
    group_1.swap(b1.o_keep, b1.o_send)

    ins, scratch = sources(tn2=f1.o_tn2, tr2=f1.o_tr2, in2=f1.o_in2, ir2=f1.o_ir2)
    outs, more = saved(
        d2=((tt, dt), F32),
        e2=((ti, di), F32),
        d2b=((tt, dt), BF16),
        e2b=((ti, di), BF16),
        tdg=((8, dt), F32),
        idg=((8, di), F32),
    )
    scratch.update(
        **more,
        wa=(text_qkv.shape, BF16),
        wb=(image_qkv.shape, BF16),
        acc_t=((tt, dt), F32),
        acc_i=((ti, di), F32),
    )
    b2 = kernel_call(
        "qkv_back",
        qkv_back_body,
        scal,
        dict(
            **ins,
            qkv_t=(text_qkv, "h"),
            qkv_i=(image_qkv, "h"),
            dsqkv=(b1.o_dsqkv, "v"),
            duqkv=(b1.o_duqkv, "v"),
            d3=(b1.o_d3, "v"),
            e3=(b1.o_e3, "v"),
            **gains,
        ),
        outs,
        scratch,
    )
    group_1.got, d2, e2, d2b, e2b = tie(group_1.got, b2.o_d2, b2.o_e2, b2.o_d2b, b2.o_e2b)
    group_1.add()
    group_1.cross()

    ins, scratch = sources(
        down_i=image_down,
        isl=f1.o_isl,
        up_i=image_up,
        down_t=text_down,
        tsl=f1.o_tsl,
        up_t=text_up,
        ia=f1.o_ia,
        i1=f1.o_i1,
        ta=f1.o_ta,
        t1=f1.o_t1,
        d2b=d2b,
        e2b=e2b,
        imix=f2.o_imix,
        e3b=b1.o_e3b,
    )
    ins.update(h_d2=(d2, "h"), h_e2=(e2, "h"))
    outs, more = packed(group_2)
    scratch.update(x1=((tt, dt), F32), y1=((ti, di), F32))
    scratch.update(**more, dht=((tt, ft), BF16), dhi=((ti, fi), BF16))
    b3 = kernel_call(
        "ffn_back",
        functools.partial(ffn_back_body, plan=group_2.members, ndp=comm.ndp),
        scal,
        ins,
        dict(**outs, o_x1=((tt, dt), F32, "h"), o_y1=((ti, di), F32, "h")),
        scratch,
    )
    group_1.parts, x1, y1, keep, send = tie(
        group_1.parts, b3.o_x1, b3.o_y1, b3.o_keep, b3.o_send
    )
    group_2.swap(keep, send)
    group_1.along()

    ins, scratch = sources(
        x1=x1, y1=y1, tn1=f1.o_tn1, tr1=f1.o_tr1, out_t=text_co_out, in1=f1.o_in1, ir1=f1.o_ir1, out_i=image_co_out
    )
    outs, more = saved(
        d1b=((tt, dt), BF16),
        e1b=((ti, di), BF16),
        dat=((tt, dc), BF16),
        dai=((ti, dc), BF16),
        own_t=((rows, nt, dt), F32),
        own_i=((rows, ni, di), F32),
        tdg=((8, dt), F32),
        idg=((8, di), F32),
    )
    scratch.update(**more, d1=((tt, dt), F32), e1=((ti, di), F32))
    b4 = kernel_call(
        "first_norm_back",
        functools.partial(first_norm_back_body, rows=rows, count_t=nt, count_i=ni),
        scal,
        dict(**ins, **gains),
        outs,
        scratch,
    )
    group_2.got, dat, dai = tie(group_2.got, b4.o_dat, b4.o_dai)
    group_2.add()
    group_2.cross()

    ins, scratch = sources(
        tqkv=f1.o_tqkv,
        pt=f1.o_pt,
        iqkv=f1.o_iqkv,
        pi=f1.o_pi,
        tatt=f1.o_tatt,
        iatt=f1.o_iatt,
        tx=f1.o_tx,
        ix=f1.o_ix,
        dat=dat,
        dai=dai,
        d1b=b4.o_d1b,
        e1b=b4.o_e1b,
        tdg1=b4.o_tdg,
        tdg2=b2.o_tdg,
        tdg3=b1.o_tdg,
        idg1=b4.o_idg,
        idg2=b2.o_idg,
        idg3=b1.o_idg,
    )
    outs, more = packed(group_3)
    outs_last, more_last = packed(group_4, "_last")
    outs.update(outs_last)
    scratch.update(
        **more, **more_last, dt=((tt, 3 * dc), BF16), di=((ti, 3 * dc), BF16), gain_rows=((GAIN_ROWS, TILE), F32)
    )
    b5 = kernel_call(
        "co_back",
        functools.partial(
            co_back_body,
            rows=rows,
            parts=n,
            count_t=nt,
            count_i=ni,
            plan=group_3.members,
            last_plan=group_4.members[0],
            ndp=comm.ndp,
            gains_at=group_4.gains_at,
        ),
        scal,
        ins,
        dict(
            **outs,
            o_dt=((rows, nt, 3 * dc), BF16, "v"),
            o_di=((rows, ni, 3 * dc), BF16, "v"),
        ),
        scratch,
    )
    (
        group_1.everyone[1],
        group_1.everyone[2],
        group_2.parts,
        dt_own,
        di_own,
        keep,
        send,
        keep_last,
        send_last,
    ) = tie(
        group_1.everyone[1],
        group_1.everyone[2],
        group_2.parts,
        b5.o_dt,
        b5.o_di,
        b5.o_keep,
        b5.o_send,
        b5.o_keep_last,
        b5.o_send_last,
    )
    group_3.swap(keep, send)
    group_4.swap(keep_last, send_last)
    group_2.along()
    b6 = kernel_call(
        "in_back",
        in_back_body,
        scal,
        dict(
            co_t=(text_co_in, "h"),
            co_i=(image_co_in, "h"),
            dt=(dt_own, "v"),
            di=(di_own, "v"),
            h_d1=(b4.o_own_t, "h"),
            h_e1=(b4.o_own_i, "h"),
        ),
        dict(o_dt=((rows, nt, dt), F32, "h"), o_di=((rows, ni, di), F32, "h")),
        dict(
            gt=((rows, nt, dt), F32),
            gi=((rows, ni, di), F32),
            wa=(text_co_in.shape, BF16),
            wb=(image_co_in.shape, BF16),
            d1=((rows, nt, dt), F32),
            e1=((rows, ni, di), F32),
        ),
    )
    group_1.everyone[3], group_3.got, group_4.got, text_in_grad, image_in_grad = tie(
        group_1.everyone[3], group_3.got, group_4.got, b6.o_dt, b6.o_di
    )
    group_3.add()
    group_3.cross()
    group_4.add()
    group_2.everyone[1], group_2.everyone[2], group_3.parts, group_4.pair = tie(
        group_2.everyone[1], group_2.everyone[2], group_3.parts, group_4.pair
    )
    group_4.cross()
    group_3.along()
    text_proj_grad, text_qkv_grad, image_qkv_grad = group_1.unpack()
    (
        text_down_grad,
        image_down_grad,
        text_up_grad,
        image_up_grad,
        image_proj_grad,
    ) = group_2.unpack()
    group_4.along()
    text_co_in_grad, text_gains_grad, image_gains_grad = group_4.unpack()
    *group_3.everyone, text_co_in_grad, text_gains_grad, image_gains_grad = tie(
        *group_3.everyone, text_co_in_grad, text_gains_grad, image_gains_grad
    )
    image_co_out_grad, image_co_in_grad, text_co_out_grad = group_3.unpack()
    return (
        f2.o_tres,
        f2.o_ires,
        text_in_grad,
        image_in_grad,
        text_co_in_grad,
        image_co_in_grad,
        text_co_out_grad,
        image_co_out_grad,
        text_up_grad,
        text_down_grad,
        image_up_grad,
        image_down_grad,
        text_qkv_grad,
        text_proj_grad,
        image_qkv_grad,
        image_proj_grad,
        text_gains_grad,
        image_gains_grad,
    )


def solution(mesh):
    slots = P("dp", "seq", None)
    rows = P("dp", None)
    return jax.shard_map(
        per_device,
        mesh=mesh,
        in_specs=(slots, slots, rows, rows) + (P(),) * 14 + (slots, slots),
        out_specs=(slots,) * 4 + (rows,) * 12 + (P(), P()),
        check_vma=False,
    )
```

```python
import functools
import types

import jax
import jax.numpy as jnp
from jax import lax
from jax.experimental import pallas as pl
from jax.experimental.pallas import tpu as pltpu
from jax.sharding import PartitionSpec as P

HT = 12
HI = 8
HC = 8

NORM_EPS = 1e-05

F32 = jnp.float32
BF16 = jnp.bfloat16
LOG2E = 1.4426950408889634
MASKED = -1.0e9 * LOG2E
SQRT_2_PI = 0.7978845608028654
GELU_CUBE = 0.044715
LANES = 128
TILE = 256
WIDE = 1536
WHOLE = 3072
GAIN_ROWS = 32
MIB = 1024 * 1024


def dot_nt(a, b):
    return lax.dot_general(a, b, (((1,), (1,)), ((), ())), preferred_element_type=F32)


def dot_nn(a, b):
    return lax.dot_general(a, b, (((1,), (0,)), ((), ())), preferred_element_type=F32)


def dot_tn(a, b):
    return lax.dot_general(a, b, (((0,), (0,)), ((), ())), preferred_element_type=F32)


class Copies:
    def __init__(self, sems):
        self.sems, self.used, self.leaving = sems, 0, []

    def fetch(self, src, dst):
        copy = pltpu.make_async_copy(src, dst, self.sems.at[self.used])
        self.used += 1
        copy.start()
        return copy

    def flush(self, src, dst):
        self.leaving.append(self.fetch(src, dst))

    def finish(self):
        for copy in self.leaving:
            copy.wait()


def nbytes(shape, dtype):
    total = jnp.dtype(dtype).itemsize
    dims = list(shape)
    dims[-1] = -(-dims[-1] // 128) * 128
    if len(dims) > 1:
        dims[-2] = -(-dims[-2] // 16) * 16
    for d in dims:
        total *= d
    return total


def kernel_call(name, body, scal, ins, outs, scratch, copies=64, extra=8):
    names = list(ins) + list(outs) + list(scratch)

    def kernel(scal_ref, *refs):
        k = types.SimpleNamespace(**dict(zip(names, refs)))
        moves = Copies(refs[-1])
        body(scal_ref, k, moves)
        moves.finish()

    def place(where):
        return pl.BlockSpec(memory_space=pltpu.HBM if where == "h" else pltpu.VMEM)

    def shape_of(shape, dtype, where):
        return pltpu.HBM(tuple(shape), dtype) if where == "h" else jax.ShapeDtypeStruct(shape, dtype)

    args = [
        pltpu.with_memory_space_constraint(x, pltpu.HBM) if where == "h" else x for x, where in ins.values()
    ]
    total = sum(nbytes(s, d) for s, d in scratch.values()) + extra * MIB
    got = pl.pallas_call(
        kernel,
        in_specs=[pl.BlockSpec(memory_space=pltpu.SMEM)] + [place(w) for _, w in ins.values()],
        out_specs=[place(w) for _, _, w in outs.values()],
        out_shape=[shape_of(*o) for o in outs.values()],
        scratch_shapes=[pltpu.VMEM(tuple(s), d) for s, d in scratch.values()]
        + [pltpu.SemaphoreType.DMA((copies,))],
        compiler_params=pltpu.CompilerParams(vmem_limit_bytes=total),
        name=name,
    )(scal, *args)
    return types.SimpleNamespace(**dict(zip(outs, got)))


def loop(count, body, unroll=1):
    def step(i, carry):
        body(i)
        return carry

    lax.fori_loop(0, count, step, 0, unroll=unroll)


def at(i, size):
    return pl.ds(pl.multiple_of(i * size, size), size)


def row_chunks(rows, body):
    size = next(c for c in (128, 80, 64, 32, 16) if rows % c == 0)
    loop(rows // size, lambda i: body(at(i, size)))


def tile_of(width, limit):
    parts = -(-width // limit)
    while width % (parts * TILE):
        parts += 1
    return width // parts


def pick(i, values):
    out = values[0]
    for k in range(1, len(values)):
        out = jnp.where(i == k, values[k], out)
    return out


def lane_halves(width):
    if width == LANES:
        return [None]
    lane = lax.broadcasted_iota(jnp.int32, (1, LANES), 1)
    return [(lane // width) == i for i in range(LANES // width)]


def keep_lanes(x, sel):
    return x if sel is None else jnp.where(sel, x, jnp.zeros_like(x))


def cols(ref, rows, tile):
    return ref[rows, tile * LANES : (tile + 1) * LANES]


def store_bias(bias_ref, down_ref, along_ref):
    for r in range(bias_ref.shape[0]):
        row = down_ref[r : r + 1].astype(F32)
        col = jnp.transpose(jnp.broadcast_to(row, (8, row.shape[1])))[:, :1]
        bias_ref[r] = jnp.where(col == along_ref[r : r + 1].astype(F32), 0.0, MASKED).astype(F32)


def attend(r, q_ref, kv_ref, bias, o_ref, p_ref, lq, lk, width):
    scale = width**-0.5 * LOG2E
    sels = lane_halves(width)
    n = o_ref.shape[1] // LANES
    qs, ks = at(r, lq), at(r, lk)
    for t in range(n):
        q, k, v = cols(q_ref, qs, t), cols(kv_ref, ks, n + t), cols(kv_ref, ks, 2 * n + t)
        out = None
        for i, sel in enumerate(sels):
            s = dot_nt(k, keep_lanes(q, sel)) * scale + bias
            e = jnp.exp2(s - jnp.max(s, axis=0, keepdims=True))
            p = (e * (1.0 / jnp.sum(e, axis=0, keepdims=True))).astype(BF16)
            p_ref[r, t * len(sels) + i] = p
            o = dot_tn(p, v)
            out = o if out is None else jnp.where(sel, o, out)
        o_ref[qs, t * LANES : (t + 1) * LANES] = out.astype(BF16)


def attend_wide(r, q_ref, kv_ref, bias, o_ref, p_ref, lq, lk):
    scale = LANES**-0.5 * LOG2E
    n = o_ref.shape[1] // LANES
    qs, ks = at(r, lq), at(r, lk)
    for t in range(n):
        q, k, v = cols(q_ref, qs, t), cols(kv_ref, ks, n + t), cols(kv_ref, ks, 2 * n + t)
        s = dot_nt(q, k) * scale + bias
        e = jnp.exp2(s - jnp.max(s, axis=1, keepdims=True))
        p = (e * (1.0 / jnp.sum(e, axis=1, keepdims=True))).astype(BF16)
        p_ref[r, t] = p
        o_ref[qs, t * LANES : (t + 1) * LANES] = dot_nn(p, v).astype(BF16)


def attend_wide_back(r, q_ref, kv_ref, da_ref, p_ref, dq_ref, dkv_ref, lq, lk):
    scale = LANES**-0.5
    n = da_ref.shape[1] // LANES
    qs, ks = at(r, lq), at(r, lk)
    for t in range(n):
        q, k, v = cols(q_ref, qs, t), cols(kv_ref, ks, n + t), cols(kv_ref, ks, 2 * n + t)
        da = cols(da_ref, qs, t)
        p = p_ref[r, t]
        pf = p.astype(F32)
        w = pf * dot_nt(da, v)
        ds = (w - pf * jnp.sum(w, axis=1, keepdims=True)).astype(BF16)
        dq_ref[qs, t * LANES : (t + 1) * LANES] = (dot_nn(ds, k) * scale).astype(BF16)
        dkv_ref[ks, (n + t) * LANES : (n + t + 1) * LANES] = (dot_tn(ds, q) * scale).astype(BF16)
        dkv_ref[ks, (2 * n + t) * LANES : (2 * n + t + 1) * LANES] = dot_tn(p, da).astype(BF16)


def attend_back(r, q_ref, kv_ref, da_ref, p_ref, dq_ref, dkv_ref, lq, lk, width):
    scale = width**-0.5
    sels = lane_halves(width)
    n = da_ref.shape[1] // LANES
    qs, ks = at(r, lq), at(r, lk)
    for t in range(n):
        q, k, v = cols(q_ref, qs, t), cols(kv_ref, ks, n + t), cols(kv_ref, ks, 2 * n + t)
        da = cols(da_ref, qs, t)
        dq = dk = dv = None
        for i, sel in enumerate(sels):
            p = p_ref[r, t * len(sels) + i]
            da_h = keep_lanes(da, sel)
            pf = p.astype(F32)
            w = pf * dot_nt(v, da_h)
            ds = (w - pf * jnp.sum(w, axis=0, keepdims=True)).astype(BF16)
            dv_h = dot_nn(p, da_h)
            dk_h = dot_nn(ds, keep_lanes(q, sel))
            dq_h = dot_tn(ds, keep_lanes(k, sel))
            dq = dq_h if dq is None else dq + dq_h
            dk = dk_h if dk is None else dk + dk_h
            dv = dv_h if dv is None else dv + dv_h
        dq_ref[qs, t * LANES : (t + 1) * LANES] = (dq * scale).astype(BF16)
        dkv_ref[ks, (n + t) * LANES : (n + t + 1) * LANES] = (dk * scale).astype(BF16)
        dkv_ref[ks, (2 * n + t) * LANES : (2 * n + t + 1) * LANES] = dv.astype(BF16)


def normalize(z):
    center = z - jnp.mean(z, axis=-1, keepdims=True)
    inv = lax.rsqrt(jnp.mean(center * center, axis=-1, keepdims=True) + NORM_EPS)
    return center * inv, inv


def fold_rows(x):
    return jnp.sum(x.reshape(x.shape[0] // 8, 8, x.shape[1]), axis=0)


def matmul_tiles(x_ref, w_ref, o_ref):
    n = o_ref.shape[1]
    tile = tile_of(n, WHOLE)

    def step(i):
        o_ref[:, at(i, tile)] = dot_nn(x_ref[...], w_ref[:, at(i, tile)]).astype(o_ref.dtype)

    loop(n // tile, step)


def norm_rows(acc_ref, res, gain, n_ref, inv_ref, low_ref=None):
    def chunk(rows):
        n, inv = normalize(acc_ref[rows] + res(rows))
        n_ref[rows] = n
        inv_ref[rows] = jnp.broadcast_to(inv, (inv.shape[0], LANES))
        if low_ref is not None:
            low_ref[rows] = (n * gain).astype(BF16)

    row_chunks(acc_ref.shape[0], chunk)


def norm_back_rows(dy_of, n_ref, inv_ref, gain, d_ref, low_ref, dg_ref):
    dg_ref[...] = jnp.zeros_like(dg_ref)

    def chunk(rows):
        dy = dy_of(rows)
        n = n_ref[rows]
        dn = dy * gain
        m1 = jnp.mean(dn, axis=-1, keepdims=True)
        m2 = jnp.mean(dn * n, axis=-1, keepdims=True)
        d = inv_ref[rows][:, :1] * (dn - m1 - n * m2)
        d_ref[rows] = d
        low_ref[rows] = d.astype(BF16)
        dg_ref[...] += fold_rows(dy * n)

    row_chunks(n_ref.shape[0], chunk)


def gelu_pair(v):
    v2 = v * v
    s = 0.5 + 0.5 * jnp.tanh(v * (SQRT_2_PI + (SQRT_2_PI * GELU_CUBE) * v2))
    a = v * s
    return a, s + a * (1.0 - s) * (2.0 * SQRT_2_PI + (6.0 * SQRT_2_PI * GELU_CUBE) * v2)


def ffn_tiles(x_ref, up_ref, down_ref, a_ref, slope_ref, acc_ref):
    width = tile_of(a_ref.shape[1], WIDE)

    def step(i):
        tile = at(i, width)
        a, slope = gelu_pair(dot_nn(x_ref[...], up_ref[:, tile]))
        a = a.astype(BF16)
        a_ref[:, tile] = a
        slope_ref[:, tile] = slope.astype(BF16)
        acc_ref[...] += dot_nn(a, down_ref[tile])

    acc_ref[...] = jnp.zeros_like(acc_ref)
    loop(a_ref.shape[1] // width, step)


def ffn_back_product(low_ref, down_ref, slope_ref, up_ref, dh_ref, acc_ref, ready):
    ready(low_ref, down_ref)
    dh = dot_nt(low_ref[...], down_ref[...])
    ready(slope_ref)
    dh = (dh * slope_ref[...].astype(F32)).astype(BF16)
    dh_ref[...] = dh
    ready(up_ref, acc_ref)
    acc_ref[...] += dot_nt(dh, up_ref[...])


def send_packed(cp, keep, send, far_keep, far_send, first, last):
    for near, far in ((send, far_send), (keep, far_keep)):
        cp.flush(near.at[:, first:last], far.at[:, first:last])


def wgrad_group(scal, cp, xs, ys, plan, ndp, keep, send, far_keep, far_send):
    by_member = all(off % 16 == 0 and (tiles * rows) % 16 == 0 for tiles, _, _, off, rows in plan)
    for x, y, p in zip(xs, ys, plan):
        wgrad_member(scal, x, y, keep, send, p, ndp)
        if by_member:
            send_packed(cp, keep, send, far_keep, far_send, p[3], p[3] + p[0] * p[4])
    if not by_member:
        send_packed(cp, keep, send, far_keep, far_send, 0, keep.shape[1])


def wgrad_member(scal_ref, x_ref, y_ref, keep_ref, send_ref, plan, ndp):
    tiles, total, split, off, rows = plan
    odd = scal_ref[0] == 1
    xt = jnp.transpose(x_ref[...])
    first = jnp.minimum(scal_ref[1] * tiles, total - tiles) if split else 0
    for t in range(tiles):
        g = dot_nn(xt, y_ref[:, at(first + t, TILE)]).astype(BF16)
        base = off + t * rows
        for j in range(ndp // 2):
            even_rows = g[2 * j * rows : (2 * j + 1) * rows]
            odd_rows = g[(2 * j + 1) * rows : (2 * j + 2) * rows]
            keep_ref[j, base : base + rows] = jnp.where(odd, odd_rows, even_rows)
            send_ref[j, base : base + rows] = jnp.where(odd, even_rows, odd_rows)


def pack_gains(gain_refs, rows_ref, keep_ref, send_ref, base):
    row = 0
    for ref in gain_refs:
        total = jnp.sum(ref[...], axis=0, keepdims=True)
        for c in range(0, ref.shape[1], TILE):
            rows_ref[row : row + 1] = total[:, c : c + TILE]
            row += 1
    for row in range(row, GAIN_ROWS):
        rows_ref[row : row + 1] = jnp.zeros((1, TILE), F32)
    low = rows_ref[...].astype(BF16)
    for j in range(keep_ref.shape[0]):
        keep_ref[j, base : base + GAIN_ROWS] = low
        send_ref[j, base : base + GAIN_ROWS] = low


def co_stage_body(scal, k, cp, *, rows, parts, count_t, count_i):
    pieces = [cp.fetch(getattr(k, f"part{i}"), k.staged.at[i]) for i in range(parts)]
    wa = cp.fetch(k.co_t, k.wa)
    wb = cp.fetch(k.co_i, k.wb)
    wo = cp.fetch(k.out_t, k.wo)
    wd = cp.fetch(k.down_t, k.wd)
    lt, li = parts * count_t, parts * count_i
    store_bias(k.bias, k.iseg, k.tseg)
    for piece in pieces:
        piece.wait()
    base = join_tiles(scal[1], k.staged, k.tx, count_t, rows, 0)
    wa.wait()
    matmul_tiles(k.tx, k.wa, k.tqkv)
    up_t = cp.fetch(k.up_t, k.wa)
    cp.flush(k.tx, k.o_tx)
    cp.flush(k.tqkv, k.o_tqkv)
    join_tiles(scal[1], k.staged, k.ix, count_i, rows, base)
    wb.wait()
    matmul_tiles(k.ix, k.wb, k.iqkv)
    wi = k.ix.shape[1]
    up_i = cp.fetch(k.up_i, k.wb.at[:, 0:wi])
    down_i = cp.fetch(k.down_i, k.wb.at[:, wi : 2 * wi])
    out_i = cp.fetch(k.out_i, k.wb.at[:, 2 * wi : 3 * wi])
    cp.flush(k.ix, k.o_ix)
    cp.flush(k.iqkv, k.o_iqkv)
    assert k.tatt.shape[1] == HC * LANES

    def heads(r):
        attend(r, k.tqkv, k.iqkv, k.bias[r], k.tatt, k.pt, lt, li, LANES)
        attend_wide(r, k.iqkv, k.tqkv, k.bias[r], k.iatt, k.pi, li, lt)

    loop(rows, heads)
    cp.flush(k.tatt, k.o_tatt)
    cp.flush(k.iatt, k.o_iatt)
    cp.flush(k.pt, k.o_pt)
    cp.flush(k.pi, k.o_pi)
    out_i.wait()
    matmul_tiles(k.iatt, k.wb.at[:, 2 * wi : 3 * wi], k.acc_i)
    ig = k.ig[...]
    norm_rows(k.acc_i, lambda r: k.ix[r].astype(F32), ig[0:1], k.in1, k.ir1, k.i1)
    up_i.wait()
    down_i.wait()
    ffn_tiles(k.i1, k.wb.at[:, 0:wi], k.wb.at[:, wi : 2 * wi], k.ia, k.isl, k.acc_i)
    norm_rows(k.acc_i, lambda r: k.in1[r] * ig[0:1], ig[1:2], k.in2, k.ir2, k.i2)
    for name in ("in1", "ir1", "i1", "ia", "isl", "in2", "ir2", "i2"):
        cp.flush(getattr(k, name), getattr(k, "o_" + name))
    wo.wait()
    matmul_tiles(k.tatt, k.wo, k.acc_t)
    tg = k.tg[...]
    norm_rows(k.acc_t, lambda r: k.tx[r].astype(F32), tg[0:1], k.tn1, k.tr1, k.t1)
    up_t.wait()
    wd.wait()
    for name in ("tn1", "tr1", "t1"):
        cp.flush(getattr(k, name), getattr(k, "o_" + name))
    ffn_tiles(k.t1, k.wa, k.wd, k.ta, k.tsl, k.acc_t)
    cp.flush(k.ta, k.o_ta)
    cp.flush(k.tsl, k.o_tsl)
    norm_rows(k.acc_t, lambda r: k.tn1[r] * tg[0:1], tg[1:2], k.tn2, k.tr2, k.t2)
    for name in ("t2", "tn2", "tr2"):
        cp.flush(getattr(k, name), getattr(k, "o_" + name))


def self_stage_body(scal, k, cp, *, rows, count_t, count_i):
    t2 = cp.fetch(k.h_t2, k.t2)
    wa = cp.fetch(k.qkv_t, k.wa)
    i2 = cp.fetch(k.h_i2, k.i2)
    wb = cp.fetch(k.qkv_i, k.wb)
    pa = cp.fetch(k.proj_t, k.pa)
    pb = cp.fetch(k.proj_i, k.pb)
    tn2 = cp.fetch(k.h_tn2, k.tn2)
    in2 = cp.fetch(k.h_in2, k.in2)
    store_bias(k.tbias, k.tseg, k.tseg)
    store_bias(k.ibias, k.iseg, k.iseg)
    lt = k.t2.shape[0] // rows
    li = k.i2.shape[0] // rows
    t2.wait()
    wa.wait()
    matmul_tiles(k.t2, k.wa, k.sqkv)
    cp.flush(k.sqkv, k.o_sqkv)
    i2.wait()
    wb.wait()
    matmul_tiles(k.i2, k.wb, k.uqkv)
    cp.flush(k.uqkv, k.o_uqkv)
    wt = k.tmix.shape[1] // HT
    wi = k.imix.shape[1] // HI

    def heads(r):
        attend(r, k.sqkv, k.sqkv, k.tbias[r], k.tmix, k.spt, lt, lt, wt)
        attend(r, k.uqkv, k.uqkv, k.ibias[r], k.imix, k.spi, li, li, wi)

    loop(rows, heads)
    for name in ("tmix", "imix", "spt", "spi"):
        cp.flush(getattr(k, name), getattr(k, "o_" + name))
    tn2.wait()
    in2.wait()
    z = scal[1]
    for mix, w, ready, acc, n2, g, n3, r3, res, count in (
        (k.tmix, k.pa, pa, k.acc_t, k.tn2, k.tg, k.tn3, k.tr3, k.tres, count_t),
        (k.imix, k.pb, pb, k.acc_i, k.in2, k.ig, k.in3, k.ir3, k.ires, count_i),
    ):
        ready.wait()
        matmul_tiles(mix, w, acc)
        gain = g[...]
        norm_rows(acc, lambda r, n2=n2, gain=gain: n2[r] * gain[1:2], None, n3, r3)
        length = mix.shape[0] // rows
        for r in range(rows):
            own = n3[pl.ds(pl.multiple_of(r * length + z * count, 8), count)]
            res[r] = (own * gain[2:3]).astype(BF16)
        for name in ("tn3", "tr3", "tres") if mix is k.tmix else ("in3", "ir3", "ires"):
            cp.flush(getattr(k, name), getattr(k, "o_" + name))


def self_back_body(scal, k, cp, *, rows, count_t, count_i, plan, ndp):
    ups = [cp.fetch(getattr(k, f"h_up{i}"), k.up.at[i]) for i in range(k.up.shape[0])]
    names = ("tn3", "tr3", "proj_t", "in3", "ir3", "proj_i", "sqkv", "spt", "uqkv", "spi")
    names += ("tmix", "t2", "i2")
    moves = {n: cp.fetch(getattr(k, "h_" + n), getattr(k, n)) for n in names}

    def ready(*which):
        for n in which:
            moves[n].wait()

    for copy in ups:
        copy.wait()
    base = join_tiles(scal[1], k.up, k.tup, count_t, rows, 0)
    join_tiles(scal[1], k.up, k.iup, count_i, rows, base)
    ready("tn3", "tr3", "proj_t")
    norm_back_rows(
        lambda r: k.tup[r].astype(F32), k.tn3, k.tr3, k.tg[2:3], k.o_d3, k.d3b, k.tdg
    )
    k.dmt[...] = dot_nt(k.d3b[...], k.proj_t[...]).astype(BF16)
    ready("in3", "ir3", "proj_i")
    norm_back_rows(
        lambda r: k.iup[r].astype(F32), k.in3, k.ir3, k.ig[2:3], k.o_e3, k.e3b, k.idg
    )
    k.dmi[...] = dot_nt(k.e3b[...], k.proj_i[...]).astype(BF16)
    ready("sqkv", "spt", "uqkv", "spi")
    lt, li = k.tup.shape[0] // rows, k.iup.shape[0] // rows
    wt = k.dmt.shape[1] // HT
    wi = k.dmi.shape[1] // HI

    def heads(r):
        attend_back(r, k.sqkv, k.sqkv, k.dmt, k.spt, k.o_dsqkv, k.o_dsqkv, lt, lt, wt)
        attend_back(r, k.uqkv, k.uqkv, k.dmi, k.spi, k.o_duqkv, k.o_duqkv, li, li, wi)

    loop(rows, heads)
    ready("tmix", "t2", "i2")
    xs, ys = (k.tmix, k.t2, k.i2), (k.d3b, k.o_dsqkv, k.o_duqkv)
    cp.flush(k.e3b, k.o_e3b)
    wgrad_group(scal, cp, xs, ys, plan, ndp, k.keep, k.send, k.o_keep, k.o_send)
    for name in ("tdg", "idg"):
        cp.flush(getattr(k, name), getattr(k, "o_" + name))


def chunked(cp, src, dst, axis, count=3):
    size = src.shape[axis] // count
    out = []
    for i in range(count):
        part = slice(i * size, (i + 1) * size)
        part = (slice(None), part) if axis == 1 else (part, slice(None))
        out.append((cp.fetch(src.at[part], dst.at[part]), part))
    return out


def qkv_back_body(scal, k, cp):
    wa = chunked(cp, k.qkv_t, k.wa, 0, 2)
    extra_t = [cp.fetch(k.h_tn2, k.tn2), cp.fetch(k.h_tr2, k.tr2)]
    wb = chunked(cp, k.qkv_i, k.wb, 0, 2)
    extra_i = [cp.fetch(k.h_in2, k.in2), cp.fetch(k.h_ir2, k.ir2)]
    for dx, w, ready, extra, acc, d3, n, inv, g, outs in (
        (k.dsqkv, k.wa, wa, extra_t, k.acc_t, k.d3, k.tn2, k.tr2, k.tg, ("d2", "d2b", "tdg")),
        (k.duqkv, k.wb, wb, extra_i, k.acc_i, k.e3, k.in2, k.ir2, k.ig, ("e2", "e2b", "idg")),
    ):
        for copy, (part, _) in ready:
            copy.wait()
            acc[:, part] = dot_nt(dx[...], w[part])
        for copy in extra:
            copy.wait()
        d2, low, dg = (getattr(k, name) for name in outs)
        norm_back_rows(lambda r, acc=acc, d3=d3: d3[r] + acc[r], n, inv, g[1:2], d2, low, dg)
        for name in outs:
            cp.flush(getattr(k, name), getattr(k, "o_" + name))


def ffn_back_body(scal, k, cp, *, plan, ndp):
    moves = {}

    def start(*names):
        for name in names:
            near = getattr(k, {"e2": "y1", "d2": "x1"}.get(name, name))
            moves[id(near)] = cp.fetch(getattr(k, "h_" + name), near)

    def ready(*refs):
        for ref in refs:
            moves.pop(id(ref)).wait()

    start("e2b", "down_i", "isl", "up_i", "e2", "d2b", "down_t", "tsl", "up_t", "d2")
    start("ta", "ia", "t1", "i1", "imix", "e3b")
    ffn_back_product(k.e2b, k.down_i, k.isl, k.up_i, k.dhi, k.y1, ready)
    cp.flush(k.y1, k.o_y1)
    ffn_back_product(k.d2b, k.down_t, k.tsl, k.up_t, k.dht, k.x1, ready)
    cp.flush(k.x1, k.o_x1)
    ready(k.ta, k.ia, k.t1, k.i1, k.imix, k.e3b)
    xs, ys = (k.ta, k.ia, k.t1, k.i1, k.imix), (k.d2b, k.e2b, k.dht, k.dhi, k.e3b)
    wgrad_group(scal, cp, xs, ys, plan, ndp, k.keep, k.send, k.o_keep, k.o_send)


def first_norm_back_body(scal, k, cp, *, rows, count_t, count_i):
    moves_t = [cp.fetch(getattr(k, "h_" + n), getattr(k, n)) for n in ("x1", "tn1", "tr1", "out_t")]
    moves_i = [cp.fetch(getattr(k, "h_" + n), getattr(k, n)) for n in ("y1", "in1", "ir1", "out_i")]
    *moves_t, out_t = moves_t
    *moves_i, out_i = moves_i
    z = scal[1]
    for moves, last, x1, n, inv, g, d1, low, dg, w, da, own, count in (
        (moves_t, out_t, k.x1, k.tn1, k.tr1, k.tg, k.d1, k.d1b, k.tdg, k.out_t, k.dat, k.own_t, count_t),
        (moves_i, out_i, k.y1, k.in1, k.ir1, k.ig, k.e1, k.e1b, k.idg, k.out_i, k.dai, k.own_i, count_i),
    ):
        for copy in moves:
            copy.wait()
        norm_back_rows(lambda r, x1=x1: x1[r], n, inv, g[0:1], d1, low, dg)
        last.wait()
        da[...] = dot_nt(low[...], w[...]).astype(BF16)
        length = x1.shape[0] // rows
        for r in range(rows):
            own[r] = d1[pl.ds(pl.multiple_of(r * length + z * count, 8), count)]
        text = x1 is k.x1
        for name in ("dat", "d1b", "own_t", "tdg") if text else ("dai", "e1b", "own_i", "idg"):
            cp.flush(getattr(k, name), getattr(k, "o_" + name))


def co_back_body(scal, k, cp, *, rows, parts, count_t, count_i, plan, last_plan, ndp, gains_at):
    names = ("tqkv", "pt", "dat", "iqkv", "pi", "dai", "iatt", "e1b", "tatt", "d1b", "ix", "tx")
    names += ("tdg1", "tdg2", "tdg3", "idg1", "idg2", "idg3")
    lt, li = parts * count_t, parts * count_i
    first = cp.used
    cp.used += 6 * rows

    def row_copies(r):
        out = []
        for i, name in enumerate(names[:6]):
            far, near = getattr(k, "h_" + name), getattr(k, name)
            part = r if name in ("pt", "pi") else at(r, near.shape[0] // rows)
            out.append(pltpu.make_async_copy(far.at[part], near.at[part], cp.sems.at[first + 6 * r + i]))
        return out

    for r in range(rows):
        for copy in row_copies(r):
            copy.start()
    moves = [cp.fetch(getattr(k, "h_" + n), getattr(k, n)) for n in names[6:]]

    def heads(r):
        for copy in row_copies(r):
            copy.wait()
        attend_back(r, k.tqkv, k.iqkv, k.dat, k.pt, k.dt, k.di, lt, li, LANES)
        attend_wide_back(r, k.iqkv, k.tqkv, k.dai, k.pi, k.di, k.dt, li, lt)

    loop(rows, heads)
    for copy in moves:
        copy.wait()
    xs, ys = (k.iatt, k.ix, k.tatt), (k.e1b, k.di, k.d1b)
    wgrad_group(scal, cp, xs, ys, plan, ndp, k.keep, k.send, k.o_keep, k.o_send)
    gains = (k.tdg1, k.tdg2, k.tdg3, k.idg1, k.idg2, k.idg3)
    pack_gains(gains, k.gain_rows, k.keep_last, k.send_last, gains_at)
    wgrad_member(scal, k.tx, k.dt, k.keep_last, k.send_last, last_plan, ndp)
    cp.flush(k.send_last, k.o_send_last)
    cp.flush(k.keep_last, k.o_keep_last)
    z = scal[1]
    for full, own, count in ((k.dt, k.o_dt, count_t), (k.di, k.o_di, count_i)):
        for r in range(rows):
            values = [
                full[(r * parts + i) * count : (r * parts + i + 1) * count] for i in range(parts)
            ]
            own[r] = pick(z, values)


def in_back_body(scal, k, cp):
    own_t = cp.fetch(k.h_d1, k.d1)
    own_i = cp.fetch(k.h_e1, k.e1)
    wa = chunked(cp, k.co_t, k.wa, 1)
    wb = chunked(cp, k.co_i, k.wb, 1)
    for dx, w, chunks, d1, out, own in (
        (k.dt, k.wa, wa, k.d1, k.gt, own_t),
        (k.di, k.wb, wb, k.e1, k.gi, own_i),
    ):
        own.wait()
        r, count, m = dx.shape
        flat = dx[...].reshape(r * count, m)
        total = d1[...].reshape(r * count, d1.shape[2])
        for copy, part in chunks:
            copy.wait()
            total = total + dot_nt(flat[part], w[part])
        out[...] = total.reshape(out.shape)
        cp.flush(out, k.o_dt if out is k.gt else k.o_di)


def pack_body(scal, k, cp, *, count):
    names = [f"{stream}{i}" for i in range(count) for stream in "ti"]
    moves = {name: cp.fetch(getattr(k, "h_" + name), getattr(k, name)) for name in names}
    for i in range(count):
        packed = getattr(k, f"s{i}")
        base = 0
        for name in (f"t{i}", f"i{i}"):
            moves[name].wait()
            ref = getattr(k, name)
            for c in range(0, ref.shape[2], TILE):
                for r in range(ref.shape[0]):
                    part = ref[r, :, c : c + TILE]
                    packed[base : base + part.shape[0]] = part
                    base += part.shape[0]
        cp.flush(packed, getattr(k, f"o{i}"))


def join_tiles(z, staged, full, count, rows, base):
    parts = staged.shape[0]
    for c in range(0, full.shape[1], TILE):
        for r in range(rows):
            values = [staged[i, base : base + count] for i in range(parts)]
            for i in range(parts):
                to = (r * parts + i) * count
                full[to : to + count, c : c + TILE] = pick(z ^ i, values)
            base += count
    return base


def unpack_body(scal, k, cp, *, plan, nseq, gains_at, gain_shapes):
    z = scal[1]
    pieces = [cp.fetch(getattr(k, f"h{i}"), getattr(k, f"p{i}")) for i in range(nseq)]
    def own_rows(first, last):
        if not hasattr(k, "parts"):
            return k.own[first:last].astype(F32)
        return sum(k.parts[i, first:last].astype(F32) for i in range(k.parts.shape[0]))

    if hasattr(k, "own"):
        cp.fetch(k.h_own, k.own).wait()
    if gain_shapes:
        sums = own_rows(gains_at, gains_at + GAIN_ROWS)
        row = 0
        for i, (count, width) in enumerate(gain_shapes):
            out = getattr(k, f"o_gain{i}")
            for g in range(count):
                for c in range(0, width, TILE):
                    out[g : g + 1, c : c + TILE] = sums[row : row + 1]
                    row += 1
    for i, (tiles, total, split, off, rows) in enumerate(plan):
        if not split:
            buf = getattr(k, f"b{i}")
            for t in range(tiles):
                buf[:, t * TILE : (t + 1) * TILE] = own_rows(off + t * rows, off + (t + 1) * rows)
            cp.flush(buf, getattr(k, f"o{i}"))
    for piece in pieces:
        piece.wait()
    for i, (tiles, total, split, off, rows) in enumerate(plan):
        if split:
            buf = getattr(k, f"b{i}")
            for s in range(nseq):
                ref = getattr(k, f"p{s}")
                first = jnp.minimum((z ^ s) * tiles, total - tiles)
                for t in range(tiles):
                    buf[:, at(first + t, TILE)] = ref[off + t * rows : off + (t + 1) * rows].astype(F32)
            cp.flush(buf, getattr(k, f"o{i}"))


class Comm:
    def __init__(self):
        self.nseq = lax.axis_size("seq")
        self.ndp = lax.axis_size("dp")
        self.z = lax.axis_index("seq")
        self.d = lax.axis_index("dp")
        self.scal = jnp.stack([self.d % 2, self.z]).astype(jnp.int32)

    def pieces_at_once(self, x):
        n = self.nseq
        return [x] + [lax.ppermute(x, "seq", [(i, i ^ k) for i in range(n)]) for k in range(1, n)]

    def pieces(self, x):
        n = self.nseq
        got = [x]
        for k in range(1, n):
            step = k & -k
            got.append(lax.ppermute(got[k ^ step], "seq", [(i, i ^ step) for i in range(n)]))
        return got

    def pack(self, *pairs):
        ins, outs, scratch = {}, {}, {}
        for i, (text, image) in enumerate(pairs):
            total = sum(x.shape[0] * x.shape[1] * (x.shape[2] // TILE) for x in (text, image))
            ins.update({f"h_t{i}": (text, "h"), f"h_i{i}": (image, "h")})
            scratch.update({f"t{i}": (text.shape, BF16), f"i{i}": (image.shape, BF16)})
            outs[f"o{i}"] = ((total, TILE), BF16, "h")
            scratch[f"s{i}"] = ((total, TILE), BF16)
        got = kernel_call(
            "pack",
            functools.partial(pack_body, count=len(pairs)),
            self.scal,
            ins,
            outs,
            scratch,
            copies=3 * len(pairs),
            extra=2,
        )
        return [getattr(got, name) for name in outs]

    def plan_of(self, members):
        plan = {}
        off = 0
        for want in (True, False):
            for i, (din, dout, split) in enumerate(members):
                if split != want:
                    continue
                total = dout // TILE
                tiles = -(-total // self.nseq) if split else total
                rows = din // self.ndp
                plan[i] = (tiles, total, split, off, rows)
                off += tiles * rows
            if want:
                split_rows = off
        return Plan(self, [plan[i] for i in range(len(members))], split_rows, off)


class Plan:
    def __init__(self, comm, members, split_rows, rows, gain_shapes=()):
        self.comm, self.members, self.split_rows, self.rows = comm, members, split_rows, rows
        self.gain_shapes = gain_shapes
        self.gains_at = rows

    def with_gains(self, shapes):
        self.gain_shapes = shapes
        self.rows += GAIN_ROWS
        return self

    def half(self):
        return (self.comm.ndp // 2, self.rows, TILE)

    def swap(self, keep, send):
        self.keep = keep
        self.got = lax.ppermute(send, "dp", [(i, i ^ 1) for i in range(self.comm.ndp)])

    def add(self):
        self.pair = (self.keep.astype(F32) + self.got.astype(F32)).astype(BF16)

    def cross(self):
        groups = [list(range(b, self.comm.ndp, 2)) for b in range(2)]
        self.parts = lax.all_to_all(
            self.pair, "dp", split_axis=0, concat_axis=0, tiled=True, axis_index_groups=groups
        )

    def along(self):
        def total(part):
            return jnp.sum(part.astype(F32), axis=0).astype(BF16)

        self.everyone = []
        if self.split_rows:
            self.everyone = self.comm.pieces(total(self.parts[:, : self.split_rows]))
        self.own = None
        if self.split_rows and self.rows > self.split_rows:
            self.own = total(self.parts[:, self.split_rows :])

    def unpack(self):
        plan = [(p[0], p[1], p[2], p[3] if p[2] else p[3] - self.split_rows, p[4]) for p in self.members]
        ins = {f"h{i}": (x, "h") for i, x in enumerate(self.everyone)}
        if self.own is not None:
            ins["h_own"] = (self.own, "h")
        elif not self.split_rows:
            ins["parts"] = (self.parts, "v")
        outs = {f"o{i}": ((p[4], p[1] * TILE), F32, "h") for i, p in enumerate(plan)}
        outs.update({f"o_gain{i}": (s, F32, "v") for i, s in enumerate(self.gain_shapes)})
        scratch = {f"p{i}": (x.shape, BF16) for i, x in enumerate(self.everyone)}
        if self.own is not None:
            scratch["own"] = (self.own.shape, BF16)
        scratch.update({f"b{i}": ((p[4], p[1] * TILE), F32) for i, p in enumerate(plan)})
        got = kernel_call(
            "unpack",
            functools.partial(
                unpack_body,
                plan=plan,
                nseq=len(self.everyone),
                gains_at=self.gains_at - self.split_rows,
                gain_shapes=self.gain_shapes,
            ),
            self.comm.scal,
            ins,
            outs,
            scratch,
            copies=16,
        )
        return [getattr(got, name) for name in outs]


def tie(*xs):
    return lax.optimization_barrier(xs)


def per_device(
    text_in,
    image_in,
    text_seg,
    image_seg,
    text_co_in,
    image_co_in,
    text_co_out,
    image_co_out,
    text_up,
    text_down,
    image_up,
    image_down,
    text_qkv,
    text_proj,
    image_qkv,
    image_proj,
    text_gains,
    image_gains,
    text_upstream,
    image_upstream,
):
    comm = Comm()
    scal = comm.scal
    n = comm.nseq
    rows, nt, dt = text_in.shape
    ni, di = image_in.shape[1:]
    lt, li = n * nt, n * ni
    tt, ti = rows * lt, rows * li
    dc = text_co_out.shape[0]
    ft, fi = text_up.shape[1], image_up.shape[1]
    segs = {"tseg": (text_seg, "v"), "iseg": (image_seg, "v")}
    gains = {"tg": (text_gains, "v"), "ig": (image_gains, "v")}

    (inputs,) = comm.pack((text_in, image_in))
    inputs = comm.pieces(inputs)
    text_upstream, image_upstream, inputs[1] = tie(text_upstream, image_upstream, inputs[1])
    (upstream,) = comm.pack((text_upstream, image_upstream))
    upstream, *inputs = tie(upstream, *inputs)
    upstream = comm.pieces_at_once(upstream)

    def saved(**shapes):
        return (
            {"o_" + name: (shape, dtype, "h") for name, (shape, dtype) in shapes.items()},
            {name: (shape, dtype) for name, (shape, dtype) in shapes.items()},
        )

    outs, scratch = saved(
        tx=((tt, dt), BF16),
        ix=((ti, di), BF16),
        tqkv=((tt, 3 * dc), BF16),
        iqkv=((ti, 3 * dc), BF16),
        tatt=((tt, dc), BF16),
        iatt=((ti, dc), BF16),
        pt=((rows, HC, li, lt), BF16),
        pi=((rows, HC, li, lt), BF16),
        tn1=((tt, dt), F32),
        tr1=((tt, LANES), F32),
        t1=((tt, dt), BF16),
        in1=((ti, di), F32),
        ir1=((ti, LANES), F32),
        i1=((ti, di), BF16),
        ta=((tt, ft), BF16),
        tsl=((tt, ft), BF16),
        ia=((ti, fi), BF16),
        isl=((ti, fi), BF16),
        tr2=((tt, LANES), F32),
        ir2=((ti, LANES), F32),
        tn2=((tt, dt), F32),
        t2=((tt, dt), BF16),
        in2=((ti, di), F32),
        i2=((ti, di), BF16),
    )
    scratch.update(
        staged=((n,) + inputs[0].shape, BF16),
        bias=((rows, li, lt), F32),
        wa=((dt, 3 * dc), BF16),
        wb=((di, 3 * dc), BF16),
        wo=((dc, dt), BF16),
        wd=((ft, dt), BF16),
        acc_t=((tt, dt), F32),
        acc_i=((ti, di), F32),
    )
    ins = {f"part{i}": (x, "h") for i, x in enumerate(inputs)}
    ins.update(
        co_t=(text_co_in, "h"),
        co_i=(image_co_in, "h"),
        out_t=(text_co_out, "h"),
        out_i=(image_co_out, "h"),
        up_t=(text_up, "h"),
        down_t=(text_down, "h"),
        up_i=(image_up, "h"),
        down_i=(image_down, "h"),
        **segs,
        **gains,
    )
    f1 = kernel_call(
        "co_stage",
        functools.partial(co_stage_body, rows=rows, parts=n, count_t=nt, count_i=ni),
        scal,
        ins,
        outs,
        scratch,
    )

    outs, scratch = saved(
        sqkv=((tt, 3 * dt), BF16),
        uqkv=((ti, 3 * di), BF16),
        tmix=((tt, dt), BF16),
        imix=((ti, di), BF16),
        spt=((rows, HT, lt, lt), BF16),
        spi=((rows, HI, li, li), BF16),
        tn3=((tt, dt), F32),
        tr3=((tt, LANES), F32),
        in3=((ti, di), F32),
        ir3=((ti, LANES), F32),
        tres=((rows, nt, dt), BF16),
        ires=((rows, ni, di), BF16),
    )
    scratch.update(
        wa=(text_qkv.shape, BF16),
        wb=(image_qkv.shape, BF16),
        pa=(text_proj.shape, BF16),
        pb=(image_proj.shape, BF16),
        acc_t=((tt, dt), F32),
        acc_i=((ti, di), F32),
        t2=((tt, dt), BF16),
        i2=((ti, di), BF16),
        tn2=((tt, dt), F32),
        in2=((ti, di), F32),
        tbias=((rows, lt, lt), F32),
        ibias=((rows, li, li), F32),
    )
    f2 = kernel_call(
        "self_stage",
        functools.partial(self_stage_body, rows=rows, count_t=nt, count_i=ni),
        scal,
        dict(
            h_t2=(f1.o_t2, "h"),
            h_i2=(f1.o_i2, "h"),
            h_tn2=(f1.o_tn2, "h"),
            h_in2=(f1.o_in2, "h"),
            qkv_t=(text_qkv, "h"),
            qkv_i=(image_qkv, "h"),
            proj_t=(text_proj, "h"),
            proj_i=(image_proj, "h"),
            **segs,
            **gains,
        ),
        outs,
        scratch,
    )

    group_1 = comm.plan_of([(dt, dt, True), (dt, 3 * dt, True), (di, 3 * di, True)])
    group_2 = comm.plan_of([(ft, dt, True), (fi, di, True), (dt, ft, True), (di, fi, True), (di, di, True)])
    group_3 = comm.plan_of([(dc, di, True), (di, 3 * dc, True), (dc, dt, True)])
    group_4 = comm.plan_of([(dt, 3 * dc, False)]).with_gains([text_gains.shape, image_gains.shape])

    def sources(**arrays):
        return (
            {"h_" + name: (x, "h") for name, x in arrays.items()},
            {name: (x.shape, x.dtype) for name, x in arrays.items()},
        )

    def packed(group, tag=""):
        shape = group.half()
        return (
            {"o_keep" + tag: (shape, BF16, "h"), "o_send" + tag: (shape, BF16, "h")},
            {"keep" + tag: (shape, BF16), "send" + tag: (shape, BF16)},
        )

    ins, scratch = sources(
        tn3=f2.o_tn3,
        tr3=f2.o_tr3,
        proj_t=text_proj,
        in3=f2.o_in3,
        ir3=f2.o_ir3,
        proj_i=image_proj,
        sqkv=f2.o_sqkv,
        spt=f2.o_spt,
        uqkv=f2.o_uqkv,
        spi=f2.o_spi,
        tmix=f2.o_tmix,
        t2=f1.o_t2,
        i2=f1.o_i2,
    )
    ins.update({f"h_up{i}": (x, "h") for i, x in enumerate(upstream)})
    outs, more = packed(group_1)
    scratch.update(
        **more,
        up=((n,) + upstream[0].shape, BF16),
        tup=((tt, dt), BF16),
        iup=((ti, di), BF16),
        d3b=((tt, dt), BF16),
        e3b=((ti, di), BF16),
        dmt=((tt, dt), BF16),
        dmi=((ti, di), BF16),
        tdg=((8, dt), F32),
        idg=((8, di), F32),
    )
    outs.update(
        o_e3b=((ti, di), BF16, "h"),
        o_d3=((tt, dt), F32, "v"),
        o_e3=((ti, di), F32, "v"),
        o_dsqkv=((tt, 3 * dt), BF16, "v"),
        o_duqkv=((ti, 3 * di), BF16, "v"),
        o_tdg=((8, dt), F32, "h"),
        o_idg=((8, di), F32, "h"),
    )
    b1 = kernel_call(
        "self_back",
        functools.partial(
            self_back_body, rows=rows, count_t=nt, count_i=ni, plan=group_1.members, ndp=comm.ndp
        ),
        scal,
        {**ins, **gains},
        outs,
        scratch,
    )
    group_1.swap(b1.o_keep, b1.o_send)

    ins, scratch = sources(tn2=f1.o_tn2, tr2=f1.o_tr2, in2=f1.o_in2, ir2=f1.o_ir2)
    outs, more = saved(
        d2=((tt, dt), F32),
        e2=((ti, di), F32),
        d2b=((tt, dt), BF16),
        e2b=((ti, di), BF16),
        tdg=((8, dt), F32),
        idg=((8, di), F32),
    )
    scratch.update(
        **more,
        wa=(text_qkv.shape, BF16),
        wb=(image_qkv.shape, BF16),
        acc_t=((tt, dt), F32),
        acc_i=((ti, di), F32),
    )
    b2 = kernel_call(
        "qkv_back",
        qkv_back_body,
        scal,
        dict(
            **ins,
            qkv_t=(text_qkv, "h"),
            qkv_i=(image_qkv, "h"),
            dsqkv=(b1.o_dsqkv, "v"),
            duqkv=(b1.o_duqkv, "v"),
            d3=(b1.o_d3, "v"),
            e3=(b1.o_e3, "v"),
            **gains,
        ),
        outs,
        scratch,
    )
    group_1.got, d2, e2, d2b, e2b = tie(group_1.got, b2.o_d2, b2.o_e2, b2.o_d2b, b2.o_e2b)
    group_1.add()
    group_1.cross()

    ins, scratch = sources(
        down_i=image_down,
        isl=f1.o_isl,
        up_i=image_up,
        down_t=text_down,
        tsl=f1.o_tsl,
        up_t=text_up,
        ia=f1.o_ia,
        i1=f1.o_i1,
        ta=f1.o_ta,
        t1=f1.o_t1,
        d2b=d2b,
        e2b=e2b,
        imix=f2.o_imix,
        e3b=b1.o_e3b,
    )
    ins.update(h_d2=(d2, "h"), h_e2=(e2, "h"))
    outs, more = packed(group_2)
    scratch.update(x1=((tt, dt), F32), y1=((ti, di), F32))
    scratch.update(**more, dht=((tt, ft), BF16), dhi=((ti, fi), BF16))
    b3 = kernel_call(
        "ffn_back",
        functools.partial(ffn_back_body, plan=group_2.members, ndp=comm.ndp),
        scal,
        ins,
        dict(**outs, o_x1=((tt, dt), F32, "h"), o_y1=((ti, di), F32, "h")),
        scratch,
    )
    group_1.parts, x1, y1, keep, send = tie(
        group_1.parts, b3.o_x1, b3.o_y1, b3.o_keep, b3.o_send
    )
    group_2.swap(keep, send)
    group_1.along()

    ins, scratch = sources(
        x1=x1, y1=y1, tn1=f1.o_tn1, tr1=f1.o_tr1, out_t=text_co_out, in1=f1.o_in1, ir1=f1.o_ir1, out_i=image_co_out
    )
    outs, more = saved(
        d1b=((tt, dt), BF16),
        e1b=((ti, di), BF16),
        dat=((tt, dc), BF16),
        dai=((ti, dc), BF16),
        own_t=((rows, nt, dt), F32),
        own_i=((rows, ni, di), F32),
        tdg=((8, dt), F32),
        idg=((8, di), F32),
    )
    scratch.update(**more, d1=((tt, dt), F32), e1=((ti, di), F32))
    b4 = kernel_call(
        "first_norm_back",
        functools.partial(first_norm_back_body, rows=rows, count_t=nt, count_i=ni),
        scal,
        dict(**ins, **gains),
        outs,
        scratch,
    )
    group_2.got, dat, dai = tie(group_2.got, b4.o_dat, b4.o_dai)
    group_2.add()
    group_2.cross()

    ins, scratch = sources(
        tqkv=f1.o_tqkv,
        pt=f1.o_pt,
        iqkv=f1.o_iqkv,
        pi=f1.o_pi,
        tatt=f1.o_tatt,
        iatt=f1.o_iatt,
        tx=f1.o_tx,
        ix=f1.o_ix,
        dat=dat,
        dai=dai,
        d1b=b4.o_d1b,
        e1b=b4.o_e1b,
        tdg1=b4.o_tdg,
        tdg2=b2.o_tdg,
        tdg3=b1.o_tdg,
        idg1=b4.o_idg,
        idg2=b2.o_idg,
        idg3=b1.o_idg,
    )
    outs, more = packed(group_3)
    outs_last, more_last = packed(group_4, "_last")
    outs.update(outs_last)
    scratch.update(
        **more, **more_last, dt=((tt, 3 * dc), BF16), di=((ti, 3 * dc), BF16), gain_rows=((GAIN_ROWS, TILE), F32)
    )
    b5 = kernel_call(
        "co_back",
        functools.partial(
            co_back_body,
            rows=rows,
            parts=n,
            count_t=nt,
            count_i=ni,
            plan=group_3.members,
            last_plan=group_4.members[0],
            ndp=comm.ndp,
            gains_at=group_4.gains_at,
        ),
        scal,
        ins,
        dict(
            **outs,
            o_dt=((rows, nt, 3 * dc), BF16, "v"),
            o_di=((rows, ni, 3 * dc), BF16, "v"),
        ),
        scratch,
    )
    (
        group_1.everyone[1],
        group_1.everyone[2],
        group_2.parts,
        dt_own,
        di_own,
        keep,
        send,
        keep_last,
        send_last,
    ) = tie(
        group_1.everyone[1],
        group_1.everyone[2],
        group_2.parts,
        b5.o_dt,
        b5.o_di,
        b5.o_keep,
        b5.o_send,
        b5.o_keep_last,
        b5.o_send_last,
    )
    group_3.swap(keep, send)
    group_4.swap(keep_last, send_last)
    group_2.along()
    b6 = kernel_call(
        "in_back",
        in_back_body,
        scal,
        dict(
            co_t=(text_co_in, "h"),
            co_i=(image_co_in, "h"),
            dt=(dt_own, "v"),
            di=(di_own, "v"),
            h_d1=(b4.o_own_t, "h"),
            h_e1=(b4.o_own_i, "h"),
        ),
        dict(o_dt=((rows, nt, dt), F32, "h"), o_di=((rows, ni, di), F32, "h")),
        dict(
            gt=((rows, nt, dt), F32),
            gi=((rows, ni, di), F32),
            wa=(text_co_in.shape, BF16),
            wb=(image_co_in.shape, BF16),
            d1=((rows, nt, dt), F32),
            e1=((rows, ni, di), F32),
        ),
    )
    group_1.everyone[3], group_3.got, group_4.got, text_in_grad, image_in_grad = tie(
        group_1.everyone[3], group_3.got, group_4.got, b6.o_dt, b6.o_di
    )
    group_3.add()
    group_3.cross()
    group_4.add()
    group_2.everyone[1], group_2.everyone[2], group_3.parts, group_4.pair = tie(
        group_2.everyone[1], group_2.everyone[2], group_3.parts, group_4.pair
    )
    group_4.cross()
    group_3.along()
    text_proj_grad, text_qkv_grad, image_qkv_grad = group_1.unpack()
    (
        text_down_grad,
        image_down_grad,
        text_up_grad,
        image_up_grad,
        image_proj_grad,
    ) = group_2.unpack()
    group_4.along()
    text_co_in_grad, text_gains_grad, image_gains_grad = group_4.unpack()
    *group_3.everyone, text_co_in_grad, text_gains_grad, image_gains_grad = tie(
        *group_3.everyone, text_co_in_grad, text_gains_grad, image_gains_grad
    )
    image_co_out_grad, image_co_in_grad, text_co_out_grad = group_3.unpack()
    return (
        f2.o_tres,
        f2.o_ires,
        text_in_grad,
        image_in_grad,
        text_co_in_grad,
        image_co_in_grad,
        text_co_out_grad,
        image_co_out_grad,
        text_up_grad,
        text_down_grad,
        image_up_grad,
        image_down_grad,
        text_qkv_grad,
        text_proj_grad,
        image_qkv_grad,
        image_proj_grad,
        text_gains_grad,
        image_gains_grad,
    )


def solution(mesh):
    slots = P("dp", "seq", None)
    rows = P("dp", None)
    return jax.shard_map(
        per_device,
        mesh=mesh,
        in_specs=(slots, slots, rows, rows) + (P(),) * 14 + (slots, slots),
        out_specs=(slots,) * 4 + (rows,) * 12 + (P(), P()),
        check_vma=False,
    )
```

```python
import functools
import types

import jax
import jax.numpy as jnp
from jax import lax
from jax.experimental import pallas as pl
from jax.experimental.pallas import tpu as pltpu
from jax.sharding import PartitionSpec as P

HT = 12
HI = 8
HC = 8

NORM_EPS = 1e-05

F32 = jnp.float32
BF16 = jnp.bfloat16
LOG2E = 1.4426950408889634
MASKED = -1.0e9 * LOG2E
SQRT_2_PI = 0.7978845608028654
GELU_CUBE = 0.044715
LANES = 128
TILE = 256
WIDE = 1536
WHOLE = 3072
GAIN_ROWS = 32
MIB = 1024 * 1024


def dot_nt(a, b):
    return lax.dot_general(a, b, (((1,), (1,)), ((), ())), preferred_element_type=F32)


def dot_nn(a, b):
    return lax.dot_general(a, b, (((1,), (0,)), ((), ())), preferred_element_type=F32)


def dot_tn(a, b):
    return lax.dot_general(a, b, (((0,), (0,)), ((), ())), preferred_element_type=F32)


class Copies:
    def __init__(self, sems):
        self.sems, self.used, self.leaving = sems, 0, []

    def fetch(self, src, dst):
        copy = pltpu.make_async_copy(src, dst, self.sems.at[self.used])
        self.used += 1
        copy.start()
        return copy

    def flush(self, src, dst):
        self.leaving.append(self.fetch(src, dst))

    def finish(self):
        for copy in self.leaving:
            copy.wait()


def nbytes(shape, dtype):
    total = jnp.dtype(dtype).itemsize
    dims = list(shape)
    dims[-1] = -(-dims[-1] // 128) * 128
    if len(dims) > 1:
        dims[-2] = -(-dims[-2] // 16) * 16
    for d in dims:
        total *= d
    return total


def kernel_call(name, body, scal, ins, outs, scratch, copies=64, extra=8):
    names = list(ins) + list(outs) + list(scratch)

    def kernel(scal_ref, *refs):
        k = types.SimpleNamespace(**dict(zip(names, refs)))
        moves = Copies(refs[-1])
        body(scal_ref, k, moves)
        moves.finish()

    def place(where):
        return pl.BlockSpec(memory_space=pltpu.HBM if where == "h" else pltpu.VMEM)

    def shape_of(shape, dtype, where):
        return pltpu.HBM(tuple(shape), dtype) if where == "h" else jax.ShapeDtypeStruct(shape, dtype)

    args = [
        pltpu.with_memory_space_constraint(x, pltpu.HBM) if where == "h" else x for x, where in ins.values()
    ]
    total = sum(nbytes(s, d) for s, d in scratch.values()) + extra * MIB
    got = pl.pallas_call(
        kernel,
        in_specs=[pl.BlockSpec(memory_space=pltpu.SMEM)] + [place(w) for _, w in ins.values()],
        out_specs=[place(w) for _, _, w in outs.values()],
        out_shape=[shape_of(*o) for o in outs.values()],
        scratch_shapes=[pltpu.VMEM(tuple(s), d) for s, d in scratch.values()]
        + [pltpu.SemaphoreType.DMA((copies,))],
        compiler_params=pltpu.CompilerParams(vmem_limit_bytes=total),
        name=name,
    )(scal, *args)
    return types.SimpleNamespace(**dict(zip(outs, got)))


def loop(count, body, unroll=1):
    def step(i, carry):
        body(i)
        return carry

    lax.fori_loop(0, count, step, 0, unroll=unroll)


def at(i, size):
    return pl.ds(pl.multiple_of(i * size, size), size)


def row_chunks(rows, body):
    size = next(c for c in (128, 80, 64, 32, 16) if rows % c == 0)
    loop(rows // size, lambda i: body(at(i, size)))


def tile_of(width, limit):
    parts = -(-width // limit)
    while width % (parts * TILE):
        parts += 1
    return width // parts


def pick(i, values):
    out = values[0]
    for k in range(1, len(values)):
        out = jnp.where(i == k, values[k], out)
    return out


def lane_halves(width):
    if width == LANES:
        return [None]
    lane = lax.broadcasted_iota(jnp.int32, (1, LANES), 1)
    return [(lane // width) == i for i in range(LANES // width)]


def keep_lanes(x, sel):
    return x if sel is None else jnp.where(sel, x, jnp.zeros_like(x))


def cols(ref, rows, tile):
    return ref[rows, tile * LANES : (tile + 1) * LANES]


def store_bias(bias_ref, down_ref, along_ref):
    for r in range(bias_ref.shape[0]):
        row = down_ref[r : r + 1].astype(F32)
        col = jnp.transpose(jnp.broadcast_to(row, (8, row.shape[1])))[:, :1]
        bias_ref[r] = jnp.where(col == along_ref[r : r + 1].astype(F32), 0.0, MASKED).astype(F32)


def attend(r, q_ref, kv_ref, bias, o_ref, p_ref, lq, lk, width):
    scale = width**-0.5 * LOG2E
    sels = lane_halves(width)
    n = o_ref.shape[1] // LANES
    qs, ks = at(r, lq), at(r, lk)
    for t in range(n):
        q, k, v = cols(q_ref, qs, t), cols(kv_ref, ks, n + t), cols(kv_ref, ks, 2 * n + t)
        out = None
        for i, sel in enumerate(sels):
            s = dot_nt(k, keep_lanes(q, sel)) * scale + bias
            e = jnp.exp2(s - jnp.max(s, axis=0, keepdims=True))
            p = (e * (1.0 / jnp.sum(e, axis=0, keepdims=True))).astype(BF16)
            p_ref[r, t * len(sels) + i] = p
            o = dot_tn(p, v)
            out = o if out is None else jnp.where(sel, o, out)
        o_ref[qs, t * LANES : (t + 1) * LANES] = out.astype(BF16)


def attend_wide(r, q_ref, kv_ref, bias, o_ref, p_ref, lq, lk):
    scale = LANES**-0.5 * LOG2E
    n = o_ref.shape[1] // LANES
    qs, ks = at(r, lq), at(r, lk)
    for t in range(n):
        q, k, v = cols(q_ref, qs, t), cols(kv_ref, ks, n + t), cols(kv_ref, ks, 2 * n + t)
        s = dot_nt(q, k) * scale + bias
        e = jnp.exp2(s - jnp.max(s, axis=1, keepdims=True))
        p = (e * (1.0 / jnp.sum(e, axis=1, keepdims=True))).astype(BF16)
        p_ref[r, t] = p
        o_ref[qs, t * LANES : (t + 1) * LANES] = dot_nn(p, v).astype(BF16)


def attend_wide_back(r, q_ref, kv_ref, da_ref, p_ref, dq_ref, dkv_ref, lq, lk):
    scale = LANES**-0.5
    n = da_ref.shape[1] // LANES
    qs, ks = at(r, lq), at(r, lk)
    for t in range(n):
        q, k, v = cols(q_ref, qs, t), cols(kv_ref, ks, n + t), cols(kv_ref, ks, 2 * n + t)
        da = cols(da_ref, qs, t)
        p = p_ref[r, t]
        pf = p.astype(F32)
        w = pf * dot_nt(da, v)
        ds = (w - pf * jnp.sum(w, axis=1, keepdims=True)).astype(BF16)
        dq_ref[qs, t * LANES : (t + 1) * LANES] = (dot_nn(ds, k) * scale).astype(BF16)
        dkv_ref[ks, (n + t) * LANES : (n + t + 1) * LANES] = (dot_tn(ds, q) * scale).astype(BF16)
        dkv_ref[ks, (2 * n + t) * LANES : (2 * n + t + 1) * LANES] = dot_tn(p, da).astype(BF16)


def attend_back(r, q_ref, kv_ref, da_ref, p_ref, dq_ref, dkv_ref, lq, lk, width):
    scale = width**-0.5
    sels = lane_halves(width)
    n = da_ref.shape[1] // LANES
    qs, ks = at(r, lq), at(r, lk)
    for t in range(n):
        q, k, v = cols(q_ref, qs, t), cols(kv_ref, ks, n + t), cols(kv_ref, ks, 2 * n + t)
        da = cols(da_ref, qs, t)
        dq = dk = dv = None
        for i, sel in enumerate(sels):
            p = p_ref[r, t * len(sels) + i]
            da_h = keep_lanes(da, sel)
            pf = p.astype(F32)
            w = pf * dot_nt(v, da_h)
            ds = (w - pf * jnp.sum(w, axis=0, keepdims=True)).astype(BF16)
            dv_h = dot_nn(p, da_h)
            dk_h = dot_nn(ds, keep_lanes(q, sel))
            dq_h = dot_tn(ds, keep_lanes(k, sel))
            dq = dq_h if dq is None else dq + dq_h
            dk = dk_h if dk is None else dk + dk_h
            dv = dv_h if dv is None else dv + dv_h
        dq_ref[qs, t * LANES : (t + 1) * LANES] = (dq * scale).astype(BF16)
        dkv_ref[ks, (n + t) * LANES : (n + t + 1) * LANES] = (dk * scale).astype(BF16)
        dkv_ref[ks, (2 * n + t) * LANES : (2 * n + t + 1) * LANES] = dv.astype(BF16)


def normalize(z):
    center = z - jnp.mean(z, axis=-1, keepdims=True)
    inv = lax.rsqrt(jnp.mean(center * center, axis=-1, keepdims=True) + NORM_EPS)
    return center * inv, inv


def fold_rows(x):
    return jnp.sum(x.reshape(x.shape[0] // 8, 8, x.shape[1]), axis=0)


def matmul_tiles(x_ref, w_ref, o_ref):
    n = o_ref.shape[1]
    tile = tile_of(n, WHOLE)

    def step(i):
        o_ref[:, at(i, tile)] = dot_nn(x_ref[...], w_ref[:, at(i, tile)]).astype(o_ref.dtype)

    loop(n // tile, step)


def norm_rows(acc_ref, res, gain, n_ref, inv_ref, low_ref=None):
    def chunk(rows):
        n, inv = normalize(acc_ref[rows] + res(rows))
        n_ref[rows] = n
        inv_ref[rows] = jnp.broadcast_to(inv, (inv.shape[0], LANES))
        if low_ref is not None:
            low_ref[rows] = (n * gain).astype(BF16)

    row_chunks(acc_ref.shape[0], chunk)


def norm_back_rows(dy_of, n_ref, inv_ref, gain, d_ref, low_ref, dg_ref):
    dg_ref[...] = jnp.zeros_like(dg_ref)

    def chunk(rows):
        dy = dy_of(rows)
        n = n_ref[rows]
        dn = dy * gain
        m1 = jnp.mean(dn, axis=-1, keepdims=True)
        m2 = jnp.mean(dn * n, axis=-1, keepdims=True)
        d = inv_ref[rows][:, :1] * (dn - m1 - n * m2)
        d_ref[rows] = d
        low_ref[rows] = d.astype(BF16)
        dg_ref[...] += fold_rows(dy * n)

    row_chunks(n_ref.shape[0], chunk)


def gelu_pair(v):
    v2 = v * v
    s = 0.5 + 0.5 * jnp.tanh(v * (SQRT_2_PI + (SQRT_2_PI * GELU_CUBE) * v2))
    a = v * s
    return a, s + a * (1.0 - s) * (2.0 * SQRT_2_PI + (6.0 * SQRT_2_PI * GELU_CUBE) * v2)


def ffn_tiles(x_ref, up_ref, down_ref, a_ref, slope_ref, acc_ref):
    width = tile_of(a_ref.shape[1], WIDE)

    def step(i):
        tile = at(i, width)
        a, slope = gelu_pair(dot_nn(x_ref[...], up_ref[:, tile]))
        a = a.astype(BF16)
        a_ref[:, tile] = a
        slope_ref[:, tile] = slope.astype(BF16)
        acc_ref[...] += dot_nn(a, down_ref[tile])

    acc_ref[...] = jnp.zeros_like(acc_ref)
    loop(a_ref.shape[1] // width, step)


def ffn_back_product(low_ref, down_ref, slope_ref, up_ref, dh_ref, acc_ref, ready):
    ready(low_ref, down_ref)
    dh = dot_nt(low_ref[...], down_ref[...])
    ready(slope_ref)
    dh = (dh * slope_ref[...].astype(F32)).astype(BF16)
    dh_ref[...] = dh
    ready(up_ref, acc_ref)
    acc_ref[...] += dot_nt(dh, up_ref[...])


def send_packed(cp, keep, send, far_keep, far_send, first, last):
    for near, far in ((send, far_send), (keep, far_keep)):
        cp.flush(near.at[:, first:last], far.at[:, first:last])


def wgrad_group(scal, cp, xs, ys, plan, ndp, keep, send, far_keep, far_send):
    by_member = all(off % 16 == 0 and (tiles * rows) % 16 == 0 for tiles, _, _, off, rows in plan)
    for x, y, p in zip(xs, ys, plan):
        wgrad_member(scal, x, y, keep, send, p, ndp)
        if by_member:
            send_packed(cp, keep, send, far_keep, far_send, p[3], p[3] + p[0] * p[4])
    if not by_member:
        send_packed(cp, keep, send, far_keep, far_send, 0, keep.shape[1])


def wgrad_member(scal_ref, x_ref, y_ref, keep_ref, send_ref, plan, ndp):
    tiles, total, split, off, rows = plan
    odd = scal_ref[0] == 1
    xt = jnp.transpose(x_ref[...])
    first = jnp.minimum(scal_ref[1] * tiles, total - tiles) if split else 0
    for t in range(tiles):
        g = dot_nn(xt, y_ref[:, at(first + t, TILE)]).astype(BF16)
        base = off + t * rows
        for j in range(ndp // 2):
            even_rows = g[2 * j * rows : (2 * j + 1) * rows]
            odd_rows = g[(2 * j + 1) * rows : (2 * j + 2) * rows]
            keep_ref[j, base : base + rows] = jnp.where(odd, odd_rows, even_rows)
            send_ref[j, base : base + rows] = jnp.where(odd, even_rows, odd_rows)


def pack_gains(gain_refs, rows_ref, keep_ref, send_ref, base):
    row = 0
    for ref in gain_refs:
        total = jnp.sum(ref[...], axis=0, keepdims=True)
        for c in range(0, ref.shape[1], TILE):
            rows_ref[row : row + 1] = total[:, c : c + TILE]
            row += 1
    for row in range(row, GAIN_ROWS):
        rows_ref[row : row + 1] = jnp.zeros((1, TILE), F32)
    low = rows_ref[...].astype(BF16)
    for j in range(keep_ref.shape[0]):
        keep_ref[j, base : base + GAIN_ROWS] = low
        send_ref[j, base : base + GAIN_ROWS] = low


def co_stage_body(scal, k, cp, *, rows, parts, count_t, count_i):
    pieces = [cp.fetch(getattr(k, f"part{i}"), k.staged.at[i]) for i in range(parts)]
    wa = cp.fetch(k.co_t, k.wa)
    wb = cp.fetch(k.co_i, k.wb)
    wo = cp.fetch(k.out_t, k.wo)
    wd = cp.fetch(k.down_t, k.wd)
    lt, li = parts * count_t, parts * count_i
    store_bias(k.bias, k.iseg, k.tseg)
    for piece in pieces:
        piece.wait()
    base = join_tiles(scal[1], k.staged, k.tx, count_t, rows, 0)
    wa.wait()
    matmul_tiles(k.tx, k.wa, k.tqkv)
    up_t = cp.fetch(k.up_t, k.wa)
    cp.flush(k.tx, k.o_tx)
    cp.flush(k.tqkv, k.o_tqkv)
    join_tiles(scal[1], k.staged, k.ix, count_i, rows, base)
    wb.wait()
    matmul_tiles(k.ix, k.wb, k.iqkv)
    wi = k.ix.shape[1]
    up_i = cp.fetch(k.up_i, k.wb.at[:, 0:wi])
    down_i = cp.fetch(k.down_i, k.wb.at[:, wi : 2 * wi])
    out_i = cp.fetch(k.out_i, k.wb.at[:, 2 * wi : 3 * wi])
    cp.flush(k.ix, k.o_ix)
    cp.flush(k.iqkv, k.o_iqkv)
    assert k.tatt.shape[1] == HC * LANES

    def heads(r):
        attend(r, k.tqkv, k.iqkv, k.bias[r], k.tatt, k.pt, lt, li, LANES)
        attend_wide(r, k.iqkv, k.tqkv, k.bias[r], k.iatt, k.pi, li, lt)

    loop(rows, heads)
    cp.flush(k.tatt, k.o_tatt)
    cp.flush(k.iatt, k.o_iatt)
    cp.flush(k.pt, k.o_pt)
    cp.flush(k.pi, k.o_pi)
    out_i.wait()
    matmul_tiles(k.iatt, k.wb.at[:, 2 * wi : 3 * wi], k.acc_i)
    ig = k.ig[...]
    norm_rows(k.acc_i, lambda r: k.ix[r].astype(F32), ig[0:1], k.in1, k.ir1, k.i1)
    up_i.wait()
    down_i.wait()
    ffn_tiles(k.i1, k.wb.at[:, 0:wi], k.wb.at[:, wi : 2 * wi], k.ia, k.isl, k.acc_i)
    norm_rows(k.acc_i, lambda r: k.in1[r] * ig[0:1], ig[1:2], k.in2, k.ir2, k.i2)
    for name in ("in1", "ir1", "i1", "ia", "isl", "in2", "ir2", "i2"):
        cp.flush(getattr(k, name), getattr(k, "o_" + name))
    wo.wait()
    matmul_tiles(k.tatt, k.wo, k.acc_t)
    tg = k.tg[...]
    norm_rows(k.acc_t, lambda r: k.tx[r].astype(F32), tg[0:1], k.tn1, k.tr1, k.t1)
    up_t.wait()
    wd.wait()
    for name in ("tn1", "tr1", "t1"):
        cp.flush(getattr(k, name), getattr(k, "o_" + name))
    ffn_tiles(k.t1, k.wa, k.wd, k.ta, k.tsl, k.acc_t)
    cp.flush(k.ta, k.o_ta)
    cp.flush(k.tsl, k.o_tsl)
    norm_rows(k.acc_t, lambda r: k.tn1[r] * tg[0:1], tg[1:2], k.tn2, k.tr2, k.t2)
    for name in ("t2", "tn2", "tr2"):
        cp.flush(getattr(k, name), getattr(k, "o_" + name))


def self_stage_body(scal, k, cp, *, rows, count_t, count_i):
    t2 = cp.fetch(k.h_t2, k.t2)
    wa = cp.fetch(k.qkv_t, k.wa)
    i2 = cp.fetch(k.h_i2, k.i2)
    wb = cp.fetch(k.qkv_i, k.wb)
    pa = cp.fetch(k.proj_t, k.pa)
    pb = cp.fetch(k.proj_i, k.pb)
    tn2 = cp.fetch(k.h_tn2, k.tn2)
    in2 = cp.fetch(k.h_in2, k.in2)
    store_bias(k.tbias, k.tseg, k.tseg)
    store_bias(k.ibias, k.iseg, k.iseg)
    lt = k.t2.shape[0] // rows
    li = k.i2.shape[0] // rows
    t2.wait()
    wa.wait()
    matmul_tiles(k.t2, k.wa, k.sqkv)
    cp.flush(k.sqkv, k.o_sqkv)
    i2.wait()
    wb.wait()
    matmul_tiles(k.i2, k.wb, k.uqkv)
    cp.flush(k.uqkv, k.o_uqkv)
    wt = k.tmix.shape[1] // HT
    wi = k.imix.shape[1] // HI

    def heads(r):
        attend(r, k.sqkv, k.sqkv, k.tbias[r], k.tmix, k.spt, lt, lt, wt)
        attend(r, k.uqkv, k.uqkv, k.ibias[r], k.imix, k.spi, li, li, wi)

    loop(rows, heads)
    for name in ("tmix", "imix", "spt", "spi"):
        cp.flush(getattr(k, name), getattr(k, "o_" + name))
    tn2.wait()
    in2.wait()
    z = scal[1]
    for mix, w, ready, acc, n2, g, n3, r3, res, count in (
        (k.tmix, k.pa, pa, k.acc_t, k.tn2, k.tg, k.tn3, k.tr3, k.tres, count_t),
        (k.imix, k.pb, pb, k.acc_i, k.in2, k.ig, k.in3, k.ir3, k.ires, count_i),
    ):
        ready.wait()
        matmul_tiles(mix, w, acc)
        gain = g[...]
        norm_rows(acc, lambda r, n2=n2, gain=gain: n2[r] * gain[1:2], None, n3, r3)
        length = mix.shape[0] // rows
        for r in range(rows):
            own = n3[pl.ds(pl.multiple_of(r * length + z * count, 8), count)]
            res[r] = (own * gain[2:3]).astype(BF16)
        for name in ("tn3", "tr3", "tres") if mix is k.tmix else ("in3", "ir3", "ires"):
            cp.flush(getattr(k, name), getattr(k, "o_" + name))


def self_back_body(scal, k, cp, *, rows, count_t, count_i, plan, ndp):
    ups = [cp.fetch(getattr(k, f"h_up{i}"), k.up.at[i]) for i in range(k.up.shape[0])]
    names = ("tn3", "tr3", "proj_t", "in3", "ir3", "proj_i", "sqkv", "spt", "uqkv", "spi")
    names += ("tmix", "t2", "i2")
    moves = {n: cp.fetch(getattr(k, "h_" + n), getattr(k, n)) for n in names}

    def ready(*which):
        for n in which:
            moves[n].wait()

    for copy in ups:
        copy.wait()
    base = join_tiles(scal[1], k.up, k.tup, count_t, rows, 0)
    join_tiles(scal[1], k.up, k.iup, count_i, rows, base)
    ready("tn3", "tr3", "proj_t")
    norm_back_rows(
        lambda r: k.tup[r].astype(F32), k.tn3, k.tr3, k.tg[2:3], k.o_d3, k.d3b, k.tdg
    )
    k.dmt[...] = dot_nt(k.d3b[...], k.proj_t[...]).astype(BF16)
    ready("in3", "ir3", "proj_i")
    norm_back_rows(
        lambda r: k.iup[r].astype(F32), k.in3, k.ir3, k.ig[2:3], k.o_e3, k.e3b, k.idg
    )
    k.dmi[...] = dot_nt(k.e3b[...], k.proj_i[...]).astype(BF16)
    ready("sqkv", "spt", "uqkv", "spi")
    lt, li = k.tup.shape[0] // rows, k.iup.shape[0] // rows
    wt = k.dmt.shape[1] // HT
    wi = k.dmi.shape[1] // HI

    def heads(r):
        attend_back(r, k.sqkv, k.sqkv, k.dmt, k.spt, k.o_dsqkv, k.o_dsqkv, lt, lt, wt)
        attend_back(r, k.uqkv, k.uqkv, k.dmi, k.spi, k.o_duqkv, k.o_duqkv, li, li, wi)

    loop(rows, heads)
    ready("tmix", "t2", "i2")
    xs, ys = (k.tmix, k.t2, k.i2), (k.d3b, k.o_dsqkv, k.o_duqkv)
    cp.flush(k.e3b, k.o_e3b)
    wgrad_group(scal, cp, xs, ys, plan, ndp, k.keep, k.send, k.o_keep, k.o_send)
    for name in ("tdg", "idg"):
        cp.flush(getattr(k, name), getattr(k, "o_" + name))


def chunked(cp, src, dst, axis, count=3):
    size = src.shape[axis] // count
    out = []
    for i in range(count):
        part = slice(i * size, (i + 1) * size)
        part = (slice(None), part) if axis == 1 else (part, slice(None))
        out.append((cp.fetch(src.at[part], dst.at[part]), part))
    return out


def qkv_back_body(scal, k, cp):
    wa = chunked(cp, k.qkv_t, k.wa, 0, 3)
    extra_t = [cp.fetch(k.h_tn2, k.tn2), cp.fetch(k.h_tr2, k.tr2)]
    wb = chunked(cp, k.qkv_i, k.wb, 0, 2)
    extra_i = [cp.fetch(k.h_in2, k.in2), cp.fetch(k.h_ir2, k.ir2)]
    for dx, w, ready, extra, acc, d3, n, inv, g, outs in (
        (k.dsqkv, k.wa, wa, extra_t, k.acc_t, k.d3, k.tn2, k.tr2, k.tg, ("d2", "d2b", "tdg")),
        (k.duqkv, k.wb, wb, extra_i, k.acc_i, k.e3, k.in2, k.ir2, k.ig, ("e2", "e2b", "idg")),
    ):
        for copy, (part, _) in ready:
            copy.wait()
            acc[:, part] = dot_nt(dx[...], w[part])
        for copy in extra:
            copy.wait()
        d2, low, dg = (getattr(k, name) for name in outs)
        norm_back_rows(lambda r, acc=acc, d3=d3: d3[r] + acc[r], n, inv, g[1:2], d2, low, dg)
        for name in outs:
            cp.flush(getattr(k, name), getattr(k, "o_" + name))


def ffn_back_body(scal, k, cp, *, plan, ndp):
    moves = {}

    def start(*names):
        for name in names:
            near = getattr(k, {"e2": "y1", "d2": "x1"}.get(name, name))
            moves[id(near)] = cp.fetch(getattr(k, "h_" + name), near)

    def ready(*refs):
        for ref in refs:
            moves.pop(id(ref)).wait()

    start("e2b", "down_i", "isl", "up_i", "e2", "d2b", "down_t", "tsl", "up_t", "d2")
    start("ta", "ia", "t1", "i1", "imix", "e3b")
    ffn_back_product(k.e2b, k.down_i, k.isl, k.up_i, k.dhi, k.y1, ready)
    cp.flush(k.y1, k.o_y1)
    ffn_back_product(k.d2b, k.down_t, k.tsl, k.up_t, k.dht, k.x1, ready)
    cp.flush(k.x1, k.o_x1)
    ready(k.ta, k.ia, k.t1, k.i1, k.imix, k.e3b)
    xs, ys = (k.ta, k.ia, k.t1, k.i1, k.imix), (k.d2b, k.e2b, k.dht, k.dhi, k.e3b)
    wgrad_group(scal, cp, xs, ys, plan, ndp, k.keep, k.send, k.o_keep, k.o_send)


def first_norm_back_body(scal, k, cp, *, rows, count_t, count_i):
    moves_t = [cp.fetch(getattr(k, "h_" + n), getattr(k, n)) for n in ("x1", "tn1", "tr1", "out_t")]
    moves_i = [cp.fetch(getattr(k, "h_" + n), getattr(k, n)) for n in ("y1", "in1", "ir1", "out_i")]
    *moves_t, out_t = moves_t
    *moves_i, out_i = moves_i
    z = scal[1]
    for moves, last, x1, n, inv, g, d1, low, dg, w, da, own, count in (
        (moves_t, out_t, k.x1, k.tn1, k.tr1, k.tg, k.d1, k.d1b, k.tdg, k.out_t, k.dat, k.own_t, count_t),
        (moves_i, out_i, k.y1, k.in1, k.ir1, k.ig, k.e1, k.e1b, k.idg, k.out_i, k.dai, k.own_i, count_i),
    ):
        for copy in moves:
            copy.wait()
        norm_back_rows(lambda r, x1=x1: x1[r], n, inv, g[0:1], d1, low, dg)
        last.wait()
        da[...] = dot_nt(low[...], w[...]).astype(BF16)
        length = x1.shape[0] // rows
        for r in range(rows):
            own[r] = d1[pl.ds(pl.multiple_of(r * length + z * count, 8), count)]
        text = x1 is k.x1
        for name in ("dat", "d1b", "own_t", "tdg") if text else ("dai", "e1b", "own_i", "idg"):
            cp.flush(getattr(k, name), getattr(k, "o_" + name))


def co_back_body(scal, k, cp, *, rows, parts, count_t, count_i, plan, last_plan, ndp, gains_at):
    names = ("tqkv", "pt", "dat", "iqkv", "pi", "dai", "iatt", "e1b", "tatt", "d1b", "ix", "tx")
    names += ("tdg1", "tdg2", "tdg3", "idg1", "idg2", "idg3")
    lt, li = parts * count_t, parts * count_i
    first = cp.used
    cp.used += 6 * rows

    def row_copies(r):
        out = []
        for i, name in enumerate(names[:6]):
            far, near = getattr(k, "h_" + name), getattr(k, name)
            part = r if name in ("pt", "pi") else at(r, near.shape[0] // rows)
            out.append(pltpu.make_async_copy(far.at[part], near.at[part], cp.sems.at[first + 6 * r + i]))
        return out

    for r in range(rows):
        for copy in row_copies(r):
            copy.start()
    moves = [cp.fetch(getattr(k, "h_" + n), getattr(k, n)) for n in names[6:]]

    def heads(r):
        for copy in row_copies(r):
            copy.wait()
        attend_back(r, k.tqkv, k.iqkv, k.dat, k.pt, k.dt, k.di, lt, li, LANES)
        attend_wide_back(r, k.iqkv, k.tqkv, k.dai, k.pi, k.di, k.dt, li, lt)

    loop(rows, heads)
    for copy in moves:
        copy.wait()
    xs, ys = (k.iatt, k.ix, k.tatt), (k.e1b, k.di, k.d1b)
    wgrad_group(scal, cp, xs, ys, plan, ndp, k.keep, k.send, k.o_keep, k.o_send)
    gains = (k.tdg1, k.tdg2, k.tdg3, k.idg1, k.idg2, k.idg3)
    pack_gains(gains, k.gain_rows, k.keep_last, k.send_last, gains_at)
    wgrad_member(scal, k.tx, k.dt, k.keep_last, k.send_last, last_plan, ndp)
    cp.flush(k.send_last, k.o_send_last)
    cp.flush(k.keep_last, k.o_keep_last)
    z = scal[1]
    for full, own, count in ((k.dt, k.o_dt, count_t), (k.di, k.o_di, count_i)):
        for r in range(rows):
            values = [
                full[(r * parts + i) * count : (r * parts + i + 1) * count] for i in range(parts)
            ]
            own[r] = pick(z, values)


def in_back_body(scal, k, cp):
    own_t = cp.fetch(k.h_d1, k.d1)
    own_i = cp.fetch(k.h_e1, k.e1)
    wa = chunked(cp, k.co_t, k.wa, 1)
    wb = chunked(cp, k.co_i, k.wb, 1)
    for dx, w, chunks, d1, out, own in (
        (k.dt, k.wa, wa, k.d1, k.gt, own_t),
        (k.di, k.wb, wb, k.e1, k.gi, own_i),
    ):
        own.wait()
        r, count, m = dx.shape
        flat = dx[...].reshape(r * count, m)
        total = d1[...].reshape(r * count, d1.shape[2])
        for copy, part in chunks:
            copy.wait()
            total = total + dot_nt(flat[part], w[part])
        out[...] = total.reshape(out.shape)
        cp.flush(out, k.o_dt if out is k.gt else k.o_di)


def pack_body(scal, k, cp, *, count):
    names = [f"{stream}{i}" for i in range(count) for stream in "ti"]
    moves = {name: cp.fetch(getattr(k, "h_" + name), getattr(k, name)) for name in names}
    for i in range(count):
        packed = getattr(k, f"s{i}")
        base = 0
        for name in (f"t{i}", f"i{i}"):
            moves[name].wait()
            ref = getattr(k, name)
            for c in range(0, ref.shape[2], TILE):
                for r in range(ref.shape[0]):
                    part = ref[r, :, c : c + TILE]
                    packed[base : base + part.shape[0]] = part
                    base += part.shape[0]
        cp.flush(packed, getattr(k, f"o{i}"))


def join_tiles(z, staged, full, count, rows, base):
    parts = staged.shape[0]
    for c in range(0, full.shape[1], TILE):
        for r in range(rows):
            values = [staged[i, base : base + count] for i in range(parts)]
            for i in range(parts):
                to = (r * parts + i) * count
                full[to : to + count, c : c + TILE] = pick(z ^ i, values)
            base += count
    return base


def unpack_body(scal, k, cp, *, plan, nseq, gains_at, gain_shapes):
    z = scal[1]
    pieces = [cp.fetch(getattr(k, f"h{i}"), getattr(k, f"p{i}")) for i in range(nseq)]
    def own_rows(first, last):
        if not hasattr(k, "parts"):
            return k.own[first:last].astype(F32)
        return sum(k.parts[i, first:last].astype(F32) for i in range(k.parts.shape[0]))

    if hasattr(k, "own"):
        cp.fetch(k.h_own, k.own).wait()
    if gain_shapes:
        sums = own_rows(gains_at, gains_at + GAIN_ROWS)
        row = 0
        for i, (count, width) in enumerate(gain_shapes):
            out = getattr(k, f"o_gain{i}")
            for g in range(count):
                for c in range(0, width, TILE):
                    out[g : g + 1, c : c + TILE] = sums[row : row + 1]
                    row += 1
    for i, (tiles, total, split, off, rows) in enumerate(plan):
        if not split:
            buf = getattr(k, f"b{i}")
            for t in range(tiles):
                buf[:, t * TILE : (t + 1) * TILE] = own_rows(off + t * rows, off + (t + 1) * rows)
            cp.flush(buf, getattr(k, f"o{i}"))
    for piece in pieces:
        piece.wait()
    for i, (tiles, total, split, off, rows) in enumerate(plan):
        if split:
            buf = getattr(k, f"b{i}")
            for s in range(nseq):
                ref = getattr(k, f"p{s}")
                first = jnp.minimum((z ^ s) * tiles, total - tiles)
                for t in range(tiles):
                    buf[:, at(first + t, TILE)] = ref[off + t * rows : off + (t + 1) * rows].astype(F32)
            cp.flush(buf, getattr(k, f"o{i}"))


class Comm:
    def __init__(self):
        self.nseq = lax.axis_size("seq")
        self.ndp = lax.axis_size("dp")
        self.z = lax.axis_index("seq")
        self.d = lax.axis_index("dp")
        self.scal = jnp.stack([self.d % 2, self.z]).astype(jnp.int32)

    def pieces_at_once(self, x):
        n = self.nseq
        return [x] + [lax.ppermute(x, "seq", [(i, i ^ k) for i in range(n)]) for k in range(1, n)]

    def pieces(self, x):
        n = self.nseq
        got = [x]
        for k in range(1, n):
            step = k & -k
            got.append(lax.ppermute(got[k ^ step], "seq", [(i, i ^ step) for i in range(n)]))
        return got

    def pack(self, *pairs):
        ins, outs, scratch = {}, {}, {}
        for i, (text, image) in enumerate(pairs):
            total = sum(x.shape[0] * x.shape[1] * (x.shape[2] // TILE) for x in (text, image))
            ins.update({f"h_t{i}": (text, "h"), f"h_i{i}": (image, "h")})
            scratch.update({f"t{i}": (text.shape, BF16), f"i{i}": (image.shape, BF16)})
            outs[f"o{i}"] = ((total, TILE), BF16, "h")
            scratch[f"s{i}"] = ((total, TILE), BF16)
        got = kernel_call(
            "pack",
            functools.partial(pack_body, count=len(pairs)),
            self.scal,
            ins,
            outs,
            scratch,
            copies=3 * len(pairs),
            extra=2,
        )
        return [getattr(got, name) for name in outs]

    def plan_of(self, members):
        plan = {}
        off = 0
        for want in (True, False):
            for i, (din, dout, split) in enumerate(members):
                if split != want:
                    continue
                total = dout // TILE
                tiles = -(-total // self.nseq) if split else total
                rows = din // self.ndp
                plan[i] = (tiles, total, split, off, rows)
                off += tiles * rows
            if want:
                split_rows = off
        return Plan(self, [plan[i] for i in range(len(members))], split_rows, off)


class Plan:
    def __init__(self, comm, members, split_rows, rows, gain_shapes=()):
        self.comm, self.members, self.split_rows, self.rows = comm, members, split_rows, rows
        self.gain_shapes = gain_shapes
        self.gains_at = rows

    def with_gains(self, shapes):
        self.gain_shapes = shapes
        self.rows += GAIN_ROWS
        return self

    def half(self):
        return (self.comm.ndp // 2, self.rows, TILE)

    def swap(self, keep, send):
        self.keep = keep
        self.got = lax.ppermute(send, "dp", [(i, i ^ 1) for i in range(self.comm.ndp)])

    def add(self):
        self.pair = (self.keep.astype(F32) + self.got.astype(F32)).astype(BF16)

    def cross(self):
        groups = [list(range(b, self.comm.ndp, 2)) for b in range(2)]
        self.parts = lax.all_to_all(
            self.pair, "dp", split_axis=0, concat_axis=0, tiled=True, axis_index_groups=groups
        )

    def along(self):
        def total(part):
            return jnp.sum(part.astype(F32), axis=0).astype(BF16)

        self.everyone = []
        if self.split_rows:
            self.everyone = self.comm.pieces(total(self.parts[:, : self.split_rows]))
        self.own = None
        if self.split_rows and self.rows > self.split_rows:
            self.own = total(self.parts[:, self.split_rows :])

    def unpack(self):
        plan = [(p[0], p[1], p[2], p[3] if p[2] else p[3] - self.split_rows, p[4]) for p in self.members]
        ins = {f"h{i}": (x, "h") for i, x in enumerate(self.everyone)}
        if self.own is not None:
            ins["h_own"] = (self.own, "h")
        elif not self.split_rows:
            ins["parts"] = (self.parts, "v")
        outs = {f"o{i}": ((p[4], p[1] * TILE), F32, "h") for i, p in enumerate(plan)}
        outs.update({f"o_gain{i}": (s, F32, "v") for i, s in enumerate(self.gain_shapes)})
        scratch = {f"p{i}": (x.shape, BF16) for i, x in enumerate(self.everyone)}
        if self.own is not None:
            scratch["own"] = (self.own.shape, BF16)
        scratch.update({f"b{i}": ((p[4], p[1] * TILE), F32) for i, p in enumerate(plan)})
        got = kernel_call(
            "unpack",
            functools.partial(
                unpack_body,
                plan=plan,
                nseq=len(self.everyone),
                gains_at=self.gains_at - self.split_rows,
                gain_shapes=self.gain_shapes,
            ),
            self.comm.scal,
            ins,
            outs,
            scratch,
            copies=16,
        )
        return [getattr(got, name) for name in outs]


def tie(*xs):
    return lax.optimization_barrier(xs)


def per_device(
    text_in,
    image_in,
    text_seg,
    image_seg,
    text_co_in,
    image_co_in,
    text_co_out,
    image_co_out,
    text_up,
    text_down,
    image_up,
    image_down,
    text_qkv,
    text_proj,
    image_qkv,
    image_proj,
    text_gains,
    image_gains,
    text_upstream,
    image_upstream,
):
    comm = Comm()
    scal = comm.scal
    n = comm.nseq
    rows, nt, dt = text_in.shape
    ni, di = image_in.shape[1:]
    lt, li = n * nt, n * ni
    tt, ti = rows * lt, rows * li
    dc = text_co_out.shape[0]
    ft, fi = text_up.shape[1], image_up.shape[1]
    segs = {"tseg": (text_seg, "v"), "iseg": (image_seg, "v")}
    gains = {"tg": (text_gains, "v"), "ig": (image_gains, "v")}

    (inputs,) = comm.pack((text_in, image_in))
    inputs = comm.pieces(inputs)
    text_upstream, image_upstream, inputs[1] = tie(text_upstream, image_upstream, inputs[1])
    (upstream,) = comm.pack((text_upstream, image_upstream))
    upstream, *inputs = tie(upstream, *inputs)
    upstream = comm.pieces_at_once(upstream)

    def saved(**shapes):
        return (
            {"o_" + name: (shape, dtype, "h") for name, (shape, dtype) in shapes.items()},
            {name: (shape, dtype) for name, (shape, dtype) in shapes.items()},
        )

    outs, scratch = saved(
        tx=((tt, dt), BF16),
        ix=((ti, di), BF16),
        tqkv=((tt, 3 * dc), BF16),
        iqkv=((ti, 3 * dc), BF16),
        tatt=((tt, dc), BF16),
        iatt=((ti, dc), BF16),
        pt=((rows, HC, li, lt), BF16),
        pi=((rows, HC, li, lt), BF16),
        tn1=((tt, dt), F32),
        tr1=((tt, LANES), F32),
        t1=((tt, dt), BF16),
        in1=((ti, di), F32),
        ir1=((ti, LANES), F32),
        i1=((ti, di), BF16),
        ta=((tt, ft), BF16),
        tsl=((tt, ft), BF16),
        ia=((ti, fi), BF16),
        isl=((ti, fi), BF16),
        tr2=((tt, LANES), F32),
        ir2=((ti, LANES), F32),
        tn2=((tt, dt), F32),
        t2=((tt, dt), BF16),
        in2=((ti, di), F32),
        i2=((ti, di), BF16),
    )
    scratch.update(
        staged=((n,) + inputs[0].shape, BF16),
        bias=((rows, li, lt), F32),
        wa=((dt, 3 * dc), BF16),
        wb=((di, 3 * dc), BF16),
        wo=((dc, dt), BF16),
        wd=((ft, dt), BF16),
        acc_t=((tt, dt), F32),
        acc_i=((ti, di), F32),
    )
    ins = {f"part{i}": (x, "h") for i, x in enumerate(inputs)}
    ins.update(
        co_t=(text_co_in, "h"),
        co_i=(image_co_in, "h"),
        out_t=(text_co_out, "h"),
        out_i=(image_co_out, "h"),
        up_t=(text_up, "h"),
        down_t=(text_down, "h"),
        up_i=(image_up, "h"),
        down_i=(image_down, "h"),
        **segs,
        **gains,
    )
    f1 = kernel_call(
        "co_stage",
        functools.partial(co_stage_body, rows=rows, parts=n, count_t=nt, count_i=ni),
        scal,
        ins,
        outs,
        scratch,
    )

    outs, scratch = saved(
        sqkv=((tt, 3 * dt), BF16),
        uqkv=((ti, 3 * di), BF16),
        tmix=((tt, dt), BF16),
        imix=((ti, di), BF16),
        spt=((rows, HT, lt, lt), BF16),
        spi=((rows, HI, li, li), BF16),
        tn3=((tt, dt), F32),
        tr3=((tt, LANES), F32),
        in3=((ti, di), F32),
        ir3=((ti, LANES), F32),
        tres=((rows, nt, dt), BF16),
        ires=((rows, ni, di), BF16),
    )
    scratch.update(
        wa=(text_qkv.shape, BF16),
        wb=(image_qkv.shape, BF16),
        pa=(text_proj.shape, BF16),
        pb=(image_proj.shape, BF16),
        acc_t=((tt, dt), F32),
        acc_i=((ti, di), F32),
        t2=((tt, dt), BF16),
        i2=((ti, di), BF16),
        tn2=((tt, dt), F32),
        in2=((ti, di), F32),
        tbias=((rows, lt, lt), F32),
        ibias=((rows, li, li), F32),
    )
    f2 = kernel_call(
        "self_stage",
        functools.partial(self_stage_body, rows=rows, count_t=nt, count_i=ni),
        scal,
        dict(
            h_t2=(f1.o_t2, "h"),
            h_i2=(f1.o_i2, "h"),
            h_tn2=(f1.o_tn2, "h"),
            h_in2=(f1.o_in2, "h"),
            qkv_t=(text_qkv, "h"),
            qkv_i=(image_qkv, "h"),
            proj_t=(text_proj, "h"),
            proj_i=(image_proj, "h"),
            **segs,
            **gains,
        ),
        outs,
        scratch,
    )

    group_1 = comm.plan_of([(dt, dt, True), (dt, 3 * dt, True), (di, 3 * di, True)])
    group_2 = comm.plan_of([(ft, dt, True), (fi, di, True), (dt, ft, True), (di, fi, True), (di, di, True)])
    group_3 = comm.plan_of([(dc, di, True), (di, 3 * dc, True), (dc, dt, True)])
    group_4 = comm.plan_of([(dt, 3 * dc, False)]).with_gains([text_gains.shape, image_gains.shape])

    def sources(**arrays):
        return (
            {"h_" + name: (x, "h") for name, x in arrays.items()},
            {name: (x.shape, x.dtype) for name, x in arrays.items()},
        )

    def packed(group, tag=""):
        shape = group.half()
        return (
            {"o_keep" + tag: (shape, BF16, "h"), "o_send" + tag: (shape, BF16, "h")},
            {"keep" + tag: (shape, BF16), "send" + tag: (shape, BF16)},
        )

    ins, scratch = sources(
        tn3=f2.o_tn3,
        tr3=f2.o_tr3,
        proj_t=text_proj,
        in3=f2.o_in3,
        ir3=f2.o_ir3,
        proj_i=image_proj,
        sqkv=f2.o_sqkv,
        spt=f2.o_spt,
        uqkv=f2.o_uqkv,
        spi=f2.o_spi,
        tmix=f2.o_tmix,
        t2=f1.o_t2,
        i2=f1.o_i2,
    )
    ins.update({f"h_up{i}": (x, "h") for i, x in enumerate(upstream)})
    outs, more = packed(group_1)
    scratch.update(
        **more,
        up=((n,) + upstream[0].shape, BF16),
        tup=((tt, dt), BF16),
        iup=((ti, di), BF16),
        d3b=((tt, dt), BF16),
        e3b=((ti, di), BF16),
        dmt=((tt, dt), BF16),
        dmi=((ti, di), BF16),
        tdg=((8, dt), F32),
        idg=((8, di), F32),
    )
    outs.update(
        o_e3b=((ti, di), BF16, "h"),
        o_d3=((tt, dt), F32, "v"),
        o_e3=((ti, di), F32, "v"),
        o_dsqkv=((tt, 3 * dt), BF16, "v"),
        o_duqkv=((ti, 3 * di), BF16, "v"),
        o_tdg=((8, dt), F32, "h"),
        o_idg=((8, di), F32, "h"),
    )
    b1 = kernel_call(
        "self_back",
        functools.partial(
            self_back_body, rows=rows, count_t=nt, count_i=ni, plan=group_1.members, ndp=comm.ndp
        ),
        scal,
        {**ins, **gains},
        outs,
        scratch,
    )
    group_1.swap(b1.o_keep, b1.o_send)

    ins, scratch = sources(tn2=f1.o_tn2, tr2=f1.o_tr2, in2=f1.o_in2, ir2=f1.o_ir2)
    outs, more = saved(
        d2=((tt, dt), F32),
        e2=((ti, di), F32),
        d2b=((tt, dt), BF16),
        e2b=((ti, di), BF16),
        tdg=((8, dt), F32),
        idg=((8, di), F32),
    )
    scratch.update(
        **more,
        wa=(text_qkv.shape, BF16),
        wb=(image_qkv.shape, BF16),
        acc_t=((tt, dt), F32),
        acc_i=((ti, di), F32),
    )
    b2 = kernel_call(
        "qkv_back",
        qkv_back_body,
        scal,
        dict(
            **ins,
            qkv_t=(text_qkv, "h"),
            qkv_i=(image_qkv, "h"),
            dsqkv=(b1.o_dsqkv, "v"),
            duqkv=(b1.o_duqkv, "v"),
            d3=(b1.o_d3, "v"),
            e3=(b1.o_e3, "v"),
            **gains,
        ),
        outs,
        scratch,
    )
    group_1.got, d2, e2, d2b, e2b = tie(group_1.got, b2.o_d2, b2.o_e2, b2.o_d2b, b2.o_e2b)
    group_1.add()
    group_1.cross()

    ins, scratch = sources(
        down_i=image_down,
        isl=f1.o_isl,
        up_i=image_up,
        down_t=text_down,
        tsl=f1.o_tsl,
        up_t=text_up,
        ia=f1.o_ia,
        i1=f1.o_i1,
        ta=f1.o_ta,
        t1=f1.o_t1,
        d2b=d2b,
        e2b=e2b,
        imix=f2.o_imix,
        e3b=b1.o_e3b,
    )
    ins.update(h_d2=(d2, "h"), h_e2=(e2, "h"))
    outs, more = packed(group_2)
    scratch.update(x1=((tt, dt), F32), y1=((ti, di), F32))
    scratch.update(**more, dht=((tt, ft), BF16), dhi=((ti, fi), BF16))
    b3 = kernel_call(
        "ffn_back",
        functools.partial(ffn_back_body, plan=group_2.members, ndp=comm.ndp),
        scal,
        ins,
        dict(**outs, o_x1=((tt, dt), F32, "h"), o_y1=((ti, di), F32, "h")),
        scratch,
    )
    group_1.parts, x1, y1, keep, send = tie(
        group_1.parts, b3.o_x1, b3.o_y1, b3.o_keep, b3.o_send
    )
    group_2.swap(keep, send)
    group_1.along()

    ins, scratch = sources(
        x1=x1, y1=y1, tn1=f1.o_tn1, tr1=f1.o_tr1, out_t=text_co_out, in1=f1.o_in1, ir1=f1.o_ir1, out_i=image_co_out
    )
    outs, more = saved(
        d1b=((tt, dt), BF16),
        e1b=((ti, di), BF16),
        dat=((tt, dc), BF16),
        dai=((ti, dc), BF16),
        own_t=((rows, nt, dt), F32),
        own_i=((rows, ni, di), F32),
        tdg=((8, dt), F32),
        idg=((8, di), F32),
    )
    scratch.update(**more, d1=((tt, dt), F32), e1=((ti, di), F32))
    b4 = kernel_call(
        "first_norm_back",
        functools.partial(first_norm_back_body, rows=rows, count_t=nt, count_i=ni),
        scal,
        dict(**ins, **gains),
        outs,
        scratch,
    )
    group_2.got, dat, dai = tie(group_2.got, b4.o_dat, b4.o_dai)
    group_2.add()
    group_2.cross()

    ins, scratch = sources(
        tqkv=f1.o_tqkv,
        pt=f1.o_pt,
        iqkv=f1.o_iqkv,
        pi=f1.o_pi,
        tatt=f1.o_tatt,
        iatt=f1.o_iatt,
        tx=f1.o_tx,
        ix=f1.o_ix,
        dat=dat,
        dai=dai,
        d1b=b4.o_d1b,
        e1b=b4.o_e1b,
        tdg1=b4.o_tdg,
        tdg2=b2.o_tdg,
        tdg3=b1.o_tdg,
        idg1=b4.o_idg,
        idg2=b2.o_idg,
        idg3=b1.o_idg,
    )
    outs, more = packed(group_3)
    outs_last, more_last = packed(group_4, "_last")
    outs.update(outs_last)
    scratch.update(
        **more, **more_last, dt=((tt, 3 * dc), BF16), di=((ti, 3 * dc), BF16), gain_rows=((GAIN_ROWS, TILE), F32)
    )
    b5 = kernel_call(
        "co_back",
        functools.partial(
            co_back_body,
            rows=rows,
            parts=n,
            count_t=nt,
            count_i=ni,
            plan=group_3.members,
            last_plan=group_4.members[0],
            ndp=comm.ndp,
            gains_at=group_4.gains_at,
        ),
        scal,
        ins,
        dict(
            **outs,
            o_dt=((rows, nt, 3 * dc), BF16, "v"),
            o_di=((rows, ni, 3 * dc), BF16, "v"),
        ),
        scratch,
    )
    (
        group_1.everyone[1],
        group_1.everyone[2],
        group_2.parts,
        dt_own,
        di_own,
        keep,
        send,
        keep_last,
        send_last,
    ) = tie(
        group_1.everyone[1],
        group_1.everyone[2],
        group_2.parts,
        b5.o_dt,
        b5.o_di,
        b5.o_keep,
        b5.o_send,
        b5.o_keep_last,
        b5.o_send_last,
    )
    group_3.swap(keep, send)
    group_4.swap(keep_last, send_last)
    group_2.along()
    b6 = kernel_call(
        "in_back",
        in_back_body,
        scal,
        dict(
            co_t=(text_co_in, "h"),
            co_i=(image_co_in, "h"),
            dt=(dt_own, "v"),
            di=(di_own, "v"),
            h_d1=(b4.o_own_t, "h"),
            h_e1=(b4.o_own_i, "h"),
        ),
        dict(o_dt=((rows, nt, dt), F32, "h"), o_di=((rows, ni, di), F32, "h")),
        dict(
            gt=((rows, nt, dt), F32),
            gi=((rows, ni, di), F32),
            wa=(text_co_in.shape, BF16),
            wb=(image_co_in.shape, BF16),
            d1=((rows, nt, dt), F32),
            e1=((rows, ni, di), F32),
        ),
    )
    group_1.everyone[3], group_3.got, group_4.got, text_in_grad, image_in_grad = tie(
        group_1.everyone[3], group_3.got, group_4.got, b6.o_dt, b6.o_di
    )
    group_3.add()
    group_3.cross()
    group_4.add()
    group_2.everyone[1], group_2.everyone[2], group_3.parts, group_4.pair = tie(
        group_2.everyone[1], group_2.everyone[2], group_3.parts, group_4.pair
    )
    group_4.cross()
    group_3.along()
    text_proj_grad, text_qkv_grad, image_qkv_grad = group_1.unpack()
    (
        text_down_grad,
        image_down_grad,
        text_up_grad,
        image_up_grad,
        image_proj_grad,
    ) = group_2.unpack()
    group_4.along()
    text_co_in_grad, text_gains_grad, image_gains_grad = group_4.unpack()
    *group_3.everyone, text_co_in_grad, text_gains_grad, image_gains_grad = tie(
        *group_3.everyone, text_co_in_grad, text_gains_grad, image_gains_grad
    )
    image_co_out_grad, image_co_in_grad, text_co_out_grad = group_3.unpack()
    return (
        f2.o_tres,
        f2.o_ires,
        text_in_grad,
        image_in_grad,
        text_co_in_grad,
        image_co_in_grad,
        text_co_out_grad,
        image_co_out_grad,
        text_up_grad,
        text_down_grad,
        image_up_grad,
        image_down_grad,
        text_qkv_grad,
        text_proj_grad,
        image_qkv_grad,
        image_proj_grad,
        text_gains_grad,
        image_gains_grad,
    )


def solution(mesh):
    slots = P("dp", "seq", None)
    rows = P("dp", None)
    return jax.shard_map(
        per_device,
        mesh=mesh,
        in_specs=(slots, slots, rows, rows) + (P(),) * 14 + (slots, slots),
        out_specs=(slots,) * 4 + (rows,) * 12 + (P(), P()),
        check_vma=False,
    )
```
